512 devices in a mesh: dp: 16 (over z_lo, x), tensor: 32 (over y, z_hi, core).
Axes of the slice: x: 4, y: 4, z: 16 (z_hi: 4, z_lo: 4; z = z_hi * 4 + z_lo), core: 2. Of those that a mesh axis runs over, the one named last changes fastest.
Arguments:
- hidden_states: bfloat16 [4096, 2048], P(('dp', 'tensor')), may hold values from -36 to 36
- attention_gain: float32 [2048], replicated, may hold values from 0.4 to 2.5
- feedforward_gain: float32 [2048], replicated, may hold values from 0.4 to 2.5
- heads_weight: bfloat16 [2048, 6144], P(None, 'tensor'), may hold values from -1.9887378 to 1.9887378
- output_weight: bfloat16 [2048, 2048], P('tensor'), may hold values from -0.125 to 0.125
- upward_weight: bfloat16 [2048, 8192], P(None, 'tensor'), may hold values from -0.125 to 0.125
- downward_weight: bfloat16 [8192, 2048], P('tensor'), may hold values from -0.0625 to 0.0625
- segments: int32 [16, 256], P('dp'), may hold values from 0 to 7, never falling along the last dimension, each value on 1 to 128 neighbouring positions
- page_targets: int32 [256, 1], P('dp'), may hold values from 0 to 15; in each aligned block of 16 rows (0 to 15, 16 to 31, ...) at most 2 rows name the same one
Outputs:
- layer_output: float32 [4096, 2048], P(('dp', 'tensor'))
- cache_pages: bfloat16 [16, 16, 2, 16, 4096], P('dp', None, None, None, 'tensor')
The draws below stay inside these ranges and needn't reach their ends.
Inputs may be any that keep to these rules, and one draw needn't show every extreme that they name: `segments`: in each group's row the numbers never fall, every number below 8 occurs, no prompt has more than 128 tokens, and one has exactly 128. `page_targets`: among the 16 pages of one request group no target is named more than 2 times, a bound that some block reaches.
All inputs are finite; a program needn't handle non-finite values.
Results may differ from the reference program's by a relative error of at most 0.011.
Values may be sent and summed in bfloat16 or wider, within the bound.
A program may use at most 64 MiB of HBM per device.

```python
import math
import jax
import jax.numpy as jnp
import numpy as np
from jax import lax

D = 2048
H = 8
HD = 256
FF = 8192
ROT = 64
TOK = 256
NSEG = 8
PAGE = 16
TOKENS = 4096
SEGMAX = 128
PAGES = 16
MOST = 2
QUARTERS = 4
HQ = 64
FF_DEV = 256
N_DP = 16
N_TENSOR = 32


def draw_hidden_states(key, part):
    normal_key = jax.random.fold_in(key, 11)
    row_key = jax.random.fold_in(key, 12)
    column_key = jax.random.fold_in(key, 13)
    column_scale = jnp.exp(jax.random.uniform(column_key, (1, D), jnp.float32, math.log(0.3), math.log(3.0)))
    row_scale = jnp.exp(jax.random.uniform(row_key, (TOKENS, 1), jnp.float32, math.log(0.5), math.log(2.0)))
    values = jax.random.truncated_normal(normal_key, -4.0, 4.0, (TOKENS, D), jnp.float32)
    return (values * row_scale * column_scale).astype(jnp.bfloat16)


def draw_heads_weight(key, part):
    query_key = jax.random.fold_in(key, 21)
    keys_key = jax.random.fold_in(key, 22)
    value_key = jax.random.fold_in(key, 23)
    factor = D ** (-0.5)
    query_part = jax.random.truncated_normal(query_key, -4.0, 4.0, (D, H, HD), jnp.float32) * factor
    keys_part = jax.random.truncated_normal(keys_key, -4.0, 4.0, (D, H, HD), jnp.float32) * factor
    value_part = jax.random.truncated_normal(value_key, -4.0, 4.0, (D, H, HD), jnp.float32) * factor
    stacked = jnp.stack([query_part.reshape(D, H, QUARTERS, HQ), keys_part.reshape(D, H, QUARTERS, HQ), value_part.reshape(D, H, QUARTERS, HQ)], axis=3)
    return stacked.reshape(D, 3 * H * HD).astype(jnp.bfloat16)


def block_scale(rng, extent, shards, least, high):
    level, own = 1.0, jax.random.fold_in(rng, 6)
    for position, parts in shards:
        draws = jnp.exp(jax.random.uniform(jax.random.fold_in(own, position), (parts,), jnp.float32, least / len(shards), high / len(shards)))
        level = level * jnp.repeat(draws, extent[position] // parts).reshape([-1 if axis == position else 1 for axis in range(len(extent))])
    return level


def split_up(count, total, reach, skew):
    portions = [(1 << 20) // math.isqrt(standing ** skew) + 1 for standing in range(2, count + 1)]
    spare, given = total - reach - (count - 1), [1] * (count - 1)
    while spare > 0:
        free = [i for i in range(count - 1) if given[i] < reach]
        whole, left = sum([portions[i] for i in free]), spare
        for i in free:
            addition = min(reach - given[i], max(1, left * portions[i] // whole), spare)
            given[i] = given[i] + addition
            spare = spare - addition
    return np.array([reach] + given)


def ragged(rng, amount, total, limit, slope):
    if amount == 2:
        one = jax.random.randint(rng, (), max(1, total - limit), min(limit, total - 1) + 1)
        return jnp.stack([one, total - one])
    tallies = jnp.asarray(split_up(amount, total, limit, slope), jnp.int32)
    twos = (amount - 1) // 2
    source_of, sink = tallies[1:1 + 2 * twos:2], tallies[2:2 + 2 * twos:2]
    room = jnp.minimum(source_of - 1, limit - sink)
    moved = jax.random.randint(jax.random.fold_in(rng, 1), (twos,), 0, 1 << 20) % (room + 1)
    tallies = tallies.at[1:1 + 2 * twos:2].set(source_of - moved).at[2:2 + 2 * twos:2].set(sink + moved)
    return tallies[jax.random.permutation(jax.random.fold_in(rng, 2), amount)]


def shared_out(key, own, number, rows, count, top, reach, lean):
    sequence = jax.random.permutation(key, count)
    packed, ordinary = shares(count, rows * top, reach, lean, True), shares(count, rows * top, reach, lean, False)
    places = jnp.arange(count)

    def named(tallies, offset_by):
        used = int((tallies > 0).sum())
        fixed = max(1, used // 4)
        moved = fixed + (places - fixed + offset_by * (used - fixed)) % max(1, count - fixed)
        return jnp.zeros((count,), jnp.int32).at[sequence[jnp.where(places < fixed, places, moved)]].set(jnp.asarray(tallies, jnp.int32))

    tallies = jnp.where(number % 4 == 0, named(packed, number // 4), named(ordinary, number - number // 4 - 1))
    mixed = jax.random.permutation(jax.random.fold_in(own, 3), count)
    donor, taker = mixed[0:count // 2 * 2:2], mixed[1:count // 2 * 2:2]
    slack = jnp.minimum(tallies[donor] - 1, reach - tallies[taker]) // 2
    slack = jnp.where((donor == sequence[0]) | (taker == sequence[0]) | (tallies[taker] == 0), 0, jnp.maximum(slack, 0))
    moved = jax.random.randint(jax.random.fold_in(own, 4), (count // 2,), 0, 1 << 20) % (slack + 1)
    tallies = tallies.at[donor].add(-moved).at[taker].add(moved)
    items = jnp.searchsorted(jnp.cumsum(tallies), jnp.arange(rows * top), side="right").astype(jnp.int32)
    listing = items.reshape(top, rows).T
    listing = listing[jax.random.permutation(jax.random.fold_in(own, 1), rows)]
    offset_by = jax.random.randint(jax.random.fold_in(own, 2), (rows, 1), 0, top)
    return jnp.take_along_axis(listing, (jnp.arange(top)[None, :] + offset_by) % top, axis=1)


def shares(number_of, total, most, lean, full):
    portions = [(1 << 20) // math.isqrt(standing ** lean) + 1 for standing in range(1, number_of + 1)]
    largest = most if full else min(most, max(-(-total // number_of), total * portions[0] // sum(portions)))
    least = 1 if total - largest >= number_of - 1 else 0
    counts, rest = [largest] + [least] * (number_of - 1), total - largest - least * (number_of - 1)
    while rest > 0:
        free = [i for i in range(1, number_of) if counts[i] < largest] or [i for i in range(1, number_of) if counts[i] < most]
        pool, budget = sum([portions[i] for i in free]), rest
        for i in free:
            more = min(most - counts[i], max(1, budget * portions[i] // pool), rest)
            counts[i] = counts[i] + more
            rest = rest - more
    return np.array(counts)


def gaussian(key, dims, scale, bound, cuts=(), kind=jnp.bfloat16):
    drawn = jax.random.normal(key, dims, jnp.float32) * scale
    if len(cuts) > 0:
        drawn = block_scale(key, dims, cuts, -0.22, 0.18) * drawn
    return jnp.clip(drawn, min=-bound, max=bound).astype(kind)


def setup_inputs(seed: int = 0) -> dict:
    splits = jax.random.split(jax.random.key(seed), 10)
    hidden_states = draw_hidden_states(jax.random.fold_in(splits[9], 71), 0)
    attention_gain = jnp.clip(jnp.exp(jax.random.uniform(splits[1], (D,), jnp.float32, math.log(0.4), math.log(2.5))), 0.4, 2.5)
    feedforward_gain = jnp.clip(jnp.exp(jax.random.uniform(splits[2], (D,), jnp.float32, math.log(0.4), math.log(2.5))), 0.4, 2.5)
    heads_weight = draw_heads_weight(jax.random.fold_in(splits[9], 71), 0)
    output_weight = gaussian(splits[4], (H * HD, D), (H * HD) ** -0.5, 0.125, ((0, 32),))
    upward_weight = gaussian(splits[5], (D, FF), D ** -0.5, 0.125, ((1, 32),))
    downward_weight = gaussian(splits[6], (FF, D), FF ** -0.5, 0.0625, ((0, 32),))
    segments = jax.vmap(lambda own: jnp.searchsorted(jnp.cumsum(ragged(own, NSEG, TOK, SEGMAX, 2)), jnp.arange(TOK), side="right"))(jax.random.split(splits[7], N_DP)).reshape((N_DP, TOK)).astype(jnp.int32)
    page_targets_keys = jax.random.split(jax.random.fold_in(splits[8], 1), (N_DP * PAGES) // PAGES)
    page_targets_turns = jax.random.permutation(jax.random.fold_in(splits[8], 3), (N_DP * PAGES) // PAGES)
    page_targets = jax.vmap(lambda own, number: shared_out(jax.random.fold_in(splits[8], 2), own, number, PAGES, N_DP, 1, MOST, 1))(page_targets_keys, page_targets_turns).reshape((N_DP * PAGES, 1))
    return dict(hidden_states=hidden_states, attention_gain=attention_gain, feedforward_gain=feedforward_gain, heads_weight=heads_weight, output_weight=output_weight, upward_weight=upward_weight, downward_weight=downward_weight, segments=segments, page_targets=page_targets)


epsilon = 1e-05
rotary_base = 10000.0

def layer_norm(values, gain):
    floats = values.astype(jnp.float32)
    center = lax.optimization_barrier(jnp.mean(floats, axis=-1, keepdims=True))
    shifted = floats - center
    spread = lax.optimization_barrier(jnp.mean(shifted * shifted, axis=-1, keepdims=True))
    return (shifted * lax.rsqrt(spread + epsilon) * gain).astype(jnp.bfloat16)

def positions_of(stream):
    indices = jnp.arange(stream.shape[0], dtype=jnp.int32)
    boundary = jnp.concatenate([jnp.ones((1,), dtype=bool), stream[1:] != stream[:-1]])
    starting = lax.cummax(jnp.where(boundary, indices, jnp.zeros_like(indices)), axis=0)
    return (indices, starting)

def rotate_heads(vectors, offsets, rotary_dims):
    half_dims = rotary_dims // 2
    frequency = jnp.exp(jnp.arange(half_dims, dtype=jnp.float32) * (-2.0 * math.log(rotary_base) / rotary_dims))
    angles = offsets.astype(jnp.float32)[:, None] * frequency[None, :]
    cosine = jnp.cos(angles)
    sine = jnp.sin(angles)
    floats = vectors.astype(jnp.float32)
    leading = floats[..., :half_dims]
    trailing = floats[..., half_dims:rotary_dims]
    rotated = jnp.concatenate([leading * cosine - trailing * sine, trailing * cosine + leading * sine, floats[..., rotary_dims:]], axis=-1)
    return rotated.astype(jnp.bfloat16)

def attend_head(queries, keys, values, stream, indices):
    scores = jnp.dot(queries, keys.T, preferred_element_type=jnp.float32) * HD ** (-0.5)
    allowed = (stream[None, :] == stream[:, None]) & (indices[None, :] <= indices[:, None])
    peak = lax.optimization_barrier(jnp.max(jnp.where(allowed, scores, -jnp.inf), axis=1, keepdims=True))
    weights = jnp.where(allowed, jnp.exp(scores - peak), 0.0)
    weight_sum = lax.optimization_barrier(jnp.sum(weights, axis=1, keepdims=True))
    mixed = jnp.dot(weights.astype(jnp.bfloat16), values, preferred_element_type=jnp.float32) / weight_sum
    return mixed.astype(jnp.bfloat16)

def reference(hidden_states, attention_gain, feedforward_gain, heads_weight, output_weight, upward_weight, downward_weight, segments, page_targets):
    group_tokens = hidden_states.reshape(N_DP, TOK, D)
    group_targets = page_targets.reshape(N_DP, PAGES)

    def one_group(inputs):
        tokens, stream, targets = inputs
        normed_attention = layer_norm(tokens, attention_gain)
        normed_feedforward = layer_norm(tokens, feedforward_gain)
        joined = jnp.dot(normed_attention, heads_weight, preferred_element_type=jnp.float32).astype(jnp.bfloat16)
        components = joined.reshape(TOK, H, QUARTERS, 3, HQ).transpose(3, 1, 0, 2, 4).reshape(3, H, TOK, HD)
        indices, starting = positions_of(stream)
        offsets = indices - starting
        queries = rotate_heads(components[0], offsets, ROT)
        keys = rotate_heads(components[1], offsets, ROT)
        values = components[2]

        def per_head(trio):
            return attend_head(trio[0], trio[1], trio[2], stream, indices)
        mixed = lax.map(per_head, (queries, keys, values))
        attended = mixed.transpose(1, 0, 2).reshape(TOK, H * HD)
        hidden = jax.nn.gelu(jnp.dot(normed_feedforward, upward_weight, preferred_element_type=jnp.float32), approximate=False).astype(jnp.bfloat16)
        groups = (attended.reshape(TOK, N_TENSOR, HQ).transpose(1, 0, 2), output_weight.reshape(N_TENSOR, HQ, D), hidden.reshape(TOK, N_TENSOR, FF_DEV).transpose(1, 0, 2), downward_weight.reshape(N_TENSOR, FF_DEV, D))

        def add_group(running, group):
            term = jnp.dot(group[0], group[1], preferred_element_type=jnp.float32) + jnp.dot(group[2], group[3], preferred_element_type=jnp.float32)
            rounded = lax.optimization_barrier(term.astype(jnp.bfloat16))
            return (running + rounded.astype(jnp.float32), None)
        summed, unused = lax.scan(add_group, jnp.zeros((TOK, D), jnp.float32), groups)
        output = tokens.astype(jnp.float32) + summed
        keyed = keys.reshape(H, TOK, QUARTERS, HQ)
        valued = values.reshape(H, TOK, QUARTERS, HQ)
        rows = jnp.stack([keyed, valued], axis=3).transpose(1, 0, 2, 3, 4).reshape(PAGES, PAGE, 2 * H * HD)
        page_numbers = jnp.arange(PAGES, dtype=jnp.int32)
        earlier = lax.optimization_barrier(jnp.sum(((targets[None, :] == targets[:, None]) & (page_numbers[None, :] < page_numbers[:, None])).astype(jnp.int32), axis=1)).astype(jnp.int32)
        slots = jnp.zeros((N_DP, MOST, PAGE, 2 * H * HD), jnp.bfloat16).at[targets, earlier].set(rows)
        return (output, slots)
    outputs, slots = lax.map(one_group, (group_tokens, segments, group_targets))
    return (outputs.reshape(TOKENS, D), slots.transpose(1, 0, 2, 3, 4))
```

```python
import functools
import math

import jax
import jax.numpy as jnp
from jax import lax
from jax.experimental import pallas as pl
from jax.experimental.pallas import tpu as pltpu
from jax.sharding import PartitionSpec as P

H = 8
HD = 256
ROT = 64
PAGE = 16


epsilon = 1e-05
rotary_base = 10000.0


def layer_norm(values, gain):
    floats = values.astype(jnp.float32)
    center = jnp.mean(floats, axis=-1, keepdims=True)
    shifted = floats - center
    spread = jnp.mean(shifted * shifted, axis=-1, keepdims=True)
    return (shifted * lax.rsqrt(spread + epsilon) * gain).astype(jnp.bfloat16)


def positions_of(stream):
    indices = jnp.arange(stream.shape[0], dtype=jnp.int32)
    boundary = jnp.concatenate([jnp.ones((1,), dtype=bool), stream[1:] != stream[:-1]])
    starting = lax.cummax(jnp.where(boundary, indices, jnp.zeros_like(indices)), axis=0)
    return (indices, starting)


def rotate_leading(vectors, offsets, rotary_dims):
    half_dims = rotary_dims // 2
    frequency = jnp.exp(
        jnp.arange(half_dims, dtype=jnp.float32) * (-2.0 * math.log(rotary_base) / rotary_dims)
    )
    angles = offsets.astype(jnp.float32)[:, None] * frequency[None, :]
    cosine = jnp.cos(angles)
    sine = jnp.sin(angles)
    floats = vectors.astype(jnp.float32)
    leading = floats[..., :half_dims]
    trailing = floats[..., half_dims:rotary_dims]
    rotated = jnp.concatenate(
        [
            leading * cosine - trailing * sine,
            trailing * cosine + leading * sine,
            floats[..., rotary_dims:],
        ],
        axis=-1,
    )
    return rotated.astype(jnp.bfloat16)


def _exchange_kernel(axis, n, shared, src_ref, out_ref, local_sem, send_sem, recv_sem):
    index = lax.axis_index(axis)
    pos = index % n
    base = index - pos
    mesh_ids = pl.DeviceIdType.MESH

    def source(q):
        return src_ref.at[0] if shared else src_ref.at[q]

    def peer_copy(q, slot):
        return pltpu.make_async_remote_copy(
            src_ref=source(q),
            dst_ref=out_ref.at[slot],
            send_sem=send_sem.at[q],
            recv_sem=recv_sem.at[slot],
            device_id={axis: base + q},
            device_id_type=mesh_ids,
        )

    barrier = pltpu.get_barrier_semaphore()

    def greet(k, carry):
        q = (pos + k) % n
        pl.semaphore_signal(barrier, inc=1, device_id={axis: base + q}, device_id_type=mesh_ids)
        return carry

    lax.fori_loop(1, n, greet, 0)
    pl.semaphore_wait(barrier, n - 1)

    local = pltpu.make_async_copy(source(pos), out_ref.at[pos], local_sem)
    local.start()

    def send(k, carry):
        q = (pos + k) % n
        peer_copy(q, pos).start()
        return carry

    lax.fori_loop(1, n, send, 0)

    def finish(k, carry):
        q = (pos + k) % n
        peer_copy(q, pos).wait_send()
        peer_copy(q, q).wait_recv()
        return carry

    lax.fori_loop(1, n, finish, 0)
    local.wait()


def exchange(blocks, axis, n, shared, collective_id):
    block_shape = blocks.shape[1:]
    return pl.pallas_call(
        functools.partial(_exchange_kernel, axis, n, shared),
        out_shape=jax.ShapeDtypeStruct((n,) + block_shape, blocks.dtype),
        in_specs=[pl.BlockSpec(memory_space=pltpu.VMEM)],
        out_specs=pl.BlockSpec(memory_space=pltpu.VMEM),
        scratch_shapes=[
            pltpu.SemaphoreType.DMA,
            pltpu.SemaphoreType.DMA((n,)),
            pltpu.SemaphoreType.DMA((n,)),
        ],
        compiler_params=pltpu.CompilerParams(collective_id=collective_id, has_side_effects=True),
    )(blocks)


def shards(
    hidden_states,
    attention_gain,
    feedforward_gain,
    heads_weight,
    output_weight,
    upward_weight,
    downward_weight,
    segments,
    page_targets,
):
    tensor_count = lax.axis_size("tensor")
    replica_count = lax.axis_size("dp")
    tensor_index = lax.axis_index("tensor")
    quarters = tensor_count // H
    quarter_width = HD // quarters
    quarter_index = tensor_index % quarters
    stream = segments[0]
    tokens_total = stream.shape[0]
    local_rows = hidden_states.shape[0]

    gathered = exchange(hidden_states[None], "tensor", tensor_count, True, 0)
    tokens = gathered.reshape(tokens_total, hidden_states.shape[1])
    normed_attention = layer_norm(tokens, attention_gain)
    normed_feedforward = layer_norm(tokens, feedforward_gain)
    joined = jnp.dot(normed_attention, heads_weight, preferred_element_type=jnp.float32).astype(
        jnp.bfloat16
    )
    upward = jnp.dot(normed_feedforward, upward_weight, preferred_element_type=jnp.float32)
    hidden = jax.nn.gelu(upward, approximate=False).astype(jnp.bfloat16)

    indices, starting = positions_of(stream)
    offsets = indices - starting
    query_piece = joined[:, :quarter_width]
    key_piece = joined[:, quarter_width : 2 * quarter_width]
    value_piece = joined[:, 2 * quarter_width :]
    leading = quarter_index == 0
    query_piece = jnp.where(leading, rotate_leading(query_piece, offsets, ROT), query_piece)
    key_piece = jnp.where(leading, rotate_leading(key_piece, offsets, ROT), key_piece)

    head_pieces = exchange(
        jnp.concatenate([query_piece, key_piece], 1)[None], "tensor", quarters, True, 1
    )
    queries = head_pieces[:, :, :quarter_width].transpose(1, 0, 2).reshape(tokens_total, HD)
    keys = head_pieces[:, :, quarter_width:].transpose(1, 0, 2).reshape(tokens_total, HD)

    scores = jnp.dot(queries, keys.T, preferred_element_type=jnp.float32) * HD ** (-0.5)
    allowed = (stream[None, :] == stream[:, None]) & (indices[None, :] <= indices[:, None])
    peak = jnp.max(jnp.where(allowed, scores, -jnp.inf), axis=1, keepdims=True)
    weights = jnp.where(allowed, jnp.exp(scores - peak), 0.0)
    weight_sum = jnp.sum(weights, axis=1, keepdims=True)
    mixed = jnp.dot(weights.astype(jnp.bfloat16), value_piece, preferred_element_type=jnp.float32)
    attended = (mixed / weight_sum).astype(jnp.bfloat16)

    partial = (
        jnp.dot(attended, output_weight, preferred_element_type=jnp.float32)
        + jnp.dot(hidden, downward_weight, preferred_element_type=jnp.float32)
    ).astype(jnp.bfloat16)
    arriving = exchange(
        partial.reshape(tensor_count, local_rows, partial.shape[1]), "tensor", tensor_count, False, 2
    )
    layer_output = hidden_states.astype(jnp.float32) + jnp.sum(
        arriving.astype(jnp.float32), axis=0
    )

    page_count = tokens_total // PAGE
    page_rows = jnp.concatenate([key_piece, value_piece], 1).reshape(
        page_count, PAGE * 2 * quarter_width
    )
    targets = page_targets[:, 0]
    page_numbers = jnp.arange(page_count, dtype=jnp.int32)
    earlier = jnp.sum(
        (
            (targets[None, :] == targets[:, None]) & (page_numbers[None, :] < page_numbers[:, None])
        ).astype(jnp.int32),
        axis=1,
    )
    capacity = 2 * page_count // replica_count
    slot_numbers = targets * capacity + earlier
    placing = (
        jnp.arange(replica_count * capacity, dtype=jnp.int32)[:, None] == slot_numbers[None, :]
    ).astype(jnp.bfloat16)
    outgoing = jnp.dot(placing, page_rows, preferred_element_type=jnp.float32).astype(jnp.bfloat16)
    outgoing = outgoing.reshape(replica_count, capacity * PAGE, 2 * quarter_width)
    incoming = exchange(outgoing, "dp", replica_count, False, 3)
    cache_pages = incoming.reshape(1, replica_count, capacity, PAGE, 2 * quarter_width)
    return (layer_output, cache_pages)


def solution(mesh):
    in_specs = (
        P(("dp", "tensor"), None),
        P(),
        P(),
        P(None, "tensor"),
        P("tensor", None),
        P(None, "tensor"),
        P("tensor", None),
        P("dp", None),
        P("dp", None),
    )
    out_specs = (P(("dp", "tensor"), None), P("dp", None, None, None, "tensor"))
    return jax.shard_map(shards, mesh=mesh, in_specs=in_specs, out_specs=out_specs, check_vma=False)
```

```python
import functools
import math

import jax
import jax.numpy as jnp
from jax import lax
from jax.experimental import pallas as pl
from jax.experimental.pallas import tpu as pltpu
from jax.sharding import PartitionSpec as P

H = 8
HD = 256
ROT = 64
PAGE = 16


epsilon = 1e-05
rotary_base = 10000.0


def layer_norm(values, gain):
    floats = values.astype(jnp.float32)
    center = jnp.mean(floats, axis=-1, keepdims=True)
    shifted = floats - center
    spread = jnp.mean(shifted * shifted, axis=-1, keepdims=True)
    return (shifted * lax.rsqrt(spread + epsilon) * gain).astype(jnp.bfloat16)


def positions_of(stream):
    indices = jnp.arange(stream.shape[0], dtype=jnp.int32)
    boundary = jnp.concatenate([jnp.ones((1,), dtype=bool), stream[1:] != stream[:-1]])
    starting = lax.cummax(jnp.where(boundary, indices, jnp.zeros_like(indices)), axis=0)
    return (indices, starting)


def rotate_leading(vectors, offsets, rotary_dims):
    half_dims = rotary_dims // 2
    frequency = jnp.exp(
        jnp.arange(half_dims, dtype=jnp.float32) * (-2.0 * math.log(rotary_base) / rotary_dims)
    )
    angles = offsets.astype(jnp.float32)[:, None] * frequency[None, :]
    cosine = jnp.cos(angles)
    sine = jnp.sin(angles)
    floats = vectors.astype(jnp.float32)
    leading = floats[..., :half_dims]
    trailing = floats[..., half_dims:rotary_dims]
    rotated = jnp.concatenate(
        [
            leading * cosine - trailing * sine,
            trailing * cosine + leading * sine,
            floats[..., rotary_dims:],
        ],
        axis=-1,
    )
    return rotated.astype(jnp.bfloat16)


def _exchange_kernel(axis, n, shared, position, member, src_ref, out_ref, local_sem, send_sem, recv_sem):
    index = lax.axis_index(axis)
    pos = position(index)
    mesh_ids = pl.DeviceIdType.MESH

    def source(q):
        return src_ref.at[0] if shared else src_ref.at[q]

    def peer_copy(q, slot):
        return pltpu.make_async_remote_copy(
            src_ref=source(q),
            dst_ref=out_ref.at[slot],
            send_sem=send_sem.at[q],
            recv_sem=recv_sem.at[slot],
            device_id={axis: member(index, q)},
            device_id_type=mesh_ids,
        )

    barrier = pltpu.get_barrier_semaphore()

    def greet(k, carry):
        q = (pos + k) % n
        pl.semaphore_signal(
            barrier, inc=1, device_id={axis: member(index, q)}, device_id_type=mesh_ids
        )
        return carry

    lax.fori_loop(1, n, greet, 0)
    pl.semaphore_wait(barrier, n - 1)

    local = pltpu.make_async_copy(source(pos), out_ref.at[pos], local_sem)
    local.start()

    def send(k, carry):
        q = (pos + k) % n
        peer_copy(q, pos).start()
        return carry

    lax.fori_loop(1, n, send, 0)

    def finish(k, carry):
        q = (pos + k) % n
        peer_copy(q, pos).wait_send()
        peer_copy(q, q).wait_recv()
        return carry

    lax.fori_loop(1, n, finish, 0)
    local.wait()


def contiguous(n):
    return (lambda index: index % n, lambda index, q: index - index % n + q)


def plane_group(index):
    return (index // 8) * 2 + index % 2


def plane_member(index, q):
    return ((q // 2) * 4 + (index // 2) % 4) * 2 + q % 2


def column_group(index):
    return (index // 2) % 4


def column_member(index, q):
    return ((index // 8) * 4 + q) * 2 + index % 2


def exchange(blocks, axis, n, shared, collective_id, group=None):
    position, member = group if group is not None else contiguous(n)
    block_shape = blocks.shape[1:]
    return pl.pallas_call(
        functools.partial(_exchange_kernel, axis, n, shared, position, member),
        out_shape=jax.ShapeDtypeStruct((n,) + block_shape, blocks.dtype),
        in_specs=[pl.BlockSpec(memory_space=pltpu.VMEM)],
        out_specs=pl.BlockSpec(memory_space=pltpu.VMEM),
        scratch_shapes=[
            pltpu.SemaphoreType.DMA,
            pltpu.SemaphoreType.DMA((n,)),
            pltpu.SemaphoreType.DMA((n,)),
        ],
        compiler_params=pltpu.CompilerParams(collective_id=collective_id, has_side_effects=True),
    )(blocks)


def shards(
    hidden_states,
    attention_gain,
    feedforward_gain,
    heads_weight,
    output_weight,
    upward_weight,
    downward_weight,
    segments,
    page_targets,
):
    tensor_count = lax.axis_size("tensor")
    replica_count = lax.axis_size("dp")
    tensor_index = lax.axis_index("tensor")
    quarters = tensor_count // H
    quarter_width = HD // quarters
    quarter_index = tensor_index % quarters
    stream = segments[0]
    tokens_total = stream.shape[0]
    local_rows = hidden_states.shape[0]

    width = hidden_states.shape[1]
    planes = tensor_count // 8
    by_column = exchange(hidden_states[None], "tensor", planes, True, 0, (column_group, column_member))
    by_plane = exchange(by_column[None], "tensor", 8, True, 4, (plane_group, plane_member))
    tokens = (
        by_plane.reshape(4, 2, planes, local_rows, width)
        .transpose(0, 2, 1, 3, 4)
        .reshape(tokens_total, width)
    )
    normed_attention = layer_norm(tokens, attention_gain)
    normed_feedforward = layer_norm(tokens, feedforward_gain)
    joined = jnp.dot(normed_attention, heads_weight, preferred_element_type=jnp.float32).astype(
        jnp.bfloat16
    )
    upward = jnp.dot(normed_feedforward, upward_weight, preferred_element_type=jnp.float32)
    hidden = jax.nn.gelu(upward, approximate=False).astype(jnp.bfloat16)

    indices, starting = positions_of(stream)
    offsets = indices - starting
    query_piece = joined[:, :quarter_width]
    key_piece = joined[:, quarter_width : 2 * quarter_width]
    value_piece = joined[:, 2 * quarter_width :]
    leading = quarter_index == 0
    query_piece = jnp.where(leading, rotate_leading(query_piece, offsets, ROT), query_piece)
    key_piece = jnp.where(leading, rotate_leading(key_piece, offsets, ROT), key_piece)

    head_pieces = exchange(
        jnp.concatenate([query_piece, key_piece], 1)[None], "tensor", quarters, True, 1
    )
    queries = head_pieces[:, :, :quarter_width].transpose(1, 0, 2).reshape(tokens_total, HD)
    keys = head_pieces[:, :, quarter_width:].transpose(1, 0, 2).reshape(tokens_total, HD)

    scores = jnp.dot(queries, keys.T, preferred_element_type=jnp.float32) * HD ** (-0.5)
    allowed = (stream[None, :] == stream[:, None]) & (indices[None, :] <= indices[:, None])
    peak = jnp.max(jnp.where(allowed, scores, -jnp.inf), axis=1, keepdims=True)
    weights = jnp.where(allowed, jnp.exp(scores - peak), 0.0)
    weight_sum = jnp.sum(weights, axis=1, keepdims=True)
    mixed = jnp.dot(weights.astype(jnp.bfloat16), value_piece, preferred_element_type=jnp.float32)
    attended = (mixed / weight_sum).astype(jnp.bfloat16)

    partial = (
        jnp.dot(attended, output_weight, preferred_element_type=jnp.float32)
        + jnp.dot(hidden, downward_weight, preferred_element_type=jnp.float32)
    ).astype(jnp.bfloat16)
    outgoing_rows = (
        partial.reshape(4, planes, 2, local_rows, width)
        .transpose(0, 2, 1, 3, 4)
        .reshape(8, planes, local_rows, width)
    )
    plane_sums = jnp.sum(
        exchange(outgoing_rows, "tensor", 8, False, 2, (plane_group, plane_member)).astype(
            jnp.float32
        ),
        axis=0,
    )
    column_sums = jnp.sum(
        exchange(plane_sums, "tensor", planes, False, 5, (column_group, column_member)), axis=0
    )
    layer_output = hidden_states.astype(jnp.float32) + column_sums

    page_count = tokens_total // PAGE
    page_rows = jnp.concatenate([key_piece, value_piece], 1).reshape(
        page_count, PAGE * 2 * quarter_width
    )
    targets = page_targets[:, 0]
    page_numbers = jnp.arange(page_count, dtype=jnp.int32)
    earlier = jnp.sum(
        (
            (targets[None, :] == targets[:, None]) & (page_numbers[None, :] < page_numbers[:, None])
        ).astype(jnp.int32),
        axis=1,
    )
    capacity = 2 * page_count // replica_count
    slot_numbers = targets * capacity + earlier
    placing = (
        jnp.arange(replica_count * capacity, dtype=jnp.int32)[:, None] == slot_numbers[None, :]
    ).astype(jnp.bfloat16)
    outgoing = jnp.dot(placing, page_rows, preferred_element_type=jnp.float32).astype(jnp.bfloat16)
    outgoing = outgoing.reshape(replica_count, capacity * PAGE, 2 * quarter_width)
    incoming = exchange(outgoing, "dp", replica_count, False, 3)
    cache_pages = incoming.reshape(1, replica_count, capacity, PAGE, 2 * quarter_width)
    return (layer_output, cache_pages)


def solution(mesh):
    in_specs = (
        P(("dp", "tensor"), None),
        P(),
        P(),
        P(None, "tensor"),
        P("tensor", None),
        P(None, "tensor"),
        P("tensor", None),
        P("dp", None),
        P("dp", None),
    )
    out_specs = (P(("dp", "tensor"), None), P("dp", None, None, None, "tensor"))
    return jax.shard_map(shards, mesh=mesh, in_specs=in_specs, out_specs=out_specs, check_vma=False)
```

```python
import functools
import math

import jax
import jax.numpy as jnp
from jax import lax
from jax.experimental import pallas as pl
from jax.experimental.pallas import tpu as pltpu
from jax.sharding import PartitionSpec as P

H = 8
HD = 256
ROT = 64
PAGE = 16


epsilon = 1e-05
rotary_base = 10000.0


def layer_norm(values, gain):
    floats = values.astype(jnp.float32)
    center = jnp.mean(floats, axis=-1, keepdims=True)
    shifted = floats - center
    spread = jnp.mean(shifted * shifted, axis=-1, keepdims=True)
    return (shifted * lax.rsqrt(spread + epsilon) * gain).astype(jnp.bfloat16)


def positions_of(stream):
    indices = jnp.arange(stream.shape[0], dtype=jnp.int32)
    boundary = jnp.concatenate([jnp.ones((1,), dtype=bool), stream[1:] != stream[:-1]])
    starting = lax.cummax(jnp.where(boundary, indices, jnp.zeros_like(indices)), axis=0)
    return (indices, starting)


def rotate_leading(vectors, offsets, rotary_dims):
    half_dims = rotary_dims // 2
    frequency = jnp.exp(
        jnp.arange(half_dims, dtype=jnp.float32) * (-2.0 * math.log(rotary_base) / rotary_dims)
    )
    angles = offsets.astype(jnp.float32)[:, None] * frequency[None, :]
    cosine = jnp.cos(angles)
    sine = jnp.sin(angles)
    floats = vectors.astype(jnp.float32)
    leading = floats[..., :half_dims]
    trailing = floats[..., half_dims:rotary_dims]
    rotated = jnp.concatenate(
        [
            leading * cosine - trailing * sine,
            trailing * cosine + leading * sine,
            floats[..., rotary_dims:],
        ],
        axis=-1,
    )
    return rotated.astype(jnp.bfloat16)


def _exchange_kernel(plans, *refs):
    count = len(plans)
    sources, outs, semaphores = refs[:count], refs[count : 2 * count], refs[2 * count :]
    mesh_ids = pl.DeviceIdType.MESH
    barrier = pltpu.get_barrier_semaphore()
    steps = []
    for number, (axis, n, shared, position, member) in enumerate(plans):
        src_ref, out_ref = sources[number], outs[number]
        local_sem, send_sem, recv_sem = semaphores[3 * number : 3 * number + 3]
        index = lax.axis_index(axis)
        pos = position(index)

        def peer_copy(q, slot, src_ref=src_ref, out_ref=out_ref, send_sem=send_sem,
                      recv_sem=recv_sem, axis=axis, member=member, index=index, shared=shared):
            return pltpu.make_async_remote_copy(
                src_ref=src_ref.at[0] if shared else src_ref.at[q],
                dst_ref=out_ref.at[slot],
                send_sem=send_sem.at[q],
                recv_sem=recv_sem.at[slot],
                device_id={axis: member(index, q)},
                device_id_type=mesh_ids,
            )

        def greet(k, carry, n=n, pos=pos, axis=axis, member=member, index=index):
            q = (pos + k) % n
            pl.semaphore_signal(
                barrier, inc=1, device_id={axis: member(index, q)}, device_id_type=mesh_ids
            )
            return carry

        lax.fori_loop(1, n, greet, 0)
        local = pltpu.make_async_copy(
            src_ref.at[0] if shared else src_ref.at[pos], out_ref.at[pos], local_sem
        )
        steps.append((n, pos, peer_copy, local))
    pl.semaphore_wait(barrier, sum(plan[1] - 1 for plan in plans))

    for n, pos, peer_copy, local in steps:
        local.start()

        def send(k, carry, n=n, pos=pos, peer_copy=peer_copy):
            peer_copy((pos + k) % n, pos).start()
            return carry

        lax.fori_loop(1, n, send, 0)

    for n, pos, peer_copy, local in steps:

        def finish(k, carry, n=n, pos=pos, peer_copy=peer_copy):
            q = (pos + k) % n
            peer_copy(q, pos).wait_send()
            peer_copy(q, q).wait_recv()
            return carry

        lax.fori_loop(1, n, finish, 0)
        local.wait()


def contiguous(n):
    return (lambda index: index % n, lambda index, q: index - index % n + q)


def plane_group(index):
    return (index // 8) * 2 + index % 2


def plane_member(index, q):
    return ((q // 2) * 4 + (index // 2) % 4) * 2 + q % 2


def column_group(index):
    return (index // 2) % 4


def column_member(index, q):
    return ((index // 8) * 4 + q) * 2 + index % 2


def exchange_all(collective_id, *requests):
    plans, blocks, shapes, scratch = [], [], [], []
    for data, axis, n, shared, group in requests:
        position, member = group if group is not None else contiguous(n)
        plans.append((axis, n, shared, position, member))
        blocks.append(data)
        shapes.append(jax.ShapeDtypeStruct((n,) + data.shape[1:], data.dtype))
        scratch += [
            pltpu.SemaphoreType.DMA,
            pltpu.SemaphoreType.DMA((n,)),
            pltpu.SemaphoreType.DMA((n,)),
        ]
    return pl.pallas_call(
        functools.partial(_exchange_kernel, tuple(plans)),
        out_shape=tuple(shapes),
        in_specs=[pl.BlockSpec(memory_space=pltpu.VMEM)] * len(blocks),
        out_specs=tuple(pl.BlockSpec(memory_space=pltpu.VMEM) for _ in blocks),
        scratch_shapes=scratch,
        compiler_params=pltpu.CompilerParams(collective_id=collective_id, has_side_effects=True),
    )(*blocks)


def exchange(blocks, axis, n, shared, collective_id, group=None):
    return exchange_all(collective_id, (blocks, axis, n, shared, group))[0]


def shards(
    hidden_states,
    attention_gain,
    feedforward_gain,
    heads_weight,
    output_weight,
    upward_weight,
    downward_weight,
    segments,
    page_targets,
):
    tensor_count = lax.axis_size("tensor")
    replica_count = lax.axis_size("dp")
    tensor_index = lax.axis_index("tensor")
    quarters = tensor_count // H
    quarter_width = HD // quarters
    quarter_index = tensor_index % quarters
    stream = segments[0]
    tokens_total = stream.shape[0]
    local_rows = hidden_states.shape[0]

    width = hidden_states.shape[1]
    planes = tensor_count // 8
    by_column = exchange(hidden_states[None], "tensor", planes, True, 0, (column_group, column_member))
    by_plane = exchange(by_column[None], "tensor", 8, True, 4, (plane_group, plane_member))
    tokens = (
        by_plane.reshape(4, 2, planes, local_rows, width)
        .transpose(0, 2, 1, 3, 4)
        .reshape(tokens_total, width)
    )
    normed_attention = layer_norm(tokens, attention_gain)
    normed_feedforward = layer_norm(tokens, feedforward_gain)
    joined = jnp.dot(normed_attention, heads_weight, preferred_element_type=jnp.float32).astype(
        jnp.bfloat16
    )
    upward = jnp.dot(normed_feedforward, upward_weight, preferred_element_type=jnp.float32)
    hidden = jax.nn.gelu(upward, approximate=False).astype(jnp.bfloat16)

    indices, starting = positions_of(stream)
    offsets = indices - starting
    query_piece = joined[:, :quarter_width]
    key_piece = joined[:, quarter_width : 2 * quarter_width]
    value_piece = joined[:, 2 * quarter_width :]
    leading = quarter_index == 0
    query_piece = jnp.where(leading, rotate_leading(query_piece, offsets, ROT), query_piece)
    key_piece = jnp.where(leading, rotate_leading(key_piece, offsets, ROT), key_piece)

    page_count = tokens_total // PAGE
    page_rows = jnp.concatenate([key_piece, value_piece], 1).reshape(
        page_count, PAGE * 2 * quarter_width
    )
    targets = page_targets[:, 0]
    page_numbers = jnp.arange(page_count, dtype=jnp.int32)
    earlier = jnp.sum(
        (
            (targets[None, :] == targets[:, None]) & (page_numbers[None, :] < page_numbers[:, None])
        ).astype(jnp.int32),
        axis=1,
    )
    capacity = 2 * page_count // replica_count
    slot_numbers = targets * capacity + earlier
    placing = (
        jnp.arange(replica_count * capacity, dtype=jnp.int32)[:, None] == slot_numbers[None, :]
    ).astype(jnp.bfloat16)
    outgoing = jnp.dot(placing, page_rows, preferred_element_type=jnp.float32).astype(jnp.bfloat16)
    outgoing = outgoing.reshape(replica_count, capacity * PAGE, 2 * quarter_width)
    head_pieces, incoming = exchange_all(
        1,
        (jnp.concatenate([query_piece, key_piece], 1)[None], "tensor", quarters, True, None),
        (outgoing, "dp", replica_count, False, None),
    )
    queries = head_pieces[:, :, :quarter_width].transpose(1, 0, 2).reshape(tokens_total, HD)
    keys = head_pieces[:, :, quarter_width:].transpose(1, 0, 2).reshape(tokens_total, HD)

    scores = jnp.dot(queries, keys.T, preferred_element_type=jnp.float32) * HD ** (-0.5)
    allowed = (stream[None, :] == stream[:, None]) & (indices[None, :] <= indices[:, None])
    peak = jnp.max(jnp.where(allowed, scores, -jnp.inf), axis=1, keepdims=True)
    weights = jnp.where(allowed, jnp.exp(scores - peak), 0.0)
    weight_sum = jnp.sum(weights, axis=1, keepdims=True)
    mixed = jnp.dot(weights.astype(jnp.bfloat16), value_piece, preferred_element_type=jnp.float32)
    attended = (mixed / weight_sum).astype(jnp.bfloat16)

    partial = (
        jnp.dot(attended, output_weight, preferred_element_type=jnp.float32)
        + jnp.dot(hidden, downward_weight, preferred_element_type=jnp.float32)
    ).astype(jnp.bfloat16)
    outgoing_rows = (
        partial.reshape(4, planes, 2, local_rows, width)
        .transpose(0, 2, 1, 3, 4)
        .reshape(8, planes, local_rows, width)
    )
    plane_sums = jnp.sum(
        exchange(outgoing_rows, "tensor", 8, False, 2, (plane_group, plane_member)).astype(
            jnp.float32
        ),
        axis=0,
    )
    column_sums = jnp.sum(
        exchange(
            plane_sums.astype(jnp.bfloat16), "tensor", planes, False, 5, (column_group, column_member)
        ).astype(jnp.float32),
        axis=0,
    )
    layer_output = hidden_states.astype(jnp.float32) + column_sums

    cache_pages = incoming.reshape(1, replica_count, capacity, PAGE, 2 * quarter_width)
    return (layer_output, cache_pages)


def solution(mesh):
    in_specs = (
        P(("dp", "tensor"), None),
        P(),
        P(),
        P(None, "tensor"),
        P("tensor", None),
        P(None, "tensor"),
        P("tensor", None),
        P("dp", None),
        P("dp", None),
    )
    out_specs = (P(("dp", "tensor"), None), P("dp", None, None, None, "tensor"))
    return jax.shard_map(shards, mesh=mesh, in_specs=in_specs, out_specs=out_specs, check_vma=False)
```

```python
import functools
import math

import jax
import jax.numpy as jnp
from jax import lax
from jax.experimental import pallas as pl
from jax.experimental.pallas import tpu as pltpu
from jax.sharding import PartitionSpec as P

H = 8
HD = 256
ROT = 64
PAGE = 16


epsilon = 1e-05
rotary_base = 10000.0


def layer_norm(values, gain):
    floats = values.astype(jnp.float32)
    center = jnp.mean(floats, axis=-1, keepdims=True)
    shifted = floats - center
    spread = jnp.mean(shifted * shifted, axis=-1, keepdims=True)
    return (shifted * lax.rsqrt(spread + epsilon) * gain).astype(jnp.bfloat16)


def positions_of(stream):
    indices = jnp.arange(stream.shape[0], dtype=jnp.int32)
    boundary = jnp.concatenate([jnp.ones((1,), dtype=bool), stream[1:] != stream[:-1]])
    starting = lax.cummax(jnp.where(boundary, indices, jnp.zeros_like(indices)), axis=0)
    return (indices, starting)


def rotate_leading(vectors, offsets, rotary_dims):
    half_dims = rotary_dims // 2
    frequency = jnp.exp(
        jnp.arange(half_dims, dtype=jnp.float32) * (-2.0 * math.log(rotary_base) / rotary_dims)
    )
    angles = offsets.astype(jnp.float32)[:, None] * frequency[None, :]
    cosine = jnp.cos(angles)
    sine = jnp.sin(angles)
    floats = vectors.astype(jnp.float32)
    leading = floats[..., :half_dims]
    trailing = floats[..., half_dims:rotary_dims]
    rotated = jnp.concatenate(
        [
            leading * cosine - trailing * sine,
            trailing * cosine + leading * sine,
            floats[..., rotary_dims:],
        ],
        axis=-1,
    )
    return rotated.astype(jnp.bfloat16)


def _exchange_kernel(plans, *refs):
    count = len(plans)
    sources, outs, semaphores = refs[:count], refs[count : 2 * count], refs[2 * count :]
    mesh_ids = pl.DeviceIdType.MESH
    barrier = pltpu.get_barrier_semaphore()
    steps = []
    for number, (axis, n, shared, position, member) in enumerate(plans):
        src_ref, out_ref = sources[number], outs[number]
        local_sem, send_sem, recv_sem = semaphores[3 * number : 3 * number + 3]
        index = lax.axis_index(axis)
        pos = position(index)

        def peer_copy(q, slot, src_ref=src_ref, out_ref=out_ref, send_sem=send_sem,
                      recv_sem=recv_sem, axis=axis, member=member, index=index, shared=shared):
            return pltpu.make_async_remote_copy(
                src_ref=src_ref.at[0] if shared else src_ref.at[q],
                dst_ref=out_ref.at[slot],
                send_sem=send_sem.at[q],
                recv_sem=recv_sem.at[slot],
                device_id={axis: member(index, q)},
                device_id_type=mesh_ids,
            )

        def greet(k, carry, n=n, pos=pos, axis=axis, member=member, index=index):
            q = (pos + k) % n
            pl.semaphore_signal(
                barrier, inc=1, device_id={axis: member(index, q)}, device_id_type=mesh_ids
            )
            return carry

        lax.fori_loop(1, n, greet, 0)
        local = pltpu.make_async_copy(
            src_ref.at[0] if shared else src_ref.at[pos], out_ref.at[pos], local_sem
        )
        steps.append((n, pos, peer_copy, local))
    pl.semaphore_wait(barrier, sum(plan[1] - 1 for plan in plans))

    for n, pos, peer_copy, local in steps:
        local.start()

        def send(k, carry, n=n, pos=pos, peer_copy=peer_copy):
            peer_copy((pos + k) % n, pos).start()
            return carry

        lax.fori_loop(1, n, send, 0)

    for n, pos, peer_copy, local in steps:

        def finish(k, carry, n=n, pos=pos, peer_copy=peer_copy):
            q = (pos + k) % n
            peer_copy(q, pos).wait_send()
            peer_copy(q, q).wait_recv()
            return carry

        lax.fori_loop(1, n, finish, 0)
        local.wait()


def contiguous(n):
    return (lambda index: index % n, lambda index, q: index - index % n + q)


def plane_group(index):
    return (index // 8) * 2 + index % 2


def plane_member(index, q):
    return ((q // 2) * 4 + (index // 2) % 4) * 2 + q % 2


def column_group(index):
    return (index // 2) % 4


def column_member(index, q):
    return ((index // 8) * 4 + q) * 2 + index % 2


def exchange_all(collective_id, *requests):
    plans, blocks, shapes, scratch = [], [], [], []
    for data, axis, n, shared, group in requests:
        position, member = group if group is not None else contiguous(n)
        plans.append((axis, n, shared, position, member))
        blocks.append(data)
        shapes.append(jax.ShapeDtypeStruct((n,) + data.shape[1:], data.dtype))
        scratch += [
            pltpu.SemaphoreType.DMA,
            pltpu.SemaphoreType.DMA((n,)),
            pltpu.SemaphoreType.DMA((n,)),
        ]
    return pl.pallas_call(
        functools.partial(_exchange_kernel, tuple(plans)),
        out_shape=tuple(shapes),
        in_specs=[pl.BlockSpec(memory_space=pltpu.VMEM)] * len(blocks),
        out_specs=tuple(pl.BlockSpec(memory_space=pltpu.VMEM) for _ in blocks),
        scratch_shapes=scratch,
        compiler_params=pltpu.CompilerParams(collective_id=collective_id, has_side_effects=True),
    )(*blocks)


def exchange(blocks, axis, n, shared, collective_id, group=None):
    return exchange_all(collective_id, (blocks, axis, n, shared, group))[0]


def _greet(barrier, groups):
    index = lax.axis_index("tensor")
    total = 0
    for n, position, member in groups:
        pos = position(index)

        def greet(k, carry, n=n, pos=pos, member=member):
            pl.semaphore_signal(
                barrier,
                inc=1,
                device_id={"tensor": member(index, (pos + k) % n)},
                device_id_type=pl.DeviceIdType.MESH,
            )
            return carry

        lax.fori_loop(1, n, greet, 0)
        total += n - 1
    pl.semaphore_wait(barrier, total)


def _gather_kernel(n_col, n_plane, col, plane, x_ref, out_ref, local_sem, send_sem, relay_sem, recv_sem):
    index = lax.axis_index("tensor")
    cpos, ppos = col[0](index), plane[0](index)
    mesh_ids = pl.DeviceIdType.MESH
    _greet(pltpu.get_barrier_semaphore(), [(n_col, *col), (n_plane, *plane)])

    def col_copy(q):
        return pltpu.make_async_remote_copy(
            x_ref, out_ref.at[cpos, ppos], send_sem.at[q], recv_sem.at[cpos, ppos],
            device_id={"tensor": col[1](index, q)}, device_id_type=mesh_ids,
        )

    def plane_copy(q):
        return pltpu.make_async_remote_copy(
            x_ref, out_ref.at[cpos, ppos], send_sem.at[n_col + q], recv_sem.at[cpos, ppos],
            device_id={"tensor": plane[1](index, q)}, device_id_type=mesh_ids,
        )

    def relay_copy(zc, q):
        return pltpu.make_async_remote_copy(
            out_ref.at[zc, ppos], out_ref.at[zc, ppos], relay_sem.at[zc, q], recv_sem.at[zc, ppos],
            device_id={"tensor": plane[1](index, q)}, device_id_type=mesh_ids,
        )

    def arrival(zc, p):
        return pltpu.make_async_remote_copy(
            x_ref, out_ref.at[zc, p], send_sem.at[0], recv_sem.at[zc, p],
            device_id={"tensor": index}, device_id_type=mesh_ids,
        )

    local = pltpu.make_async_copy(x_ref, out_ref.at[cpos, ppos], local_sem)
    local.start()

    def send_col(k, carry):
        col_copy((cpos + k) % n_col).start()
        return carry

    def send_plane(k, carry):
        plane_copy((ppos + k) % n_plane).start()
        return carry

    lax.fori_loop(1, n_col, send_col, 0)
    lax.fori_loop(1, n_plane, send_plane, 0)

    def relay(k, carry):
        zc = (cpos + k) % n_col
        arrival(zc, ppos).wait_recv()

        def forward(m, inner):
            relay_copy(zc, (ppos + m) % n_plane).start()
            return inner

        return lax.fori_loop(1, n_plane, forward, carry)

    lax.fori_loop(1, n_col, relay, 0)

    def finish_col(k, carry):
        col_copy((cpos + k) % n_col).wait_send()
        return carry

    def finish_plane(m, carry):
        q = (ppos + m) % n_plane
        plane_copy(q).wait_send()
        arrival(cpos, q).wait_recv()
        return carry

    def finish_relay(k, carry):
        zc = (cpos + k) % n_col

        def inner(m, c):
            q = (ppos + m) % n_plane
            relay_copy(zc, q).wait_send()
            arrival(zc, q).wait_recv()
            return c

        return lax.fori_loop(1, n_plane, inner, carry)

    lax.fori_loop(1, n_col, finish_col, 0)
    lax.fori_loop(1, n_plane, finish_plane, 0)
    lax.fori_loop(1, n_col, finish_relay, 0)
    local.wait()


def gather_tokens(x, col, plane, n_col, n_plane, collective_id):
    return pl.pallas_call(
        functools.partial(_gather_kernel, n_col, n_plane, col, plane),
        out_shape=jax.ShapeDtypeStruct((n_col, n_plane) + x.shape, x.dtype),
        in_specs=[pl.BlockSpec(memory_space=pltpu.VMEM)],
        out_specs=pl.BlockSpec(memory_space=pltpu.VMEM),
        scratch_shapes=[
            pltpu.SemaphoreType.DMA,
            pltpu.SemaphoreType.DMA((n_col + n_plane,)),
            pltpu.SemaphoreType.DMA((n_col, n_plane)),
            pltpu.SemaphoreType.DMA((n_col, n_plane)),
        ],
        compiler_params=pltpu.CompilerParams(collective_id=collective_id, has_side_effects=True),
    )(x)


def _reduce_kernel(n_col, n_plane, col, plane, rows_ref, out_ref, inbox, stage, inbox2,
                   local_sem, send_sem, recv_sem, local2_sem, send2_sem, recv2_sem):
    index = lax.axis_index("tensor")
    cpos, ppos = col[0](index), plane[0](index)
    mesh_ids = pl.DeviceIdType.MESH
    _greet(pltpu.get_barrier_semaphore(), [(n_col, *col), (n_plane, *plane)])

    def plane_copy(q, slot):
        return pltpu.make_async_remote_copy(
            rows_ref.at[q], inbox.at[slot], send_sem.at[q], recv_sem.at[slot],
            device_id={"tensor": plane[1](index, q)}, device_id_type=mesh_ids,
        )

    def col_copy(q, slot):
        return pltpu.make_async_remote_copy(
            stage.at[q], inbox2.at[slot], send2_sem.at[q], recv2_sem.at[slot],
            device_id={"tensor": col[1](index, q)}, device_id_type=mesh_ids,
        )

    local = pltpu.make_async_copy(rows_ref.at[ppos], inbox.at[ppos], local_sem)
    local.start()

    def send_plane(m, carry):
        plane_copy((ppos + m) % n_plane, ppos).start()
        return carry

    lax.fori_loop(1, n_plane, send_plane, 0)

    def finish_plane(m, carry):
        q = (ppos + m) % n_plane
        plane_copy(q, ppos).wait_send()
        plane_copy(q, q).wait_recv()
        return carry

    lax.fori_loop(1, n_plane, finish_plane, 0)
    local.wait()

    total = inbox[0].astype(jnp.float32)
    for sender in range(1, n_plane):
        total = total + inbox[sender].astype(jnp.float32)
    stage[...] = total.astype(stage.dtype)

    local2 = pltpu.make_async_copy(stage.at[cpos], inbox2.at[cpos], local2_sem)
    local2.start()

    def send_col(k, carry):
        col_copy((cpos + k) % n_col, cpos).start()
        return carry

    lax.fori_loop(1, n_col, send_col, 0)

    def finish_col(k, carry):
        q = (cpos + k) % n_col
        col_copy(q, cpos).wait_send()
        col_copy(q, q).wait_recv()
        return carry

    lax.fori_loop(1, n_col, finish_col, 0)
    local2.wait()

    result = inbox2[0].astype(jnp.float32)
    for sender in range(1, n_col):
        result = result + inbox2[sender].astype(jnp.float32)
    out_ref[...] = result


def reduce_rows(rows, col, plane, n_col, n_plane, collective_id):
    block = rows.shape[2:]
    return pl.pallas_call(
        functools.partial(_reduce_kernel, n_col, n_plane, col, plane),
        out_shape=jax.ShapeDtypeStruct(block, jnp.float32),
        in_specs=[pl.BlockSpec(memory_space=pltpu.VMEM)],
        out_specs=pl.BlockSpec(memory_space=pltpu.VMEM),
        scratch_shapes=[
            pltpu.VMEM(rows.shape, rows.dtype),
            pltpu.VMEM((n_col,) + block, rows.dtype),
            pltpu.VMEM((n_col,) + block, rows.dtype),
            pltpu.SemaphoreType.DMA,
            pltpu.SemaphoreType.DMA((n_plane,)),
            pltpu.SemaphoreType.DMA((n_plane,)),
            pltpu.SemaphoreType.DMA,
            pltpu.SemaphoreType.DMA((n_col,)),
            pltpu.SemaphoreType.DMA((n_col,)),
        ],
        compiler_params=pltpu.CompilerParams(collective_id=collective_id, has_side_effects=True),
    )(rows)


def shards(
    hidden_states,
    attention_gain,
    feedforward_gain,
    heads_weight,
    output_weight,
    upward_weight,
    downward_weight,
    segments,
    page_targets,
):
    tensor_count = lax.axis_size("tensor")
    replica_count = lax.axis_size("dp")
    tensor_index = lax.axis_index("tensor")
    quarters = tensor_count // H
    quarter_width = HD // quarters
    quarter_index = tensor_index % quarters
    stream = segments[0]
    tokens_total = stream.shape[0]
    local_rows = hidden_states.shape[0]

    width = hidden_states.shape[1]
    planes = tensor_count // 8
    gathered = gather_tokens(
        hidden_states, (column_group, column_member), (plane_group, plane_member), planes, 8, 0
    )
    tokens = (
        gathered.reshape(planes, 4, 2, local_rows, width)
        .transpose(1, 0, 2, 3, 4)
        .reshape(tokens_total, width)
    )
    normed_attention = layer_norm(tokens, attention_gain)
    normed_feedforward = layer_norm(tokens, feedforward_gain)
    joined = jnp.dot(normed_attention, heads_weight, preferred_element_type=jnp.float32).astype(
        jnp.bfloat16
    )
    upward = jnp.dot(normed_feedforward, upward_weight, preferred_element_type=jnp.float32)
    hidden = jax.nn.gelu(upward, approximate=False).astype(jnp.bfloat16)

    indices, starting = positions_of(stream)
    offsets = indices - starting
    query_piece = joined[:, :quarter_width]
    key_piece = joined[:, quarter_width : 2 * quarter_width]
    value_piece = joined[:, 2 * quarter_width :]
    leading = quarter_index == 0
    query_piece = jnp.where(leading, rotate_leading(query_piece, offsets, ROT), query_piece)
    key_piece = jnp.where(leading, rotate_leading(key_piece, offsets, ROT), key_piece)

    page_count = tokens_total // PAGE
    page_rows = jnp.concatenate([key_piece, value_piece], 1).reshape(
        page_count, PAGE * 2 * quarter_width
    )
    targets = page_targets[:, 0]
    page_numbers = jnp.arange(page_count, dtype=jnp.int32)
    earlier = jnp.sum(
        (
            (targets[None, :] == targets[:, None]) & (page_numbers[None, :] < page_numbers[:, None])
        ).astype(jnp.int32),
        axis=1,
    )
    capacity = 2 * page_count // replica_count
    slot_numbers = targets * capacity + earlier
    placing = (
        jnp.arange(replica_count * capacity, dtype=jnp.int32)[:, None] == slot_numbers[None, :]
    ).astype(jnp.bfloat16)
    outgoing = jnp.dot(placing, page_rows, preferred_element_type=jnp.float32).astype(jnp.bfloat16)
    outgoing = outgoing.reshape(replica_count, capacity * PAGE, 2 * quarter_width)
    head_pieces, incoming = exchange_all(
        1,
        (jnp.concatenate([query_piece, key_piece], 1)[None], "tensor", quarters, True, None),
        (outgoing, "dp", replica_count, False, None),
    )
    queries = head_pieces[:, :, :quarter_width].transpose(1, 0, 2).reshape(tokens_total, HD)
    keys = head_pieces[:, :, quarter_width:].transpose(1, 0, 2).reshape(tokens_total, HD)

    scores = jnp.dot(queries, keys.T, preferred_element_type=jnp.float32) * HD ** (-0.5)
    allowed = (stream[None, :] == stream[:, None]) & (indices[None, :] <= indices[:, None])
    peak = jnp.max(jnp.where(allowed, scores, -jnp.inf), axis=1, keepdims=True)
    weights = jnp.where(allowed, jnp.exp(scores - peak), 0.0)
    weight_sum = jnp.sum(weights, axis=1, keepdims=True)
    mixed = jnp.dot(weights.astype(jnp.bfloat16), value_piece, preferred_element_type=jnp.float32)
    attended = (mixed / weight_sum).astype(jnp.bfloat16)

    partial = (
        jnp.dot(attended, output_weight, preferred_element_type=jnp.float32)
        + jnp.dot(hidden, downward_weight, preferred_element_type=jnp.float32)
    ).astype(jnp.bfloat16)
    outgoing_rows = (
        partial.reshape(4, planes, 2, local_rows, width)
        .transpose(0, 2, 1, 3, 4)
        .reshape(8, planes, local_rows, width)
    )
    column_sums = reduce_rows(
        outgoing_rows, (column_group, column_member), (plane_group, plane_member), planes, 8, 2
    )
    layer_output = hidden_states.astype(jnp.float32) + column_sums

    cache_pages = incoming.reshape(1, replica_count, capacity, PAGE, 2 * quarter_width)
    return (layer_output, cache_pages)


def solution(mesh):
    in_specs = (
        P(("dp", "tensor"), None),
        P(),
        P(),
        P(None, "tensor"),
        P("tensor", None),
        P(None, "tensor"),
        P("tensor", None),
        P("dp", None),
        P("dp", None),
    )
    out_specs = (P(("dp", "tensor"), None), P("dp", None, None, None, "tensor"))
    return jax.shard_map(shards, mesh=mesh, in_specs=in_specs, out_specs=out_specs, check_vma=False)
```

```python
import functools
import math

import jax
import jax.numpy as jnp
from jax import lax
from jax.experimental import pallas as pl
from jax.experimental.pallas import tpu as pltpu
from jax.sharding import PartitionSpec as P

H = 8
HD = 256
ROT = 64
PAGE = 16


epsilon = 1e-05
rotary_base = 10000.0


def layer_norm(values, gain):
    floats = values.astype(jnp.float32)
    center = jnp.mean(floats, axis=-1, keepdims=True)
    shifted = floats - center
    spread = jnp.mean(shifted * shifted, axis=-1, keepdims=True)
    return (shifted * lax.rsqrt(spread + epsilon) * gain).astype(jnp.bfloat16)


def positions_of(stream):
    indices = jnp.arange(stream.shape[0], dtype=jnp.int32)
    boundary = jnp.concatenate([jnp.ones((1,), dtype=bool), stream[1:] != stream[:-1]])
    starting = lax.cummax(jnp.where(boundary, indices, jnp.zeros_like(indices)), axis=0)
    return (indices, starting)


def rotate_leading(vectors, offsets, rotary_dims):
    half_dims = rotary_dims // 2
    frequency = jnp.exp(
        jnp.arange(half_dims, dtype=jnp.float32) * (-2.0 * math.log(rotary_base) / rotary_dims)
    )
    angles = offsets.astype(jnp.float32)[:, None] * frequency[None, :]
    cosine = jnp.cos(angles)
    sine = jnp.sin(angles)
    floats = vectors.astype(jnp.float32)
    leading = floats[..., :half_dims]
    trailing = floats[..., half_dims:rotary_dims]
    rotated = jnp.concatenate(
        [
            leading * cosine - trailing * sine,
            trailing * cosine + leading * sine,
            floats[..., rotary_dims:],
        ],
        axis=-1,
    )
    return rotated.astype(jnp.bfloat16)


def _exchange_kernel(plans, work, extra_in, extra_out, *refs):
    count = len(plans)
    sources, refs = refs[:count], refs[count:]
    inputs, refs = refs[:extra_in], refs[extra_in:]
    outs, refs = refs[:count], refs[count:]
    results, semaphores = refs[:extra_out], refs[extra_out:]
    mesh_ids = pl.DeviceIdType.MESH
    barrier = pltpu.get_barrier_semaphore()
    steps = []
    for number, (axis, n, shared, position, member) in enumerate(plans):
        src_ref, out_ref = sources[number], outs[number]
        local_sem, send_sem, recv_sem = semaphores[3 * number : 3 * number + 3]
        index = lax.axis_index(axis)
        pos = position(index)

        def peer_copy(q, slot, src_ref=src_ref, out_ref=out_ref, send_sem=send_sem,
                      recv_sem=recv_sem, axis=axis, member=member, index=index, shared=shared):
            return pltpu.make_async_remote_copy(
                src_ref=src_ref.at[0] if shared else src_ref.at[q],
                dst_ref=out_ref.at[slot],
                send_sem=send_sem.at[q],
                recv_sem=recv_sem.at[slot],
                device_id={axis: member(index, q)},
                device_id_type=mesh_ids,
            )

        def greet(k, carry, n=n, pos=pos, axis=axis, member=member, index=index):
            q = (pos + k) % n
            pl.semaphore_signal(
                barrier, inc=1, device_id={axis: member(index, q)}, device_id_type=mesh_ids
            )
            return carry

        lax.fori_loop(1, n, greet, 0)
        local = pltpu.make_async_copy(
            src_ref.at[0] if shared else src_ref.at[pos], out_ref.at[pos], local_sem
        )
        steps.append((n, pos, peer_copy, local))
    pl.semaphore_wait(barrier, sum(plan[1] - 1 for plan in plans))

    for n, pos, peer_copy, local in steps:
        local.start()

        def send(k, carry, n=n, pos=pos, peer_copy=peer_copy):
            peer_copy((pos + k) % n, pos).start()
            return carry

        lax.fori_loop(1, n, send, 0)

    if work is not None:
        work(*inputs, *results)

    for n, pos, peer_copy, local in steps:

        def finish(k, carry, n=n, pos=pos, peer_copy=peer_copy):
            q = (pos + k) % n
            peer_copy(q, pos).wait_send()
            peer_copy(q, q).wait_recv()
            return carry

        lax.fori_loop(1, n, finish, 0)
        local.wait()


def contiguous(n):
    return (lambda index: index % n, lambda index, q: index - index % n + q)


def plane_group(index):
    return (index // 8) * 2 + index % 2


def plane_member(index, q):
    return ((q // 2) * 4 + (index // 2) % 4) * 2 + q % 2


def token_block(zc, p):
    return ((p // 2) * 4 + zc) * 2 + p % 2


def plane_rows(rows_ref, q):
    return rows_ref.at[q // 2, :, q % 2]


def column_group(index):
    return (index // 2) % 4


def column_member(index, q):
    return ((index // 8) * 4 + q) * 2 + index % 2


def exchange_all(collective_id, *requests, work=None, inputs=(), results=()):
    plans, blocks, shapes, scratch = [], [], [], []
    for data, axis, n, shared, group in requests:
        position, member = group if group is not None else contiguous(n)
        plans.append((axis, n, shared, position, member))
        blocks.append(data)
        shapes.append(jax.ShapeDtypeStruct((n,) + data.shape[1:], data.dtype))
        scratch += [
            pltpu.SemaphoreType.DMA,
            pltpu.SemaphoreType.DMA((n,)),
            pltpu.SemaphoreType.DMA((n,)),
        ]
    operands = blocks + list(inputs)
    out_shapes = shapes + list(results)
    return pl.pallas_call(
        functools.partial(_exchange_kernel, tuple(plans), work, len(inputs), len(results)),
        out_shape=tuple(out_shapes),
        in_specs=[pl.BlockSpec(memory_space=pltpu.VMEM)] * len(operands),
        out_specs=tuple(pl.BlockSpec(memory_space=pltpu.VMEM) for _ in out_shapes),
        scratch_shapes=scratch,
        compiler_params=pltpu.CompilerParams(collective_id=collective_id, has_side_effects=True),
    )(*operands)


def exchange(blocks, axis, n, shared, collective_id, group=None):
    return exchange_all(collective_id, (blocks, axis, n, shared, group))[0]


def _feedforward(normed_ref, upward_ref, downward_ref, out_ref):
    upward = jnp.dot(normed_ref[...], upward_ref[...], preferred_element_type=jnp.float32)
    hidden = (0.5 * upward * (1.0 + lax.erf(upward * math.sqrt(0.5)))).astype(jnp.bfloat16)
    out_ref[...] = jnp.dot(hidden, downward_ref[...], preferred_element_type=jnp.float32)


def _greet(barrier, groups):
    index = lax.axis_index("tensor")
    total = 0
    for n, position, member in groups:
        pos = position(index)

        def greet(k, carry, n=n, pos=pos, member=member):
            pl.semaphore_signal(
                barrier,
                inc=1,
                device_id={"tensor": member(index, (pos + k) % n)},
                device_id_type=pl.DeviceIdType.MESH,
            )
            return carry

        lax.fori_loop(1, n, greet, 0)
        total += n - 1
    pl.semaphore_wait(barrier, total)


def _gather_kernel(n_col, n_plane, col, plane, slot, x_ref, out_ref, local_sem, send_sem, relay_sem, recv_sem):
    index = lax.axis_index("tensor")
    cpos, ppos = col[0](index), plane[0](index)
    mesh_ids = pl.DeviceIdType.MESH
    _greet(pltpu.get_barrier_semaphore(), [(n_col, *col), (n_plane, *plane)])

    def col_copy(q):
        return pltpu.make_async_remote_copy(
            x_ref, out_ref.at[slot(cpos, ppos)], send_sem.at[q], recv_sem.at[cpos, ppos],
            device_id={"tensor": col[1](index, q)}, device_id_type=mesh_ids,
        )

    def plane_copy(q):
        return pltpu.make_async_remote_copy(
            x_ref, out_ref.at[slot(cpos, ppos)], send_sem.at[n_col + q], recv_sem.at[cpos, ppos],
            device_id={"tensor": plane[1](index, q)}, device_id_type=mesh_ids,
        )

    def relay_copy(zc, q):
        return pltpu.make_async_remote_copy(
            out_ref.at[slot(zc, ppos)], out_ref.at[slot(zc, ppos)], relay_sem.at[zc, q], recv_sem.at[zc, ppos],
            device_id={"tensor": plane[1](index, q)}, device_id_type=mesh_ids,
        )

    def arrival(zc, p):
        return pltpu.make_async_remote_copy(
            x_ref, out_ref.at[slot(zc, p)], send_sem.at[0], recv_sem.at[zc, p],
            device_id={"tensor": index}, device_id_type=mesh_ids,
        )

    local = pltpu.make_async_copy(x_ref, out_ref.at[slot(cpos, ppos)], local_sem)
    local.start()

    def send_col(k, carry):
        col_copy((cpos + k) % n_col).start()
        return carry

    def send_plane(k, carry):
        plane_copy((ppos + k) % n_plane).start()
        return carry

    lax.fori_loop(1, n_col, send_col, 0)
    lax.fori_loop(1, n_plane, send_plane, 0)

    def relay(k, carry):
        zc = (cpos + k) % n_col
        arrival(zc, ppos).wait_recv()

        def forward(m, inner):
            relay_copy(zc, (ppos + m) % n_plane).start()
            return inner

        return lax.fori_loop(1, n_plane, forward, carry)

    lax.fori_loop(1, n_col, relay, 0)

    def finish_col(k, carry):
        col_copy((cpos + k) % n_col).wait_send()
        return carry

    def finish_plane(m, carry):
        q = (ppos + m) % n_plane
        plane_copy(q).wait_send()
        arrival(cpos, q).wait_recv()
        return carry

    def finish_relay(k, carry):
        zc = (cpos + k) % n_col

        def inner(m, c):
            q = (ppos + m) % n_plane
            relay_copy(zc, q).wait_send()
            arrival(zc, q).wait_recv()
            return c

        return lax.fori_loop(1, n_plane, inner, carry)

    lax.fori_loop(1, n_col, finish_col, 0)
    lax.fori_loop(1, n_plane, finish_plane, 0)
    lax.fori_loop(1, n_col, finish_relay, 0)
    local.wait()


def gather_tokens(x, col, plane, slot, n_col, n_plane, collective_id):
    return pl.pallas_call(
        functools.partial(_gather_kernel, n_col, n_plane, col, plane, slot),
        out_shape=jax.ShapeDtypeStruct((n_col * n_plane,) + x.shape, x.dtype),
        in_specs=[pl.BlockSpec(memory_space=pltpu.VMEM)],
        out_specs=pl.BlockSpec(memory_space=pltpu.VMEM),
        scratch_shapes=[
            pltpu.SemaphoreType.DMA,
            pltpu.SemaphoreType.DMA((n_col + n_plane,)),
            pltpu.SemaphoreType.DMA((n_col, n_plane)),
            pltpu.SemaphoreType.DMA((n_col, n_plane)),
        ],
        compiler_params=pltpu.CompilerParams(collective_id=collective_id, has_side_effects=True),
    )(x)


def _reduce_kernel(n_col, n_plane, col, plane, pick, rows_ref, x_ref, out_ref, inbox, stage, inbox2,
                   local_sem, send_sem, recv_sem, local2_sem, send2_sem, recv2_sem):
    index = lax.axis_index("tensor")
    cpos, ppos = col[0](index), plane[0](index)
    mesh_ids = pl.DeviceIdType.MESH
    _greet(pltpu.get_barrier_semaphore(), [(n_col, *col), (n_plane, *plane)])

    def plane_copy(q, slot):
        return pltpu.make_async_remote_copy(
            pick(rows_ref, q), inbox.at[slot], send_sem.at[q], recv_sem.at[slot],
            device_id={"tensor": plane[1](index, q)}, device_id_type=mesh_ids,
        )

    def col_copy(q, slot):
        return pltpu.make_async_remote_copy(
            stage.at[q], inbox2.at[slot], send2_sem.at[q], recv2_sem.at[slot],
            device_id={"tensor": col[1](index, q)}, device_id_type=mesh_ids,
        )

    local = pltpu.make_async_copy(pick(rows_ref, ppos), inbox.at[ppos], local_sem)
    local.start()

    def send_plane(m, carry):
        plane_copy((ppos + m) % n_plane, ppos).start()
        return carry

    lax.fori_loop(1, n_plane, send_plane, 0)

    def finish_plane(m, carry):
        q = (ppos + m) % n_plane
        plane_copy(q, ppos).wait_send()
        plane_copy(q, q).wait_recv()
        return carry

    lax.fori_loop(1, n_plane, finish_plane, 0)
    local.wait()

    total = inbox[0].astype(jnp.float32)
    for sender in range(1, n_plane):
        total = total + inbox[sender].astype(jnp.float32)
    stage[...] = total.astype(stage.dtype)

    local2 = pltpu.make_async_copy(stage.at[cpos], inbox2.at[cpos], local2_sem)
    local2.start()

    def send_col(k, carry):
        col_copy((cpos + k) % n_col, cpos).start()
        return carry

    lax.fori_loop(1, n_col, send_col, 0)

    def finish_col(k, carry):
        q = (cpos + k) % n_col
        col_copy(q, cpos).wait_send()
        col_copy(q, q).wait_recv()
        return carry

    lax.fori_loop(1, n_col, finish_col, 0)
    local2.wait()

    result = x_ref[...].astype(jnp.float32) + inbox2[0].astype(jnp.float32)
    for sender in range(1, n_col):
        result = result + inbox2[sender].astype(jnp.float32)
    out_ref[...] = result


def reduce_rows(rows, x, col, plane, pick, n_col, n_plane, collective_id):
    block = x.shape
    return pl.pallas_call(
        functools.partial(_reduce_kernel, n_col, n_plane, col, plane, pick),
        out_shape=jax.ShapeDtypeStruct(block, jnp.float32),
        in_specs=[pl.BlockSpec(memory_space=pltpu.VMEM)] * 2,
        out_specs=pl.BlockSpec(memory_space=pltpu.VMEM),
        scratch_shapes=[
            pltpu.VMEM((n_plane, n_col) + block, rows.dtype),
            pltpu.VMEM((n_col,) + block, rows.dtype),
            pltpu.VMEM((n_col,) + block, rows.dtype),
            pltpu.SemaphoreType.DMA,
            pltpu.SemaphoreType.DMA((n_plane,)),
            pltpu.SemaphoreType.DMA((n_plane,)),
            pltpu.SemaphoreType.DMA,
            pltpu.SemaphoreType.DMA((n_col,)),
            pltpu.SemaphoreType.DMA((n_col,)),
        ],
        compiler_params=pltpu.CompilerParams(collective_id=collective_id, has_side_effects=True),
    )(rows, x)


def shards(
    hidden_states,
    attention_gain,
    feedforward_gain,
    heads_weight,
    output_weight,
    upward_weight,
    downward_weight,
    segments,
    page_targets,
):
    tensor_count = lax.axis_size("tensor")
    replica_count = lax.axis_size("dp")
    tensor_index = lax.axis_index("tensor")
    quarters = tensor_count // H
    quarter_width = HD // quarters
    quarter_index = tensor_index % quarters
    stream = segments[0]
    tokens_total = stream.shape[0]
    local_rows = hidden_states.shape[0]

    width = hidden_states.shape[1]
    planes = tensor_count // 8
    gathered = gather_tokens(
        hidden_states,
        (column_group, column_member),
        (plane_group, plane_member),
        token_block,
        planes,
        8,
        0,
    )
    tokens = gathered.reshape(tokens_total, width)
    normed_attention = layer_norm(tokens, attention_gain)
    normed_feedforward = layer_norm(tokens, feedforward_gain)
    joined = jnp.dot(normed_attention, heads_weight, preferred_element_type=jnp.float32).astype(
        jnp.bfloat16
    )

    indices, starting = positions_of(stream)
    offsets = indices - starting
    query_piece = joined[:, :quarter_width]
    key_piece = joined[:, quarter_width : 2 * quarter_width]
    value_piece = joined[:, 2 * quarter_width :]
    leading = quarter_index == 0
    query_piece = jnp.where(leading, rotate_leading(query_piece, offsets, ROT), query_piece)
    key_piece = jnp.where(leading, rotate_leading(key_piece, offsets, ROT), key_piece)

    page_count = tokens_total // PAGE
    page_rows = jnp.concatenate([key_piece, value_piece], 1).reshape(
        page_count, PAGE * 2 * quarter_width
    )
    targets = page_targets[:, 0]
    page_numbers = jnp.arange(page_count, dtype=jnp.int32)
    earlier = jnp.sum(
        (
            (targets[None, :] == targets[:, None]) & (page_numbers[None, :] < page_numbers[:, None])
        ).astype(jnp.int32),
        axis=1,
    )
    capacity = 2 * page_count // replica_count
    slot_numbers = targets * capacity + earlier
    placing = (
        jnp.arange(replica_count * capacity, dtype=jnp.int32)[:, None] == slot_numbers[None, :]
    ).astype(jnp.bfloat16)
    outgoing = jnp.dot(placing, page_rows, preferred_element_type=jnp.float32).astype(jnp.bfloat16)
    outgoing = outgoing.reshape(replica_count, capacity * PAGE, 2 * quarter_width)
    head_pieces, incoming, feedforward = exchange_all(
        1,
        (jnp.concatenate([query_piece, key_piece], 1)[None], "tensor", quarters, True, None),
        (outgoing, "dp", replica_count, False, None),
        work=_feedforward,
        inputs=(normed_feedforward, upward_weight, downward_weight),
        results=(jax.ShapeDtypeStruct((tokens_total, width), jnp.float32),),
    )
    queries = head_pieces[:, :, :quarter_width].transpose(1, 0, 2).reshape(tokens_total, HD)
    keys = head_pieces[:, :, quarter_width:].transpose(1, 0, 2).reshape(tokens_total, HD)

    scores = jnp.dot(queries, keys.T, preferred_element_type=jnp.float32) * HD ** (-0.5)
    allowed = (stream[None, :] == stream[:, None]) & (indices[None, :] <= indices[:, None])
    peak = jnp.max(jnp.where(allowed, scores, -jnp.inf), axis=1, keepdims=True)
    weights = jnp.where(allowed, jnp.exp(scores - peak), 0.0)
    weight_sum = jnp.sum(weights, axis=1, keepdims=True)
    mixed = jnp.dot(weights.astype(jnp.bfloat16), value_piece, preferred_element_type=jnp.float32)
    attended = (mixed / weight_sum).astype(jnp.bfloat16)

    partial = (
        jnp.dot(attended, output_weight, preferred_element_type=jnp.float32) + feedforward
    ).astype(jnp.bfloat16)
    layer_output = reduce_rows(
        partial.reshape(4, planes, 2, local_rows, width),
        hidden_states,
        (column_group, column_member),
        (plane_group, plane_member),
        plane_rows,
        planes,
        8,
        2,
    )

    cache_pages = incoming.reshape(1, replica_count, capacity, PAGE, 2 * quarter_width)
    return (layer_output, cache_pages)


def solution(mesh):
    in_specs = (
        P(("dp", "tensor"), None),
        P(),
        P(),
        P(None, "tensor"),
        P("tensor", None),
        P(None, "tensor"),
        P("tensor", None),
        P("dp", None),
        P("dp", None),
    )
    out_specs = (P(("dp", "tensor"), None), P("dp", None, None, None, "tensor"))
    return jax.shard_map(shards, mesh=mesh, in_specs=in_specs, out_specs=out_specs, check_vma=False)
```

```python
import functools
import math

import jax
import jax.numpy as jnp
from jax import lax
from jax.experimental import pallas as pl
from jax.experimental.pallas import tpu as pltpu
from jax.sharding import PartitionSpec as P

H = 8
HD = 256
ROT = 64
PAGE = 16


epsilon = 1e-05
rotary_base = 10000.0


def layer_norm(values, gain):
    floats = values.astype(jnp.float32)
    center = jnp.mean(floats, axis=-1, keepdims=True)
    shifted = floats - center
    spread = jnp.mean(shifted * shifted, axis=-1, keepdims=True)
    return (shifted * lax.rsqrt(spread + epsilon) * gain).astype(jnp.bfloat16)


def positions_of(stream):
    indices = jnp.arange(stream.shape[0], dtype=jnp.int32)
    boundary = jnp.concatenate([jnp.ones((1,), dtype=bool), stream[1:] != stream[:-1]])
    starting = lax.cummax(jnp.where(boundary, indices, jnp.zeros_like(indices)), axis=0)
    return (indices, starting)


def rotate_leading(vectors, offsets, rotary_dims):
    half_dims = rotary_dims // 2
    frequency = jnp.exp(
        jnp.arange(half_dims, dtype=jnp.float32) * (-2.0 * math.log(rotary_base) / rotary_dims)
    )
    angles = offsets.astype(jnp.float32)[:, None] * frequency[None, :]
    cosine = jnp.cos(angles)
    sine = jnp.sin(angles)
    floats = vectors.astype(jnp.float32)
    leading = floats[..., :half_dims]
    trailing = floats[..., half_dims:rotary_dims]
    rotated = jnp.concatenate(
        [
            leading * cosine - trailing * sine,
            trailing * cosine + leading * sine,
            floats[..., rotary_dims:],
        ],
        axis=-1,
    )
    return rotated.astype(jnp.bfloat16)


def _exchange_kernel(plans, work, extra_in, extra_out, *refs):
    count = len(plans)
    sources, refs = refs[:count], refs[count:]
    inputs, refs = refs[:extra_in], refs[extra_in:]
    outs, refs = refs[:count], refs[count:]
    results, semaphores = refs[:extra_out], refs[extra_out:]
    mesh_ids = pl.DeviceIdType.MESH
    barrier = pltpu.get_barrier_semaphore()
    steps = []
    for number, (axis, n, shared, position, member) in enumerate(plans):
        src_ref, out_ref = sources[number], outs[number]
        local_sem, send_sem, recv_sem = semaphores[3 * number : 3 * number + 3]
        index = lax.axis_index(axis)
        pos = position(index)

        def peer_copy(q, slot, src_ref=src_ref, out_ref=out_ref, send_sem=send_sem,
                      recv_sem=recv_sem, axis=axis, member=member, index=index, shared=shared):
            return pltpu.make_async_remote_copy(
                src_ref=src_ref.at[0] if shared else src_ref.at[q],
                dst_ref=out_ref.at[slot],
                send_sem=send_sem.at[q],
                recv_sem=recv_sem.at[slot],
                device_id={axis: member(index, q)},
                device_id_type=mesh_ids,
            )

        def greet(k, carry, n=n, pos=pos, axis=axis, member=member, index=index):
            q = (pos + k) % n
            pl.semaphore_signal(
                barrier, inc=1, device_id={axis: member(index, q)}, device_id_type=mesh_ids
            )
            return carry

        lax.fori_loop(1, n, greet, 0)
        local = pltpu.make_async_copy(
            src_ref.at[0] if shared else src_ref.at[pos], out_ref.at[pos], local_sem
        )
        steps.append((n, pos, peer_copy, local))
    pl.semaphore_wait(barrier, sum(plan[1] - 1 for plan in plans))

    for n, pos, peer_copy, local in steps:
        local.start()

        def send(k, carry, n=n, pos=pos, peer_copy=peer_copy):
            peer_copy((pos + k) % n, pos).start()
            return carry

        lax.fori_loop(1, n, send, 0)

    if work is not None:
        work(*inputs, *results)

    for n, pos, peer_copy, local in steps:

        def finish(k, carry, n=n, pos=pos, peer_copy=peer_copy):
            q = (pos + k) % n
            peer_copy(q, pos).wait_send()
            peer_copy(q, q).wait_recv()
            return carry

        lax.fori_loop(1, n, finish, 0)
        local.wait()


def contiguous(n):
    return (lambda index: index % n, lambda index, q: index - index % n + q)


def plane_group(index):
    return (index // 8) * 2 + index % 2


def plane_member(index, q):
    return ((q // 2) * 4 + (index // 2) % 4) * 2 + q % 2


def token_block(zc, p):
    return ((p // 2) * 4 + zc) * 2 + p % 2


def plane_rows(rows_ref, q):
    return rows_ref.at[q // 2, :, q % 2]


def column_group(index):
    return (index // 2) % 4


def column_member(index, q):
    return ((index // 8) * 4 + q) * 2 + index % 2


def exchange_all(collective_id, *requests, work=None, inputs=(), results=()):
    plans, blocks, shapes, scratch = [], [], [], []
    for data, axis, n, shared, group in requests:
        position, member = group if group is not None else contiguous(n)
        plans.append((axis, n, shared, position, member))
        blocks.append(data)
        shapes.append(jax.ShapeDtypeStruct((n,) + data.shape[1:], data.dtype))
        scratch += [
            pltpu.SemaphoreType.DMA,
            pltpu.SemaphoreType.DMA((n,)),
            pltpu.SemaphoreType.DMA((n,)),
        ]
    operands = blocks + list(inputs)
    out_shapes = shapes + list(results)
    return pl.pallas_call(
        functools.partial(_exchange_kernel, tuple(plans), work, len(inputs), len(results)),
        out_shape=tuple(out_shapes),
        in_specs=[pl.BlockSpec(memory_space=pltpu.VMEM)] * len(operands),
        out_specs=tuple(pl.BlockSpec(memory_space=pltpu.VMEM) for _ in out_shapes),
        scratch_shapes=scratch,
        compiler_params=pltpu.CompilerParams(collective_id=collective_id, has_side_effects=True),
    )(*operands)


def exchange(blocks, axis, n, shared, collective_id, group=None):
    return exchange_all(collective_id, (blocks, axis, n, shared, group))[0]


def _feedforward(normed_ref, upward_ref, downward_ref, out_ref):
    upward = jnp.dot(normed_ref[...], upward_ref[...], preferred_element_type=jnp.float32)
    hidden = (0.5 * upward * (1.0 + lax.erf(upward * math.sqrt(0.5)))).astype(jnp.bfloat16)
    out_ref[...] = jnp.dot(hidden, downward_ref[...], preferred_element_type=jnp.float32)


def _greet(barrier, groups):
    index = lax.axis_index("tensor")
    total = 0
    for n, position, member in groups:
        pos = position(index)

        def greet(k, carry, n=n, pos=pos, member=member):
            pl.semaphore_signal(
                barrier,
                inc=1,
                device_id={"tensor": member(index, (pos + k) % n)},
                device_id_type=pl.DeviceIdType.MESH,
            )
            return carry

        lax.fori_loop(1, n, greet, 0)
        total += n - 1
    pl.semaphore_wait(barrier, total)


def _gather_kernel(n_col, n_plane, col, plane, slot, x_ref, out_ref, local_sem, send_sem, relay_sem, recv_sem):
    index = lax.axis_index("tensor")
    cpos, ppos = col[0](index), plane[0](index)
    mesh_ids = pl.DeviceIdType.MESH
    _greet(pltpu.get_barrier_semaphore(), [(n_col, *col), (n_plane, *plane)])

    def col_copy(q):
        return pltpu.make_async_remote_copy(
            x_ref, out_ref.at[slot(cpos, ppos)], send_sem.at[q], recv_sem.at[cpos, ppos],
            device_id={"tensor": col[1](index, q)}, device_id_type=mesh_ids,
        )

    def plane_copy(q):
        return pltpu.make_async_remote_copy(
            x_ref, out_ref.at[slot(cpos, ppos)], send_sem.at[n_col + q], recv_sem.at[cpos, ppos],
            device_id={"tensor": plane[1](index, q)}, device_id_type=mesh_ids,
        )

    def relay_copy(zc, q):
        return pltpu.make_async_remote_copy(
            out_ref.at[slot(zc, ppos)], out_ref.at[slot(zc, ppos)], relay_sem.at[zc, q], recv_sem.at[zc, ppos],
            device_id={"tensor": plane[1](index, q)}, device_id_type=mesh_ids,
        )

    def arrival(zc, p):
        return pltpu.make_async_remote_copy(
            x_ref, out_ref.at[slot(zc, p)], send_sem.at[0], recv_sem.at[zc, p],
            device_id={"tensor": index}, device_id_type=mesh_ids,
        )

    local = pltpu.make_async_copy(x_ref, out_ref.at[slot(cpos, ppos)], local_sem)
    local.start()

    def send_col(k, carry):
        col_copy((cpos + k) % n_col).start()
        return carry

    def send_plane(k, carry):
        plane_copy((ppos + k) % n_plane).start()
        return carry

    lax.fori_loop(1, n_col, send_col, 0)
    lax.fori_loop(1, n_plane, send_plane, 0)

    def relay(k, carry):
        zc = (cpos + k) % n_col
        arrival(zc, ppos).wait_recv()

        def forward(m, inner):
            relay_copy(zc, (ppos + m) % n_plane).start()
            return inner

        return lax.fori_loop(1, n_plane, forward, carry)

    lax.fori_loop(1, n_col, relay, 0)

    def finish_col(k, carry):
        col_copy((cpos + k) % n_col).wait_send()
        return carry

    def finish_plane(m, carry):
        q = (ppos + m) % n_plane
        plane_copy(q).wait_send()
        arrival(cpos, q).wait_recv()
        return carry

    def finish_relay(k, carry):
        zc = (cpos + k) % n_col

        def inner(m, c):
            q = (ppos + m) % n_plane
            relay_copy(zc, q).wait_send()
            arrival(zc, q).wait_recv()
            return c

        return lax.fori_loop(1, n_plane, inner, carry)

    lax.fori_loop(1, n_col, finish_col, 0)
    lax.fori_loop(1, n_plane, finish_plane, 0)
    lax.fori_loop(1, n_col, finish_relay, 0)
    local.wait()


def gather_tokens(x, col, plane, slot, n_col, n_plane, collective_id):
    return pl.pallas_call(
        functools.partial(_gather_kernel, n_col, n_plane, col, plane, slot),
        out_shape=jax.ShapeDtypeStruct((n_col * n_plane,) + x.shape, x.dtype),
        in_specs=[pl.BlockSpec(memory_space=pltpu.VMEM)],
        out_specs=pl.BlockSpec(memory_space=pltpu.VMEM),
        scratch_shapes=[
            pltpu.SemaphoreType.DMA,
            pltpu.SemaphoreType.DMA((n_col + n_plane,)),
            pltpu.SemaphoreType.DMA((n_col, n_plane)),
            pltpu.SemaphoreType.DMA((n_col, n_plane)),
        ],
        compiler_params=pltpu.CompilerParams(collective_id=collective_id, has_side_effects=True),
    )(x)


def _reduce_kernel(n_col, n_plane, col, plane, pick, rows_ref, x_ref, out_ref, inbox, stage, inbox2,
                   local_sem, send_sem, recv_sem, local2_sem, send2_sem, recv2_sem):
    index = lax.axis_index("tensor")
    cpos, ppos = col[0](index), plane[0](index)
    mesh_ids = pl.DeviceIdType.MESH
    _greet(pltpu.get_barrier_semaphore(), [(n_col, *col), (n_plane, *plane)])

    def plane_copy(q, slot):
        return pltpu.make_async_remote_copy(
            pick(rows_ref, q), inbox.at[slot], send_sem.at[q], recv_sem.at[slot],
            device_id={"tensor": plane[1](index, q)}, device_id_type=mesh_ids,
        )

    def col_copy(q, slot):
        return pltpu.make_async_remote_copy(
            stage.at[q], inbox2.at[slot], send2_sem.at[q], recv2_sem.at[slot],
            device_id={"tensor": col[1](index, q)}, device_id_type=mesh_ids,
        )

    local = pltpu.make_async_copy(pick(rows_ref, ppos), inbox.at[ppos], local_sem)
    local.start()

    def send_plane(m, carry):
        plane_copy((ppos + m) % n_plane, ppos).start()
        return carry

    lax.fori_loop(1, n_plane, send_plane, 0)

    def finish_plane(m, carry):
        q = (ppos + m) % n_plane
        plane_copy(q, ppos).wait_send()
        plane_copy(q, q).wait_recv()
        return carry

    lax.fori_loop(1, n_plane, finish_plane, 0)
    local.wait()

    total = inbox[0].astype(jnp.float32)
    for sender in range(1, n_plane):
        total = total + inbox[sender].astype(jnp.float32)
    stage[...] = total.astype(stage.dtype)

    local2 = pltpu.make_async_copy(stage.at[cpos], inbox2.at[cpos], local2_sem)
    local2.start()

    def send_col(k, carry):
        col_copy((cpos + k) % n_col, cpos).start()
        return carry

    lax.fori_loop(1, n_col, send_col, 0)

    def finish_col(k, carry):
        q = (cpos + k) % n_col
        col_copy(q, cpos).wait_send()
        col_copy(q, q).wait_recv()
        return carry

    lax.fori_loop(1, n_col, finish_col, 0)
    local2.wait()

    result = x_ref[...].astype(jnp.float32) + inbox2[0].astype(jnp.float32)
    for sender in range(1, n_col):
        result = result + inbox2[sender].astype(jnp.float32)
    out_ref[...] = result


def reduce_rows(rows, x, col, plane, pick, n_col, n_plane, collective_id):
    block = x.shape
    return pl.pallas_call(
        functools.partial(_reduce_kernel, n_col, n_plane, col, plane, pick),
        out_shape=jax.ShapeDtypeStruct(block, jnp.float32),
        in_specs=[pl.BlockSpec(memory_space=pltpu.VMEM)] * 2,
        out_specs=pl.BlockSpec(memory_space=pltpu.VMEM),
        scratch_shapes=[
            pltpu.VMEM((n_plane, n_col) + block, rows.dtype),
            pltpu.VMEM((n_col,) + block, rows.dtype),
            pltpu.VMEM((n_col,) + block, rows.dtype),
            pltpu.SemaphoreType.DMA,
            pltpu.SemaphoreType.DMA((n_plane,)),
            pltpu.SemaphoreType.DMA((n_plane,)),
            pltpu.SemaphoreType.DMA,
            pltpu.SemaphoreType.DMA((n_col,)),
            pltpu.SemaphoreType.DMA((n_col,)),
        ],
        compiler_params=pltpu.CompilerParams(collective_id=collective_id, has_side_effects=True),
    )(rows, x)


def shards(
    hidden_states,
    attention_gain,
    feedforward_gain,
    heads_weight,
    output_weight,
    upward_weight,
    downward_weight,
    segments,
    page_targets,
):
    tensor_count = lax.axis_size("tensor")
    replica_count = lax.axis_size("dp")
    tensor_index = lax.axis_index("tensor")
    quarters = tensor_count // H
    quarter_width = HD // quarters
    quarter_index = tensor_index % quarters
    stream = segments[0]
    tokens_total = stream.shape[0]
    local_rows = hidden_states.shape[0]

    width = hidden_states.shape[1]
    planes = tensor_count // 8
    gathered = gather_tokens(
        hidden_states,
        (column_group, column_member),
        (plane_group, plane_member),
        token_block,
        planes,
        8,
        0,
    )
    tokens = gathered.reshape(tokens_total, width)
    normed_attention = layer_norm(tokens, attention_gain)
    normed_feedforward = layer_norm(tokens, feedforward_gain)
    partner_weight = lax.ppermute(
        heads_weight[:, : 2 * quarter_width],
        "tensor",
        [(source, source ^ 2) for source in range(tensor_count)],
    )
    joined = jnp.dot(normed_attention, heads_weight, preferred_element_type=jnp.float32).astype(
        jnp.bfloat16
    )
    partner_joined = jnp.dot(
        normed_attention, partner_weight, preferred_element_type=jnp.float32
    ).astype(jnp.bfloat16)

    indices, starting = positions_of(stream)
    offsets = indices - starting
    query_piece = joined[:, :quarter_width]
    key_piece = joined[:, quarter_width : 2 * quarter_width]
    value_piece = joined[:, 2 * quarter_width :]
    partner_query = partner_joined[:, :quarter_width]
    partner_key = partner_joined[:, quarter_width:]
    leading = quarter_index == 0
    partner_leading = quarter_index == 2
    query_piece = jnp.where(leading, rotate_leading(query_piece, offsets, ROT), query_piece)
    key_piece = jnp.where(leading, rotate_leading(key_piece, offsets, ROT), key_piece)
    partner_query = jnp.where(
        partner_leading, rotate_leading(partner_query, offsets, ROT), partner_query
    )
    partner_key = jnp.where(partner_leading, rotate_leading(partner_key, offsets, ROT), partner_key)
    held = jnp.concatenate([query_piece, key_piece, partner_query, partner_key], 1)

    page_count = tokens_total // PAGE
    page_rows = jnp.concatenate([key_piece, value_piece], 1).reshape(
        page_count, PAGE * 2 * quarter_width
    )
    targets = page_targets[:, 0]
    page_numbers = jnp.arange(page_count, dtype=jnp.int32)
    earlier = jnp.sum(
        (
            (targets[None, :] == targets[:, None]) & (page_numbers[None, :] < page_numbers[:, None])
        ).astype(jnp.int32),
        axis=1,
    )
    capacity = 2 * page_count // replica_count
    slot_numbers = targets * capacity + earlier
    placing = (
        jnp.arange(replica_count * capacity, dtype=jnp.int32)[:, None] == slot_numbers[None, :]
    ).astype(jnp.bfloat16)
    outgoing = jnp.dot(placing, page_rows, preferred_element_type=jnp.float32).astype(jnp.bfloat16)
    outgoing = outgoing.reshape(replica_count, capacity * PAGE, 2 * quarter_width)
    head_pieces, incoming, feedforward = exchange_all(
        1,
        (held[None], "tensor", 2, True, None),
        (outgoing, "dp", replica_count, False, None),
        work=_feedforward,
        inputs=(normed_feedforward, upward_weight, downward_weight),
        results=(jax.ShapeDtypeStruct((tokens_total, width), jnp.float32),),
    )
    pieces = head_pieces.reshape(2, tokens_total, 2, 2, quarter_width)
    pieces = jnp.where(quarter_index // 2 == 0, pieces, pieces[:, :, ::-1])
    queries = pieces[:, :, :, 0].transpose(1, 2, 0, 3).reshape(tokens_total, HD)
    keys = pieces[:, :, :, 1].transpose(1, 2, 0, 3).reshape(tokens_total, HD)

    scores = jnp.dot(queries, keys.T, preferred_element_type=jnp.float32) * HD ** (-0.5)
    allowed = (stream[None, :] == stream[:, None]) & (indices[None, :] <= indices[:, None])
    peak = jnp.max(jnp.where(allowed, scores, -jnp.inf), axis=1, keepdims=True)
    weights = jnp.where(allowed, jnp.exp(scores - peak), 0.0)
    weight_sum = jnp.sum(weights, axis=1, keepdims=True)
    mixed = jnp.dot(weights.astype(jnp.bfloat16), value_piece, preferred_element_type=jnp.float32)
    attended = (mixed / weight_sum).astype(jnp.bfloat16)

    partial = (
        jnp.dot(attended, output_weight, preferred_element_type=jnp.float32) + feedforward
    ).astype(jnp.bfloat16)
    layer_output = reduce_rows(
        partial.reshape(4, planes, 2, local_rows, width),
        hidden_states,
        (column_group, column_member),
        (plane_group, plane_member),
        plane_rows,
        planes,
        8,
        2,
    )

    cache_pages = incoming.reshape(1, replica_count, capacity, PAGE, 2 * quarter_width)
    return (layer_output, cache_pages)


def solution(mesh):
    in_specs = (
        P(("dp", "tensor"), None),
        P(),
        P(),
        P(None, "tensor"),
        P("tensor", None),
        P(None, "tensor"),
        P("tensor", None),
        P("dp", None),
        P("dp", None),
    )
    out_specs = (P(("dp", "tensor"), None), P("dp", None, None, None, "tensor"))
    return jax.shard_map(shards, mesh=mesh, in_specs=in_specs, out_specs=out_specs, check_vma=False)
```

```python
import functools
import math

import jax
import jax.numpy as jnp
from jax import lax
from jax.experimental import pallas as pl
from jax.experimental.pallas import tpu as pltpu
from jax.sharding import PartitionSpec as P

H = 8
HD = 256
ROT = 64
PAGE = 16


epsilon = 1e-05
rotary_base = 10000.0


def layer_norm(values, gain):
    floats = values.astype(jnp.float32)
    center = jnp.mean(floats, axis=-1, keepdims=True)
    shifted = floats - center
    spread = jnp.mean(shifted * shifted, axis=-1, keepdims=True)
    return (shifted * lax.rsqrt(spread + epsilon) * gain).astype(jnp.bfloat16)


def positions_of(stream):
    indices = jnp.arange(stream.shape[0], dtype=jnp.int32)
    boundary = jnp.concatenate([jnp.ones((1,), dtype=bool), stream[1:] != stream[:-1]])
    starting = lax.cummax(jnp.where(boundary, indices, jnp.zeros_like(indices)), axis=0)
    return (indices, starting)


def rotate_leading(vectors, offsets, rotary_dims):
    half_dims = rotary_dims // 2
    frequency = jnp.exp(
        jnp.arange(half_dims, dtype=jnp.float32) * (-2.0 * math.log(rotary_base) / rotary_dims)
    )
    angles = offsets.astype(jnp.float32)[:, None] * frequency[None, :]
    cosine = jnp.cos(angles)
    sine = jnp.sin(angles)
    floats = vectors.astype(jnp.float32)
    leading = floats[..., :half_dims]
    trailing = floats[..., half_dims:rotary_dims]
    rotated = jnp.concatenate(
        [
            leading * cosine - trailing * sine,
            trailing * cosine + leading * sine,
            floats[..., rotary_dims:],
        ],
        axis=-1,
    )
    return rotated.astype(jnp.bfloat16)


def _exchange_kernel(plans, work, extra_in, extra_out, *refs):
    count = len(plans)
    sources, refs = refs[:count], refs[count:]
    inputs, refs = refs[:extra_in], refs[extra_in:]
    outs, refs = refs[:count], refs[count:]
    results, semaphores = refs[:extra_out], refs[extra_out:]
    mesh_ids = pl.DeviceIdType.MESH
    barrier = pltpu.get_barrier_semaphore()
    steps = []
    for number, (axis, n, shared, position, member) in enumerate(plans):
        src_ref, out_ref = sources[number], outs[number]
        local_sem, send_sem, recv_sem = semaphores[3 * number : 3 * number + 3]
        index = lax.axis_index(axis)
        pos = position(index)

        def peer_copy(q, slot, src_ref=src_ref, out_ref=out_ref, send_sem=send_sem,
                      recv_sem=recv_sem, axis=axis, member=member, index=index, shared=shared):
            return pltpu.make_async_remote_copy(
                src_ref=src_ref.at[0] if shared else src_ref.at[q],
                dst_ref=out_ref.at[slot],
                send_sem=send_sem.at[q],
                recv_sem=recv_sem.at[slot],
                device_id={axis: member(index, q)},
                device_id_type=mesh_ids,
            )

        def greet(k, carry, n=n, pos=pos, axis=axis, member=member, index=index):
            q = (pos + k) % n
            pl.semaphore_signal(
                barrier, inc=1, device_id={axis: member(index, q)}, device_id_type=mesh_ids
            )
            return carry

        lax.fori_loop(1, n, greet, 0)
        local = pltpu.make_async_copy(
            src_ref.at[0] if shared else src_ref.at[pos], out_ref.at[pos], local_sem
        )
        steps.append((n, pos, peer_copy, local))
    pl.semaphore_wait(barrier, sum(plan[1] - 1 for plan in plans))

    for n, pos, peer_copy, local in steps:
        local.start()

        def send(k, carry, n=n, pos=pos, peer_copy=peer_copy):
            peer_copy((pos + k) % n, pos).start()
            return carry

        lax.fori_loop(1, n, send, 0)

    if work is not None:
        work(*inputs, *results)

    for n, pos, peer_copy, local in steps:

        def finish(k, carry, n=n, pos=pos, peer_copy=peer_copy):
            q = (pos + k) % n
            peer_copy(q, pos).wait_send()
            peer_copy(q, q).wait_recv()
            return carry

        lax.fori_loop(1, n, finish, 0)
        local.wait()


def contiguous(n):
    return (lambda index: index % n, lambda index, q: index - index % n + q)


def plane_group(index):
    return (index // 8) * 2 + index % 2


def plane_member(index, q):
    return ((q // 2) * 4 + (index // 2) % 4) * 2 + q % 2


def token_block(zc, p):
    return ((p // 2) * 4 + zc) * 2 + p % 2


def plane_rows(rows_ref, q, z):
    return rows_ref.at[q // 2, z, q % 2]


def column_group(index):
    return (index // 2) % 4


def column_member(index, q):
    return ((index // 8) * 4 + q) * 2 + index % 2


def exchange_all(collective_id, *requests, work=None, inputs=(), results=()):
    plans, blocks, shapes, scratch = [], [], [], []
    for data, axis, n, shared, group in requests:
        position, member = group if group is not None else contiguous(n)
        plans.append((axis, n, shared, position, member))
        blocks.append(data)
        shapes.append(jax.ShapeDtypeStruct((n,) + data.shape[1:], data.dtype))
        scratch += [
            pltpu.SemaphoreType.DMA,
            pltpu.SemaphoreType.DMA((n,)),
            pltpu.SemaphoreType.DMA((n,)),
        ]
    operands = blocks + list(inputs)
    out_shapes = shapes + list(results)
    return pl.pallas_call(
        functools.partial(_exchange_kernel, tuple(plans), work, len(inputs), len(results)),
        out_shape=tuple(out_shapes),
        in_specs=[pl.BlockSpec(memory_space=pltpu.VMEM)] * len(operands),
        out_specs=tuple(pl.BlockSpec(memory_space=pltpu.VMEM) for _ in out_shapes),
        scratch_shapes=scratch,
        compiler_params=pltpu.CompilerParams(collective_id=collective_id, has_side_effects=True),
    )(*operands)


def exchange(blocks, axis, n, shared, collective_id, group=None):
    return exchange_all(collective_id, (blocks, axis, n, shared, group))[0]


def _feedforward(normed_ref, upward_ref, downward_ref, out_ref):
    upward = jnp.dot(normed_ref[...], upward_ref[...], preferred_element_type=jnp.float32)
    hidden = (0.5 * upward * (1.0 + lax.erf(upward * math.sqrt(0.5)))).astype(jnp.bfloat16)
    out_ref[...] = jnp.dot(hidden, downward_ref[...], preferred_element_type=jnp.float32)


def _greet(barrier, groups):
    index = lax.axis_index("tensor")
    total = 0
    for n, position, member in groups:
        pos = position(index)

        def greet(k, carry, n=n, pos=pos, member=member):
            pl.semaphore_signal(
                barrier,
                inc=1,
                device_id={"tensor": member(index, (pos + k) % n)},
                device_id_type=pl.DeviceIdType.MESH,
            )
            return carry

        lax.fori_loop(1, n, greet, 0)
        total += n - 1
    pl.semaphore_wait(barrier, total)


def _gather_kernel(n_col, n_plane, col, plane, slot, x_ref, out_ref, local_sem, send_sem, relay_sem, recv_sem):
    index = lax.axis_index("tensor")
    cpos, ppos = col[0](index), plane[0](index)
    mesh_ids = pl.DeviceIdType.MESH
    _greet(pltpu.get_barrier_semaphore(), [(n_col, *col), (n_plane, *plane)])

    def col_copy(q):
        return pltpu.make_async_remote_copy(
            x_ref, out_ref.at[slot(cpos, ppos)], send_sem.at[q], recv_sem.at[cpos, ppos],
            device_id={"tensor": col[1](index, q)}, device_id_type=mesh_ids,
        )

    def plane_copy(q):
        return pltpu.make_async_remote_copy(
            x_ref, out_ref.at[slot(cpos, ppos)], send_sem.at[n_col + q], recv_sem.at[cpos, ppos],
            device_id={"tensor": plane[1](index, q)}, device_id_type=mesh_ids,
        )

    def relay_copy(zc, q):
        return pltpu.make_async_remote_copy(
            out_ref.at[slot(zc, ppos)], out_ref.at[slot(zc, ppos)], relay_sem.at[zc, q], recv_sem.at[zc, ppos],
            device_id={"tensor": plane[1](index, q)}, device_id_type=mesh_ids,
        )

    def arrival(zc, p):
        return pltpu.make_async_remote_copy(
            x_ref, out_ref.at[slot(zc, p)], send_sem.at[0], recv_sem.at[zc, p],
            device_id={"tensor": index}, device_id_type=mesh_ids,
        )

    local = pltpu.make_async_copy(x_ref, out_ref.at[slot(cpos, ppos)], local_sem)
    local.start()

    def send_col(k, carry):
        col_copy((cpos + k) % n_col).start()
        return carry

    def send_plane(k, carry):
        plane_copy((ppos + k) % n_plane).start()
        return carry

    lax.fori_loop(1, n_col, send_col, 0)
    lax.fori_loop(1, n_plane, send_plane, 0)

    def relay(k, carry):
        zc = (cpos + k) % n_col
        arrival(zc, ppos).wait_recv()

        def forward(m, inner):
            relay_copy(zc, (ppos + m) % n_plane).start()
            return inner

        return lax.fori_loop(1, n_plane, forward, carry)

    lax.fori_loop(1, n_col, relay, 0)

    def finish_col(k, carry):
        col_copy((cpos + k) % n_col).wait_send()
        return carry

    def finish_plane(m, carry):
        q = (ppos + m) % n_plane
        plane_copy(q).wait_send()
        arrival(cpos, q).wait_recv()
        return carry

    def finish_relay(k, carry):
        zc = (cpos + k) % n_col

        def inner(m, c):
            q = (ppos + m) % n_plane
            relay_copy(zc, q).wait_send()
            arrival(zc, q).wait_recv()
            return c

        return lax.fori_loop(1, n_plane, inner, carry)

    lax.fori_loop(1, n_col, finish_col, 0)
    lax.fori_loop(1, n_plane, finish_plane, 0)
    lax.fori_loop(1, n_col, finish_relay, 0)
    local.wait()


def gather_tokens(x, col, plane, slot, n_col, n_plane, collective_id):
    return pl.pallas_call(
        functools.partial(_gather_kernel, n_col, n_plane, col, plane, slot),
        out_shape=jax.ShapeDtypeStruct((n_col * n_plane,) + x.shape, x.dtype),
        in_specs=[pl.BlockSpec(memory_space=pltpu.VMEM)],
        out_specs=pl.BlockSpec(memory_space=pltpu.VMEM),
        scratch_shapes=[
            pltpu.SemaphoreType.DMA,
            pltpu.SemaphoreType.DMA((n_col + n_plane,)),
            pltpu.SemaphoreType.DMA((n_col, n_plane)),
            pltpu.SemaphoreType.DMA((n_col, n_plane)),
        ],
        compiler_params=pltpu.CompilerParams(collective_id=collective_id, has_side_effects=True),
    )(x)


def _reduce_kernel(n_col, n_plane, col, plane, pick, rows_ref, x_ref, out_ref, inbox, stage, inbox2,
                   local_sem, send_sem, recv_sem, send2_sem, recv2_sem):
    index = lax.axis_index("tensor")
    cpos, ppos = col[0](index), plane[0](index)
    mesh_ids = pl.DeviceIdType.MESH
    _greet(pltpu.get_barrier_semaphore(), [(n_col, *col), (n_plane, *plane)])

    def plane_copy(q, z, slot):
        return pltpu.make_async_remote_copy(
            pick(rows_ref, q, z), inbox.at[z, slot], send_sem.at[z, q], recv_sem.at[z, slot],
            device_id={"tensor": plane[1](index, q)}, device_id_type=mesh_ids,
        )

    def col_copy(q, slot):
        return pltpu.make_async_remote_copy(
            stage.at[q], inbox2.at[slot], send2_sem.at[q], recv2_sem.at[slot],
            device_id={"tensor": col[1](index, q)}, device_id_type=mesh_ids,
        )

    order = [(cpos + 1 + k) % n_col for k in range(n_col)]
    locals_ = []
    for z in order:
        local = pltpu.make_async_copy(pick(rows_ref, ppos, z), inbox.at[z, ppos], local_sem.at[z])
        local.start()
        locals_.append(local)

        def send_plane(m, carry, z=z):
            plane_copy((ppos + m) % n_plane, z, ppos).start()
            return carry

        lax.fori_loop(1, n_plane, send_plane, 0)

    def plane_sum(z, local):
        def arrive(m, carry):
            plane_copy((ppos + m) % n_plane, z, (ppos + m) % n_plane).wait_recv()
            return carry

        lax.fori_loop(1, n_plane, arrive, 0)
        local.wait()
        total = inbox[z, 0].astype(jnp.float32)
        for sender in range(1, n_plane):
            total = total + inbox[z, sender].astype(jnp.float32)
        return total

    for z, local in zip(order[:-1], locals_[:-1]):
        stage[z] = plane_sum(z, local).astype(stage.dtype)
        col_copy(z, cpos).start()

    result = x_ref[...].astype(jnp.float32) + plane_sum(cpos, locals_[-1])

    def finish_plane(m, carry):
        q = (ppos + m) % n_plane
        for z in order:
            plane_copy(q, z, ppos).wait_send()
        return carry

    lax.fori_loop(1, n_plane, finish_plane, 0)

    for z in order[:-1]:
        col_copy(z, cpos).wait_send()
        col_copy(z, z).wait_recv()
        result = result + inbox2[z].astype(jnp.float32)
    out_ref[...] = result


def reduce_rows(rows, x, col, plane, pick, n_col, n_plane, collective_id):
    block = x.shape
    return pl.pallas_call(
        functools.partial(_reduce_kernel, n_col, n_plane, col, plane, pick),
        out_shape=jax.ShapeDtypeStruct(block, jnp.float32),
        in_specs=[pl.BlockSpec(memory_space=pltpu.VMEM)] * 2,
        out_specs=pl.BlockSpec(memory_space=pltpu.VMEM),
        scratch_shapes=[
            pltpu.VMEM((n_col, n_plane) + block, rows.dtype),
            pltpu.VMEM((n_col,) + block, rows.dtype),
            pltpu.VMEM((n_col,) + block, rows.dtype),
            pltpu.SemaphoreType.DMA((n_col,)),
            pltpu.SemaphoreType.DMA((n_col, n_plane)),
            pltpu.SemaphoreType.DMA((n_col, n_plane)),
            pltpu.SemaphoreType.DMA((n_col,)),
            pltpu.SemaphoreType.DMA((n_col,)),
        ],
        compiler_params=pltpu.CompilerParams(collective_id=collective_id, has_side_effects=True),
    )(rows, x)


def shards(
    hidden_states,
    attention_gain,
    feedforward_gain,
    heads_weight,
    output_weight,
    upward_weight,
    downward_weight,
    segments,
    page_targets,
):
    tensor_count = lax.axis_size("tensor")
    replica_count = lax.axis_size("dp")
    tensor_index = lax.axis_index("tensor")
    quarters = tensor_count // H
    quarter_width = HD // quarters
    quarter_index = tensor_index % quarters
    stream = segments[0]
    tokens_total = stream.shape[0]
    local_rows = hidden_states.shape[0]

    width = hidden_states.shape[1]
    planes = tensor_count // 8
    gathered = gather_tokens(
        hidden_states,
        (column_group, column_member),
        (plane_group, plane_member),
        token_block,
        planes,
        8,
        0,
    )
    tokens = gathered.reshape(tokens_total, width)
    normed_attention = layer_norm(tokens, attention_gain)
    normed_feedforward = layer_norm(tokens, feedforward_gain)
    joined = jnp.dot(normed_attention, heads_weight, preferred_element_type=jnp.float32).astype(
        jnp.bfloat16
    )

    indices, starting = positions_of(stream)
    offsets = indices - starting
    query_piece = joined[:, :quarter_width]
    key_piece = joined[:, quarter_width : 2 * quarter_width]
    value_piece = joined[:, 2 * quarter_width :]
    leading = quarter_index == 0
    query_piece = jnp.where(leading, rotate_leading(query_piece, offsets, ROT), query_piece)
    key_piece = jnp.where(leading, rotate_leading(key_piece, offsets, ROT), key_piece)

    page_count = tokens_total // PAGE
    page_rows = jnp.concatenate([key_piece, value_piece], 1).reshape(
        page_count, PAGE * 2 * quarter_width
    )
    targets = page_targets[:, 0]
    page_numbers = jnp.arange(page_count, dtype=jnp.int32)
    earlier = jnp.sum(
        (
            (targets[None, :] == targets[:, None]) & (page_numbers[None, :] < page_numbers[:, None])
        ).astype(jnp.int32),
        axis=1,
    )
    capacity = 2 * page_count // replica_count
    slot_numbers = targets * capacity + earlier
    placing = (
        jnp.arange(replica_count * capacity, dtype=jnp.int32)[:, None] == slot_numbers[None, :]
    ).astype(jnp.bfloat16)
    outgoing = jnp.dot(placing, page_rows, preferred_element_type=jnp.float32).astype(jnp.bfloat16)
    outgoing = outgoing.reshape(replica_count, capacity * PAGE, 2 * quarter_width)
    head_pieces, incoming, feedforward = exchange_all(
        1,
        (jnp.concatenate([query_piece, key_piece], 1)[None], "tensor", quarters, True, None),
        (outgoing, "dp", replica_count, False, None),
        work=_feedforward,
        inputs=(normed_feedforward, upward_weight, downward_weight),
        results=(jax.ShapeDtypeStruct((tokens_total, width), jnp.float32),),
    )
    queries = head_pieces[:, :, :quarter_width].transpose(1, 0, 2).reshape(tokens_total, HD)
    keys = head_pieces[:, :, quarter_width:].transpose(1, 0, 2).reshape(tokens_total, HD)

    scores = jnp.dot(queries, keys.T, preferred_element_type=jnp.float32) * HD ** (-0.5)
    allowed = (stream[None, :] == stream[:, None]) & (indices[None, :] <= indices[:, None])
    peak = jnp.max(jnp.where(allowed, scores, -jnp.inf), axis=1, keepdims=True)
    weights = jnp.where(allowed, jnp.exp(scores - peak), 0.0)
    weight_sum = jnp.sum(weights, axis=1, keepdims=True)
    mixed = jnp.dot(weights.astype(jnp.bfloat16), value_piece, preferred_element_type=jnp.float32)
    attended = (mixed / weight_sum).astype(jnp.bfloat16)

    partial = (
        jnp.dot(attended, output_weight, preferred_element_type=jnp.float32) + feedforward
    ).astype(jnp.bfloat16)
    layer_output = reduce_rows(
        partial.reshape(4, planes, 2, local_rows, width),
        hidden_states,
        (column_group, column_member),
        (plane_group, plane_member),
        plane_rows,
        planes,
        8,
        2,
    )

    cache_pages = incoming.reshape(1, replica_count, capacity, PAGE, 2 * quarter_width)
    return (layer_output, cache_pages)


def solution(mesh):
    in_specs = (
        P(("dp", "tensor"), None),
        P(),
        P(),
        P(None, "tensor"),
        P("tensor", None),
        P(None, "tensor"),
        P("tensor", None),
        P("dp", None),
        P("dp", None),
    )
    out_specs = (P(("dp", "tensor"), None), P("dp", None, None, None, "tensor"))
    return jax.shard_map(shards, mesh=mesh, in_specs=in_specs, out_specs=out_specs, check_vma=False)
```

```python
import functools
import math

import jax
import jax.numpy as jnp
from jax import lax
from jax.experimental import pallas as pl
from jax.experimental.pallas import tpu as pltpu
from jax.sharding import PartitionSpec as P

H = 8
HD = 256
ROT = 64
PAGE = 16


epsilon = 1e-05
rotary_base = 10000.0


def layer_norm(values, gain):
    floats = values.astype(jnp.float32)
    center = jnp.mean(floats, axis=-1, keepdims=True)
    shifted = floats - center
    spread = jnp.mean(shifted * shifted, axis=-1, keepdims=True)
    return (shifted * lax.rsqrt(spread + epsilon) * gain).astype(jnp.bfloat16)


def positions_of(stream):
    indices = jnp.arange(stream.shape[0], dtype=jnp.int32)
    boundary = jnp.concatenate([jnp.ones((1,), dtype=bool), stream[1:] != stream[:-1]])
    starting = lax.cummax(jnp.where(boundary, indices, jnp.zeros_like(indices)), axis=0)
    return (indices, starting)


def rotate_leading(vectors, offsets, rotary_dims):
    half_dims = rotary_dims // 2
    frequency = jnp.exp(
        jnp.arange(half_dims, dtype=jnp.float32) * (-2.0 * math.log(rotary_base) / rotary_dims)
    )
    angles = offsets.astype(jnp.float32)[:, None] * frequency[None, :]
    cosine = jnp.cos(angles)
    sine = jnp.sin(angles)
    floats = vectors.astype(jnp.float32)
    leading = floats[..., :half_dims]
    trailing = floats[..., half_dims:rotary_dims]
    rotated = jnp.concatenate(
        [
            leading * cosine - trailing * sine,
            trailing * cosine + leading * sine,
            floats[..., rotary_dims:],
        ],
        axis=-1,
    )
    return rotated.astype(jnp.bfloat16)


def _exchange_kernel(plans, work, extra_in, extra_out, *refs):
    count = len(plans)
    sources, refs = refs[:count], refs[count:]
    inputs, refs = refs[:extra_in], refs[extra_in:]
    outs, refs = refs[:count], refs[count:]
    results, semaphores = refs[:extra_out], refs[extra_out:]
    mesh_ids = pl.DeviceIdType.MESH
    barrier = pltpu.get_barrier_semaphore()
    steps = []
    for number, (axis, n, shared, position, member) in enumerate(plans):
        src_ref, out_ref = sources[number], outs[number]
        local_sem, send_sem, recv_sem = semaphores[3 * number : 3 * number + 3]
        index = lax.axis_index(axis)
        pos = position(index)

        def peer_copy(q, slot, src_ref=src_ref, out_ref=out_ref, send_sem=send_sem,
                      recv_sem=recv_sem, axis=axis, member=member, index=index, shared=shared):
            return pltpu.make_async_remote_copy(
                src_ref=src_ref.at[0] if shared else src_ref.at[q],
                dst_ref=out_ref.at[slot],
                send_sem=send_sem.at[q],
                recv_sem=recv_sem.at[slot],
                device_id={axis: member(index, q)},
                device_id_type=mesh_ids,
            )

        def greet(k, carry, n=n, pos=pos, axis=axis, member=member, index=index):
            q = (pos + k) % n
            pl.semaphore_signal(
                barrier, inc=1, device_id={axis: member(index, q)}, device_id_type=mesh_ids
            )
            return carry

        lax.fori_loop(1, n, greet, 0)
        local = pltpu.make_async_copy(
            src_ref.at[0] if shared else src_ref.at[pos], out_ref.at[pos], local_sem
        )
        steps.append((n, pos, peer_copy, local))
    carried = work[0](*inputs) if work is not None else None
    pl.semaphore_wait(barrier, sum(plan[1] - 1 for plan in plans))

    for n, pos, peer_copy, local in steps:
        local.start()

        def send(k, carry, n=n, pos=pos, peer_copy=peer_copy):
            peer_copy((pos + k) % n, pos).start()
            return carry

        lax.fori_loop(1, n, send, 0)

    if work is not None:
        work[1](carried, *inputs, *results)

    for n, pos, peer_copy, local in steps:

        def finish(k, carry, n=n, pos=pos, peer_copy=peer_copy):
            q = (pos + k) % n
            peer_copy(q, pos).wait_send()
            peer_copy(q, q).wait_recv()
            return carry

        lax.fori_loop(1, n, finish, 0)
        local.wait()


def contiguous(n):
    return (lambda index: index % n, lambda index, q: index - index % n + q)


def plane_group(index):
    return (index // 8) * 2 + index % 2


def plane_member(index, q):
    return ((q // 2) * 4 + (index // 2) % 4) * 2 + q % 2


def token_block(zc, p):
    return ((p // 2) * 4 + zc) * 2 + p % 2


def plane_rows(rows_ref, q, z):
    return rows_ref.at[q // 2, z, q % 2]


def column_group(index):
    return (index // 2) % 4


def column_member(index, q):
    return ((index // 8) * 4 + q) * 2 + index % 2


def exchange_all(collective_id, *requests, work=None, inputs=(), results=()):
    plans, blocks, shapes, scratch = [], [], [], []
    for data, axis, n, shared, group in requests:
        position, member = group if group is not None else contiguous(n)
        plans.append((axis, n, shared, position, member))
        blocks.append(data)
        shapes.append(jax.ShapeDtypeStruct((n,) + data.shape[1:], data.dtype))
        scratch += [
            pltpu.SemaphoreType.DMA,
            pltpu.SemaphoreType.DMA((n,)),
            pltpu.SemaphoreType.DMA((n,)),
        ]
    operands = blocks + list(inputs)
    out_shapes = shapes + list(results)
    return pl.pallas_call(
        functools.partial(_exchange_kernel, tuple(plans), work, len(inputs), len(results)),
        out_shape=tuple(out_shapes),
        in_specs=[pl.BlockSpec(memory_space=pltpu.VMEM)] * len(operands),
        out_specs=tuple(pl.BlockSpec(memory_space=pltpu.VMEM) for _ in out_shapes),
        scratch_shapes=scratch,
        compiler_params=pltpu.CompilerParams(collective_id=collective_id, has_side_effects=True),
    )(*operands)


def exchange(blocks, axis, n, shared, collective_id, group=None):
    return exchange_all(collective_id, (blocks, axis, n, shared, group))[0]


def _feedforward_up(normed_ref, upward_ref, downward_ref):
    upward = jnp.dot(normed_ref[...], upward_ref[...], preferred_element_type=jnp.float32)
    return (0.5 * upward * (1.0 + lax.erf(upward * math.sqrt(0.5)))).astype(jnp.bfloat16)


def _feedforward_down(hidden, normed_ref, upward_ref, downward_ref, out_ref):
    out_ref[...] = jnp.dot(hidden, downward_ref[...], preferred_element_type=jnp.float32)


def _greet(barrier, groups, extra=0):
    index = lax.axis_index("tensor")
    total = 0
    for n, position, member in groups:
        pos = position(index)

        def greet(k, carry, n=n, pos=pos, member=member):
            pl.semaphore_signal(
                barrier,
                inc=1,
                device_id={"tensor": member(index, (pos + k) % n)},
                device_id_type=pl.DeviceIdType.MESH,
            )
            return carry

        lax.fori_loop(1, n, greet, 0)
        total += n - 1
    pl.semaphore_wait(barrier, total + extra)


def _gather_kernel(n_col, n_plane, col, plane, slot, x_ref, out_ref, local_sem, send_sem, relay_sem, recv_sem):
    index = lax.axis_index("tensor")
    cpos, ppos = col[0](index), plane[0](index)
    mesh_ids = pl.DeviceIdType.MESH
    _greet(pltpu.get_barrier_semaphore(), [(n_col, *col), (n_plane, *plane)])

    def col_copy(q):
        return pltpu.make_async_remote_copy(
            x_ref, out_ref.at[slot(cpos, ppos)], send_sem.at[q], recv_sem.at[cpos, ppos],
            device_id={"tensor": col[1](index, q)}, device_id_type=mesh_ids,
        )

    def plane_copy(q):
        return pltpu.make_async_remote_copy(
            x_ref, out_ref.at[slot(cpos, ppos)], send_sem.at[n_col + q], recv_sem.at[cpos, ppos],
            device_id={"tensor": plane[1](index, q)}, device_id_type=mesh_ids,
        )

    def relay_copy(zc, q):
        return pltpu.make_async_remote_copy(
            out_ref.at[slot(zc, ppos)], out_ref.at[slot(zc, ppos)], relay_sem.at[zc, q], recv_sem.at[zc, ppos],
            device_id={"tensor": plane[1](index, q)}, device_id_type=mesh_ids,
        )

    def arrival(zc, p):
        return pltpu.make_async_remote_copy(
            x_ref, out_ref.at[slot(zc, p)], send_sem.at[0], recv_sem.at[zc, p],
            device_id={"tensor": index}, device_id_type=mesh_ids,
        )

    local = pltpu.make_async_copy(x_ref, out_ref.at[slot(cpos, ppos)], local_sem)
    local.start()

    def send_col(k, carry):
        col_copy((cpos + k) % n_col).start()
        return carry

    def send_plane(k, carry):
        plane_copy((ppos + k) % n_plane).start()
        return carry

    lax.fori_loop(1, n_col, send_col, 0)
    lax.fori_loop(1, n_plane, send_plane, 0)

    def relay(k, carry):
        zc = (cpos + k) % n_col
        arrival(zc, ppos).wait_recv()

        def forward(m, inner):
            relay_copy(zc, (ppos + m) % n_plane).start()
            return inner

        return lax.fori_loop(1, n_plane, forward, carry)

    lax.fori_loop(1, n_col, relay, 0)

    def finish_col(k, carry):
        col_copy((cpos + k) % n_col).wait_send()
        return carry

    def finish_plane(m, carry):
        q = (ppos + m) % n_plane
        plane_copy(q).wait_send()
        arrival(cpos, q).wait_recv()
        return carry

    def finish_relay(k, carry):
        zc = (cpos + k) % n_col

        def inner(m, c):
            q = (ppos + m) % n_plane
            relay_copy(zc, q).wait_send()
            arrival(zc, q).wait_recv()
            return c

        return lax.fori_loop(1, n_plane, inner, carry)

    lax.fori_loop(1, n_col, finish_col, 0)
    lax.fori_loop(1, n_plane, finish_plane, 0)
    lax.fori_loop(1, n_col, finish_relay, 0)
    local.wait()


def gather_tokens(x, col, plane, slot, n_col, n_plane, collective_id):
    return pl.pallas_call(
        functools.partial(_gather_kernel, n_col, n_plane, col, plane, slot),
        out_shape=jax.ShapeDtypeStruct((n_col * n_plane,) + x.shape, x.dtype),
        in_specs=[pl.BlockSpec(memory_space=pltpu.VMEM)],
        out_specs=pl.BlockSpec(memory_space=pltpu.VMEM),
        scratch_shapes=[
            pltpu.SemaphoreType.DMA,
            pltpu.SemaphoreType.DMA((n_col + n_plane,)),
            pltpu.SemaphoreType.DMA((n_col, n_plane)),
            pltpu.SemaphoreType.DMA((n_col, n_plane)),
        ],
        compiler_params=pltpu.CompilerParams(collective_id=collective_id, has_side_effects=True),
    )(x)


def _reduce_kernel(n_col, n_plane, n_dp, col, plane, pick, rows_ref, x_ref, pages_ref, out_ref,
                   pages_out, inbox, stage, inbox2, local_sem, send_sem, recv_sem, send2_sem, recv2_sem,
                   page_local_sem, page_send_sem, page_recv_sem):
    index = lax.axis_index("tensor")
    cpos, ppos = col[0](index), plane[0](index)
    mesh_ids = pl.DeviceIdType.MESH
    barrier = pltpu.get_barrier_semaphore()
    group = lax.axis_index("dp")

    def page_copy(g, slot):
        return pltpu.make_async_remote_copy(
            pages_ref.at[g], pages_out.at[slot], page_send_sem.at[g], page_recv_sem.at[slot],
            device_id={"dp": g}, device_id_type=mesh_ids,
        )

    def greet_group(k, carry):
        pl.semaphore_signal(
            barrier, inc=1, device_id={"dp": (group + k) % n_dp}, device_id_type=mesh_ids
        )
        return carry

    lax.fori_loop(1, n_dp, greet_group, 0)
    _greet(barrier, [(n_col, *col), (n_plane, *plane)], extra=n_dp - 1)
    page_local = pltpu.make_async_copy(pages_ref.at[group], pages_out.at[group], page_local_sem)
    page_local.start()

    def send_pages(k, carry):
        page_copy((group + k) % n_dp, group).start()
        return carry

    lax.fori_loop(1, n_dp, send_pages, 0)

    def plane_copy(q, z, slot):
        return pltpu.make_async_remote_copy(
            pick(rows_ref, q, z), inbox.at[z, slot], send_sem.at[z, q], recv_sem.at[z, slot],
            device_id={"tensor": plane[1](index, q)}, device_id_type=mesh_ids,
        )

    def col_copy(q, slot):
        return pltpu.make_async_remote_copy(
            stage.at[q], inbox2.at[slot], send2_sem.at[q], recv2_sem.at[slot],
            device_id={"tensor": col[1](index, q)}, device_id_type=mesh_ids,
        )

    order = [(cpos + 1 + k) % n_col for k in range(n_col)]
    locals_ = []
    for z in order:
        local = pltpu.make_async_copy(pick(rows_ref, ppos, z), inbox.at[z, ppos], local_sem.at[z])
        local.start()
        locals_.append(local)

        def send_plane(m, carry, z=z):
            plane_copy((ppos + m) % n_plane, z, ppos).start()
            return carry

        lax.fori_loop(1, n_plane, send_plane, 0)

    def plane_sum(z, local):
        def arrive(m, carry):
            plane_copy((ppos + m) % n_plane, z, (ppos + m) % n_plane).wait_recv()
            return carry

        lax.fori_loop(1, n_plane, arrive, 0)
        local.wait()
        total = inbox[z, 0].astype(jnp.float32)
        for sender in range(1, n_plane):
            total = total + inbox[z, sender].astype(jnp.float32)
        return total

    for z, local in zip(order[:-1], locals_[:-1]):
        stage[z] = plane_sum(z, local).astype(stage.dtype)
        col_copy(z, cpos).start()

    result = x_ref[...].astype(jnp.float32) + plane_sum(cpos, locals_[-1])

    def finish_plane(m, carry):
        q = (ppos + m) % n_plane
        for z in order:
            plane_copy(q, z, ppos).wait_send()
        return carry

    lax.fori_loop(1, n_plane, finish_plane, 0)

    for z in order[:-1]:
        col_copy(z, cpos).wait_send()
        col_copy(z, z).wait_recv()
        result = result + inbox2[z].astype(jnp.float32)
    out_ref[...] = result

    def finish_pages(k, carry):
        g = (group + k) % n_dp
        page_copy(g, group).wait_send()
        page_copy(g, g).wait_recv()
        return carry

    lax.fori_loop(1, n_dp, finish_pages, 0)
    page_local.wait()


def reduce_rows(rows, x, pages, col, plane, pick, n_col, n_plane, collective_id):
    block = x.shape
    n_dp = pages.shape[0]
    return pl.pallas_call(
        functools.partial(_reduce_kernel, n_col, n_plane, n_dp, col, plane, pick),
        out_shape=(
            jax.ShapeDtypeStruct(block, jnp.float32),
            jax.ShapeDtypeStruct(pages.shape, pages.dtype),
        ),
        in_specs=[pl.BlockSpec(memory_space=pltpu.VMEM)] * 3,
        out_specs=(pl.BlockSpec(memory_space=pltpu.VMEM), pl.BlockSpec(memory_space=pltpu.VMEM)),
        scratch_shapes=[
            pltpu.VMEM((n_col, n_plane) + block, rows.dtype),
            pltpu.VMEM((n_col,) + block, rows.dtype),
            pltpu.VMEM((n_col,) + block, rows.dtype),
            pltpu.SemaphoreType.DMA((n_col,)),
            pltpu.SemaphoreType.DMA((n_col, n_plane)),
            pltpu.SemaphoreType.DMA((n_col, n_plane)),
            pltpu.SemaphoreType.DMA((n_col,)),
            pltpu.SemaphoreType.DMA((n_col,)),
            pltpu.SemaphoreType.DMA,
            pltpu.SemaphoreType.DMA((n_dp,)),
            pltpu.SemaphoreType.DMA((n_dp,)),
        ],
        compiler_params=pltpu.CompilerParams(collective_id=collective_id, has_side_effects=True),
    )(rows, x, pages)


def shards(
    hidden_states,
    attention_gain,
    feedforward_gain,
    heads_weight,
    output_weight,
    upward_weight,
    downward_weight,
    segments,
    page_targets,
):
    tensor_count = lax.axis_size("tensor")
    replica_count = lax.axis_size("dp")
    tensor_index = lax.axis_index("tensor")
    quarters = tensor_count // H
    quarter_width = HD // quarters
    quarter_index = tensor_index % quarters
    stream = segments[0]
    tokens_total = stream.shape[0]
    local_rows = hidden_states.shape[0]

    width = hidden_states.shape[1]
    planes = tensor_count // 8
    gathered = gather_tokens(
        hidden_states,
        (column_group, column_member),
        (plane_group, plane_member),
        token_block,
        planes,
        8,
        0,
    )
    tokens = gathered.reshape(tokens_total, width)
    normed_attention = layer_norm(tokens, attention_gain)
    normed_feedforward = layer_norm(tokens, feedforward_gain)
    joined = jnp.dot(normed_attention, heads_weight, preferred_element_type=jnp.float32).astype(
        jnp.bfloat16
    )

    indices, starting = positions_of(stream)
    offsets = indices - starting
    query_piece = joined[:, :quarter_width]
    key_piece = joined[:, quarter_width : 2 * quarter_width]
    value_piece = joined[:, 2 * quarter_width :]
    leading = quarter_index == 0
    query_piece = jnp.where(leading, rotate_leading(query_piece, offsets, ROT), query_piece)
    key_piece = jnp.where(leading, rotate_leading(key_piece, offsets, ROT), key_piece)

    page_count = tokens_total // PAGE
    page_rows = jnp.concatenate([key_piece, value_piece], 1).reshape(
        page_count, PAGE * 2 * quarter_width
    )
    targets = page_targets[:, 0]
    page_numbers = jnp.arange(page_count, dtype=jnp.int32)
    earlier = jnp.sum(
        (
            (targets[None, :] == targets[:, None]) & (page_numbers[None, :] < page_numbers[:, None])
        ).astype(jnp.int32),
        axis=1,
    )
    capacity = 2 * page_count // replica_count
    slot_numbers = targets * capacity + earlier
    placing = (
        jnp.arange(replica_count * capacity, dtype=jnp.int32)[:, None] == slot_numbers[None, :]
    ).astype(jnp.bfloat16)
    outgoing = jnp.dot(placing, page_rows, preferred_element_type=jnp.float32).astype(jnp.bfloat16)
    outgoing = outgoing.reshape(replica_count, capacity * PAGE, 2 * quarter_width)
    head_pieces, feedforward = exchange_all(
        1,
        (jnp.concatenate([query_piece, key_piece], 1)[None], "tensor", quarters, True, None),
        work=(_feedforward_up, _feedforward_down),
        inputs=(normed_feedforward, upward_weight, downward_weight),
        results=(jax.ShapeDtypeStruct((tokens_total, width), jnp.float32),),
    )
    queries = head_pieces[:, :, :quarter_width].transpose(1, 0, 2).reshape(tokens_total, HD)
    keys = head_pieces[:, :, quarter_width:].transpose(1, 0, 2).reshape(tokens_total, HD)

    scores = jnp.dot(queries, keys.T, preferred_element_type=jnp.float32) * HD ** (-0.5)
    allowed = (stream[None, :] == stream[:, None]) & (indices[None, :] <= indices[:, None])
    peak = jnp.max(jnp.where(allowed, scores, -jnp.inf), axis=1, keepdims=True)
    weights = jnp.where(allowed, jnp.exp(scores - peak), 0.0)
    weight_sum = jnp.sum(weights, axis=1, keepdims=True)
    mixed = jnp.dot(weights.astype(jnp.bfloat16), value_piece, preferred_element_type=jnp.float32)
    attended = (mixed / weight_sum).astype(jnp.bfloat16)

    partial = (
        jnp.dot(attended, output_weight, preferred_element_type=jnp.float32) + feedforward
    ).astype(jnp.bfloat16)
    layer_output, incoming = reduce_rows(
        partial.reshape(4, planes, 2, local_rows, width),
        hidden_states,
        outgoing,
        (column_group, column_member),
        (plane_group, plane_member),
        plane_rows,
        planes,
        8,
        2,
    )

    cache_pages = incoming.reshape(1, replica_count, capacity, PAGE, 2 * quarter_width)
    return (layer_output, cache_pages)


def solution(mesh):
    in_specs = (
        P(("dp", "tensor"), None),
        P(),
        P(),
        P(None, "tensor"),
        P("tensor", None),
        P(None, "tensor"),
        P("tensor", None),
        P("dp", None),
        P("dp", None),
    )
    out_specs = (P(("dp", "tensor"), None), P("dp", None, None, None, "tensor"))
    return jax.shard_map(shards, mesh=mesh, in_specs=in_specs, out_specs=out_specs, check_vma=False)
```

```python
import functools
import math

import jax
import jax.numpy as jnp
from jax import lax
from jax.experimental import pallas as pl
from jax.experimental.pallas import tpu as pltpu
from jax.sharding import PartitionSpec as P

H = 8
HD = 256
ROT = 64
PAGE = 16


epsilon = 1e-05
rotary_base = 10000.0


def layer_norm(values, gain):
    floats = values.astype(jnp.float32)
    center = jnp.mean(floats, axis=-1, keepdims=True)
    shifted = floats - center
    spread = jnp.mean(shifted * shifted, axis=-1, keepdims=True)
    return (shifted * lax.rsqrt(spread + epsilon) * gain).astype(jnp.bfloat16)


def positions_of(stream):
    indices = jnp.arange(stream.shape[0], dtype=jnp.int32)
    boundary = jnp.concatenate([jnp.ones((1,), dtype=bool), stream[1:] != stream[:-1]])
    starting = lax.cummax(jnp.where(boundary, indices, jnp.zeros_like(indices)), axis=0)
    return (indices, starting)


def rotate_leading(vectors, offsets, rotary_dims):
    half_dims = rotary_dims // 2
    frequency = jnp.exp(
        jnp.arange(half_dims, dtype=jnp.float32) * (-2.0 * math.log(rotary_base) / rotary_dims)
    )
    angles = offsets.astype(jnp.float32)[:, None] * frequency[None, :]
    cosine = jnp.cos(angles)
    sine = jnp.sin(angles)
    floats = vectors.astype(jnp.float32)
    leading = floats[..., :half_dims]
    trailing = floats[..., half_dims:rotary_dims]
    rotated = jnp.concatenate(
        [
            leading * cosine - trailing * sine,
            trailing * cosine + leading * sine,
            floats[..., rotary_dims:],
        ],
        axis=-1,
    )
    return rotated.astype(jnp.bfloat16)


def _exchange_kernel(plans, work, extra_in, extra_out, *refs):
    count = len(plans)
    sources, refs = refs[:count], refs[count:]
    inputs, refs = refs[:extra_in], refs[extra_in:]
    outs, refs = refs[:count], refs[count:]
    results, semaphores = refs[:extra_out], refs[extra_out:]
    mesh_ids = pl.DeviceIdType.MESH
    barrier = pltpu.get_barrier_semaphore()
    steps = []
    for number, (axis, n, shared, position, member) in enumerate(plans):
        src_ref, out_ref = sources[number], outs[number]
        local_sem, send_sem, recv_sem = semaphores[3 * number : 3 * number + 3]
        index = lax.axis_index(axis)
        pos = position(index)

        def peer_copy(q, slot, src_ref=src_ref, out_ref=out_ref, send_sem=send_sem,
                      recv_sem=recv_sem, axis=axis, member=member, index=index, shared=shared):
            return pltpu.make_async_remote_copy(
                src_ref=src_ref.at[0] if shared else src_ref.at[q],
                dst_ref=out_ref.at[slot],
                send_sem=send_sem.at[q],
                recv_sem=recv_sem.at[slot],
                device_id={axis: member(index, q)},
                device_id_type=mesh_ids,
            )

        def greet(k, carry, n=n, pos=pos, axis=axis, member=member, index=index):
            q = (pos + k) % n
            pl.semaphore_signal(
                barrier, inc=1, device_id={axis: member(index, q)}, device_id_type=mesh_ids
            )
            return carry

        lax.fori_loop(1, n, greet, 0)
        local = pltpu.make_async_copy(
            src_ref.at[0] if shared else src_ref.at[pos], out_ref.at[pos], local_sem
        )
        steps.append((n, pos, peer_copy, local))
    carried = work[0](*inputs) if work is not None else None
    pl.semaphore_wait(barrier, sum(plan[1] - 1 for plan in plans))

    for n, pos, peer_copy, local in steps:
        local.start()

        def send(k, carry, n=n, pos=pos, peer_copy=peer_copy):
            peer_copy((pos + k) % n, pos).start()
            return carry

        lax.fori_loop(1, n, send, 0)

    if work is not None:
        work[1](carried, *inputs, *results)

    for n, pos, peer_copy, local in steps:

        def finish(k, carry, n=n, pos=pos, peer_copy=peer_copy):
            q = (pos + k) % n
            peer_copy(q, pos).wait_send()
            peer_copy(q, q).wait_recv()
            return carry

        lax.fori_loop(1, n, finish, 0)
        local.wait()


def contiguous(n):
    return (lambda index: index % n, lambda index, q: index - index % n + q)


def plane_group(index):
    return (index // 8) * 2 + index % 2


def plane_member(index, q):
    return ((q // 2) * 4 + (index // 2) % 4) * 2 + q % 2


def token_block(zc, p):
    return ((p // 2) * 4 + zc) * 2 + p % 2


def plane_rows(rows_ref, q, z):
    return rows_ref.at[q // 2, z, q % 2]


def column_group(index):
    return (index // 2) % 4


def column_member(index, q):
    return ((index // 8) * 4 + q) * 2 + index % 2


def exchange_all(collective_id, *requests, work=None, inputs=(), results=()):
    plans, blocks, shapes, scratch = [], [], [], []
    for data, axis, n, shared, group in requests:
        position, member = group if group is not None else contiguous(n)
        plans.append((axis, n, shared, position, member))
        blocks.append(data)
        shapes.append(jax.ShapeDtypeStruct((n,) + data.shape[1:], data.dtype))
        scratch += [
            pltpu.SemaphoreType.DMA,
            pltpu.SemaphoreType.DMA((n,)),
            pltpu.SemaphoreType.DMA((n,)),
        ]
    operands = blocks + list(inputs)
    out_shapes = shapes + list(results)
    return pl.pallas_call(
        functools.partial(_exchange_kernel, tuple(plans), work, len(inputs), len(results)),
        out_shape=tuple(out_shapes),
        in_specs=[pl.BlockSpec(memory_space=pltpu.VMEM)] * len(operands),
        out_specs=tuple(pl.BlockSpec(memory_space=pltpu.VMEM) for _ in out_shapes),
        scratch_shapes=scratch,
        compiler_params=pltpu.CompilerParams(collective_id=collective_id, has_side_effects=True),
    )(*operands)


def exchange(blocks, axis, n, shared, collective_id, group=None):
    return exchange_all(collective_id, (blocks, axis, n, shared, group))[0]


def _feedforward_up(normed_ref, upward_ref, downward_ref):
    upward = jnp.dot(normed_ref[...], upward_ref[...], preferred_element_type=jnp.float32)
    return (0.5 * upward * (1.0 + lax.erf(upward * math.sqrt(0.5)))).astype(jnp.bfloat16)


def _feedforward_down(hidden, normed_ref, upward_ref, downward_ref, out_ref):
    out_ref[...] = jnp.dot(hidden, downward_ref[...], preferred_element_type=jnp.float32)


def _head_kernel(n, tokens_ref, gain_a_ref, gain_f_ref, wq_ref, wk_ref, wv_ref, cos_ref, sin_ref,
                 turn_ref, up_ref, down_ref, pieces_ref, key_ref, value_ref, ff_ref, held_ref, normed_ref,
                 local_sem, send_sem, recv_sem):
    index = lax.axis_index("tensor")
    pos = index % n
    base = index - pos
    mesh_ids = pl.DeviceIdType.MESH
    barrier = pltpu.get_barrier_semaphore()

    def greet(k, carry):
        pl.semaphore_signal(
            barrier, inc=1, device_id={"tensor": base + (pos + k) % n}, device_id_type=mesh_ids
        )
        return carry

    lax.fori_loop(1, n, greet, 0)

    floats = tokens_ref[...].astype(jnp.float32)
    center = jnp.mean(floats, axis=-1, keepdims=True)
    shifted = floats - center
    spread = jnp.mean(shifted * shifted, axis=-1, keepdims=True)
    scale = lax.rsqrt(spread + epsilon)
    normed = (shifted * scale * gain_a_ref[...]).astype(jnp.bfloat16)
    normed_ref[...] = (shifted * scale * gain_f_ref[...]).astype(jnp.bfloat16)

    def project(w_ref):
        return jnp.dot(normed, w_ref[...], preferred_element_type=jnp.float32).astype(jnp.bfloat16)

    def rotate(piece):
        turned = jnp.dot(piece, turn_ref[...], preferred_element_type=jnp.float32)
        rotated = piece.astype(jnp.float32) * cos_ref[...] + turned * sin_ref[...]
        return jnp.where(pos == 0, rotated.astype(jnp.bfloat16), piece)

    held_ref[0] = rotate(project(wq_ref))
    key = rotate(project(wk_ref))
    held_ref[1] = key
    key_ref[...] = key
    value_ref[...] = project(wv_ref)
    pl.semaphore_wait(barrier, n - 1)

    def peer_copy(q, slot):
        return pltpu.make_async_remote_copy(
            held_ref, pieces_ref.at[slot], send_sem.at[q], recv_sem.at[slot],
            device_id={"tensor": base + q}, device_id_type=mesh_ids,
        )

    local = pltpu.make_async_copy(held_ref, pieces_ref.at[pos], local_sem)
    local.start()

    def send(k, carry):
        peer_copy((pos + k) % n, pos).start()
        return carry

    lax.fori_loop(1, n, send, 0)

    upward = jnp.dot(normed_ref[...], up_ref[...], preferred_element_type=jnp.float32)
    hidden = (0.5 * upward * (1.0 + lax.erf(upward * math.sqrt(0.5)))).astype(jnp.bfloat16)
    ff_ref[...] = jnp.dot(hidden, down_ref[...], preferred_element_type=jnp.float32)

    def finish(k, carry):
        q = (pos + k) % n
        peer_copy(q, pos).wait_send()
        peer_copy(q, q).wait_recv()
        return carry

    lax.fori_loop(1, n, finish, 0)
    local.wait()


def head_stage(n, tokens, gains, weights, cosine, sine, turn, upward_weight, downward_weight):
    rows = tokens.shape[0]
    width = weights[0].shape[1]
    operands = (tokens, *gains, *weights, cosine, sine, turn, upward_weight, downward_weight)
    return pl.pallas_call(
        functools.partial(_head_kernel, n),
        out_shape=(
            jax.ShapeDtypeStruct((n, 2, rows, width), jnp.bfloat16),
            jax.ShapeDtypeStruct((rows, width), jnp.bfloat16),
            jax.ShapeDtypeStruct((rows, width), jnp.bfloat16),
            jax.ShapeDtypeStruct((rows, downward_weight.shape[1]), jnp.float32),
        ),
        in_specs=[pl.BlockSpec(memory_space=pltpu.VMEM)] * len(operands),
        out_specs=tuple(pl.BlockSpec(memory_space=pltpu.VMEM) for _ in range(4)),
        scratch_shapes=[
            pltpu.VMEM((2, rows, width), jnp.bfloat16),
            pltpu.VMEM(tokens.shape, jnp.bfloat16),
            pltpu.SemaphoreType.DMA,
            pltpu.SemaphoreType.DMA((n,)),
            pltpu.SemaphoreType.DMA((n,)),
        ],
        compiler_params=pltpu.CompilerParams(collective_id=1, has_side_effects=True),
    )(*operands)


def _greet(barrier, groups, extra=0):
    index = lax.axis_index("tensor")
    total = 0
    for n, position, member in groups:
        pos = position(index)

        def greet(k, carry, n=n, pos=pos, member=member):
            pl.semaphore_signal(
                barrier,
                inc=1,
                device_id={"tensor": member(index, (pos + k) % n)},
                device_id_type=pl.DeviceIdType.MESH,
            )
            return carry

        lax.fori_loop(1, n, greet, 0)
        total += n - 1
    pl.semaphore_wait(barrier, total + extra)


def _gather_kernel(n_col, n_plane, col, plane, slot, x_ref, out_ref, local_sem, send_sem, relay_sem, recv_sem):
    index = lax.axis_index("tensor")
    cpos, ppos = col[0](index), plane[0](index)
    mesh_ids = pl.DeviceIdType.MESH
    _greet(pltpu.get_barrier_semaphore(), [(n_col, *col), (n_plane, *plane)])

    def col_copy(q):
        return pltpu.make_async_remote_copy(
            x_ref, out_ref.at[slot(cpos, ppos)], send_sem.at[q], recv_sem.at[cpos, ppos],
            device_id={"tensor": col[1](index, q)}, device_id_type=mesh_ids,
        )

    def plane_copy(q):
        return pltpu.make_async_remote_copy(
            x_ref, out_ref.at[slot(cpos, ppos)], send_sem.at[n_col + q], recv_sem.at[cpos, ppos],
            device_id={"tensor": plane[1](index, q)}, device_id_type=mesh_ids,
        )

    def relay_copy(zc, q):
        return pltpu.make_async_remote_copy(
            out_ref.at[slot(zc, ppos)], out_ref.at[slot(zc, ppos)], relay_sem.at[zc, q], recv_sem.at[zc, ppos],
            device_id={"tensor": plane[1](index, q)}, device_id_type=mesh_ids,
        )

    def arrival(zc, p):
        return pltpu.make_async_remote_copy(
            x_ref, out_ref.at[slot(zc, p)], send_sem.at[0], recv_sem.at[zc, p],
            device_id={"tensor": index}, device_id_type=mesh_ids,
        )

    local = pltpu.make_async_copy(x_ref, out_ref.at[slot(cpos, ppos)], local_sem)
    local.start()

    def send_col(k, carry):
        col_copy((cpos + k) % n_col).start()
        return carry

    def send_plane(k, carry):
        plane_copy((ppos + k) % n_plane).start()
        return carry

    lax.fori_loop(1, n_col, send_col, 0)
    lax.fori_loop(1, n_plane, send_plane, 0)

    def relay(k, carry):
        zc = (cpos + k) % n_col
        arrival(zc, ppos).wait_recv()

        def forward(m, inner):
            relay_copy(zc, (ppos + m) % n_plane).start()
            return inner

        return lax.fori_loop(1, n_plane, forward, carry)

    lax.fori_loop(1, n_col, relay, 0)

    def finish_col(k, carry):
        col_copy((cpos + k) % n_col).wait_send()
        return carry

    def finish_plane(m, carry):
        q = (ppos + m) % n_plane
        plane_copy(q).wait_send()
        arrival(cpos, q).wait_recv()
        return carry

    def finish_relay(k, carry):
        zc = (cpos + k) % n_col

        def inner(m, c):
            q = (ppos + m) % n_plane
            relay_copy(zc, q).wait_send()
            arrival(zc, q).wait_recv()
            return c

        return lax.fori_loop(1, n_plane, inner, carry)

    lax.fori_loop(1, n_col, finish_col, 0)
    lax.fori_loop(1, n_plane, finish_plane, 0)
    lax.fori_loop(1, n_col, finish_relay, 0)
    local.wait()


def gather_tokens(x, col, plane, slot, n_col, n_plane, collective_id):
    return pl.pallas_call(
        functools.partial(_gather_kernel, n_col, n_plane, col, plane, slot),
        out_shape=jax.ShapeDtypeStruct((n_col * n_plane,) + x.shape, x.dtype),
        in_specs=[pl.BlockSpec(memory_space=pltpu.VMEM)],
        out_specs=pl.BlockSpec(memory_space=pltpu.VMEM),
        scratch_shapes=[
            pltpu.SemaphoreType.DMA,
            pltpu.SemaphoreType.DMA((n_col + n_plane,)),
            pltpu.SemaphoreType.DMA((n_col, n_plane)),
            pltpu.SemaphoreType.DMA((n_col, n_plane)),
        ],
        compiler_params=pltpu.CompilerParams(collective_id=collective_id, has_side_effects=True),
    )(x)


def _reduce_kernel(n_col, n_plane, n_dp, col, plane, pick, rows_ref, x_ref, pages_ref, out_ref,
                   pages_out, inbox, stage, inbox2, local_sem, send_sem, recv_sem, send2_sem, recv2_sem,
                   page_local_sem, page_send_sem, page_recv_sem):
    index = lax.axis_index("tensor")
    cpos, ppos = col[0](index), plane[0](index)
    mesh_ids = pl.DeviceIdType.MESH
    barrier = pltpu.get_barrier_semaphore()
    group = lax.axis_index("dp")

    def page_copy(g, slot):
        return pltpu.make_async_remote_copy(
            pages_ref.at[g], pages_out.at[slot], page_send_sem.at[g], page_recv_sem.at[slot],
            device_id={"dp": g}, device_id_type=mesh_ids,
        )

    def greet_group(k, carry):
        pl.semaphore_signal(
            barrier, inc=1, device_id={"dp": (group + k) % n_dp}, device_id_type=mesh_ids
        )
        return carry

    lax.fori_loop(1, n_dp, greet_group, 0)
    _greet(barrier, [(n_col, *col), (n_plane, *plane)], extra=n_dp - 1)
    page_local = pltpu.make_async_copy(pages_ref.at[group], pages_out.at[group], page_local_sem)
    page_local.start()

    def send_pages(k, carry):
        page_copy((group + k) % n_dp, group).start()
        return carry

    lax.fori_loop(1, n_dp, send_pages, 0)

    def plane_copy(q, z, slot):
        return pltpu.make_async_remote_copy(
            pick(rows_ref, q, z), inbox.at[z, slot], send_sem.at[z, q], recv_sem.at[z, slot],
            device_id={"tensor": plane[1](index, q)}, device_id_type=mesh_ids,
        )

    def col_copy(q, slot):
        return pltpu.make_async_remote_copy(
            stage.at[q], inbox2.at[slot], send2_sem.at[q], recv2_sem.at[slot],
            device_id={"tensor": col[1](index, q)}, device_id_type=mesh_ids,
        )

    order = [(cpos + 1 + k) % n_col for k in range(n_col)]
    locals_ = []
    for z in order:
        local = pltpu.make_async_copy(pick(rows_ref, ppos, z), inbox.at[z, ppos], local_sem.at[z])
        local.start()
        locals_.append(local)

        def send_plane(m, carry, z=z):
            plane_copy((ppos + m) % n_plane, z, ppos).start()
            return carry

        lax.fori_loop(1, n_plane, send_plane, 0)

    def plane_sum(z, local):
        def arrive(m, carry):
            plane_copy((ppos + m) % n_plane, z, (ppos + m) % n_plane).wait_recv()
            return carry

        lax.fori_loop(1, n_plane, arrive, 0)
        local.wait()
        total = inbox[z, 0].astype(jnp.float32)
        for sender in range(1, n_plane):
            total = total + inbox[z, sender].astype(jnp.float32)
        return total

    for z, local in zip(order[:-1], locals_[:-1]):
        stage[z] = plane_sum(z, local).astype(stage.dtype)
        col_copy(z, cpos).start()

    result = x_ref[...].astype(jnp.float32) + plane_sum(cpos, locals_[-1])

    def finish_plane(m, carry):
        q = (ppos + m) % n_plane
        for z in order:
            plane_copy(q, z, ppos).wait_send()
        return carry

    lax.fori_loop(1, n_plane, finish_plane, 0)

    for z in order[:-1]:
        col_copy(z, cpos).wait_send()
        col_copy(z, z).wait_recv()
        result = result + inbox2[z].astype(jnp.float32)
    out_ref[...] = result

    def finish_pages(k, carry):
        g = (group + k) % n_dp
        page_copy(g, group).wait_send()
        page_copy(g, g).wait_recv()
        return carry

    lax.fori_loop(1, n_dp, finish_pages, 0)
    page_local.wait()


def reduce_rows(rows, x, pages, col, plane, pick, n_col, n_plane, collective_id):
    block = x.shape
    n_dp = pages.shape[0]
    return pl.pallas_call(
        functools.partial(_reduce_kernel, n_col, n_plane, n_dp, col, plane, pick),
        out_shape=(
            jax.ShapeDtypeStruct(block, jnp.float32),
            jax.ShapeDtypeStruct(pages.shape, pages.dtype),
        ),
        in_specs=[pl.BlockSpec(memory_space=pltpu.VMEM)] * 3,
        out_specs=(pl.BlockSpec(memory_space=pltpu.VMEM), pl.BlockSpec(memory_space=pltpu.VMEM)),
        scratch_shapes=[
            pltpu.VMEM((n_col, n_plane) + block, rows.dtype),
            pltpu.VMEM((n_col,) + block, rows.dtype),
            pltpu.VMEM((n_col,) + block, rows.dtype),
            pltpu.SemaphoreType.DMA((n_col,)),
            pltpu.SemaphoreType.DMA((n_col, n_plane)),
            pltpu.SemaphoreType.DMA((n_col, n_plane)),
            pltpu.SemaphoreType.DMA((n_col,)),
            pltpu.SemaphoreType.DMA((n_col,)),
            pltpu.SemaphoreType.DMA,
            pltpu.SemaphoreType.DMA((n_dp,)),
            pltpu.SemaphoreType.DMA((n_dp,)),
        ],
        compiler_params=pltpu.CompilerParams(collective_id=collective_id, has_side_effects=True),
    )(rows, x, pages)


def shards(
    hidden_states,
    attention_gain,
    feedforward_gain,
    heads_weight,
    output_weight,
    upward_weight,
    downward_weight,
    segments,
    page_targets,
):
    tensor_count = lax.axis_size("tensor")
    replica_count = lax.axis_size("dp")
    tensor_index = lax.axis_index("tensor")
    quarters = tensor_count // H
    quarter_width = HD // quarters
    quarter_index = tensor_index % quarters
    stream = segments[0]
    tokens_total = stream.shape[0]
    local_rows = hidden_states.shape[0]

    width = hidden_states.shape[1]
    planes = tensor_count // 8
    gathered = gather_tokens(
        hidden_states,
        (column_group, column_member),
        (plane_group, plane_member),
        token_block,
        planes,
        8,
        0,
    )
    tokens = gathered.reshape(tokens_total, width)
    indices, starting = positions_of(stream)
    offsets = indices - starting
    half = ROT // 2
    frequency = jnp.exp(
        jnp.arange(half, dtype=jnp.float32) * (-2.0 * math.log(rotary_base) / ROT)
    )
    angles = offsets.astype(jnp.float32)[:, None] * frequency[None, :]
    cosine = jnp.tile(jnp.cos(angles), (1, 2))
    sine = jnp.tile(jnp.sin(angles), (1, 2))
    lanes = jnp.arange(quarter_width)
    turn = (
        jnp.where(lanes[:, None] == lanes[None, :] + half, -1.0, 0.0)
        + jnp.where(lanes[:, None] + half == lanes[None, :], 1.0, 0.0)
    ).astype(jnp.bfloat16)
    pieces, key_piece, value_piece, feedforward = head_stage(
        quarters,
        tokens,
        (attention_gain[None], feedforward_gain[None]),
        (
            heads_weight[:, :quarter_width],
            heads_weight[:, quarter_width : 2 * quarter_width],
            heads_weight[:, 2 * quarter_width :],
        ),
        cosine,
        sine,
        turn,
        upward_weight,
        downward_weight,
    )
    queries = pieces[:, 0].transpose(1, 0, 2).reshape(tokens_total, HD)
    keys = pieces[:, 1].transpose(1, 0, 2).reshape(tokens_total, HD)

    page_count = tokens_total // PAGE
    page_rows = jnp.concatenate([key_piece, value_piece], 1).reshape(
        page_count, PAGE * 2 * quarter_width
    )
    targets = page_targets[:, 0]
    page_numbers = jnp.arange(page_count, dtype=jnp.int32)
    earlier = jnp.sum(
        (
            (targets[None, :] == targets[:, None]) & (page_numbers[None, :] < page_numbers[:, None])
        ).astype(jnp.int32),
        axis=1,
    )
    capacity = 2 * page_count // replica_count
    slot_numbers = targets * capacity + earlier
    placing = (
        jnp.arange(replica_count * capacity, dtype=jnp.int32)[:, None] == slot_numbers[None, :]
    ).astype(jnp.bfloat16)
    outgoing = jnp.dot(placing, page_rows, preferred_element_type=jnp.float32).astype(jnp.bfloat16)
    outgoing = outgoing.reshape(replica_count, capacity * PAGE, 2 * quarter_width)
    scores = jnp.dot(queries, keys.T, preferred_element_type=jnp.float32) * HD ** (-0.5)
    allowed = (stream[None, :] == stream[:, None]) & (indices[None, :] <= indices[:, None])
    peak = jnp.max(jnp.where(allowed, scores, -jnp.inf), axis=1, keepdims=True)
    weights = jnp.where(allowed, jnp.exp(scores - peak), 0.0)
    weight_sum = jnp.sum(weights, axis=1, keepdims=True)
    mixed = jnp.dot(weights.astype(jnp.bfloat16), value_piece, preferred_element_type=jnp.float32)
    attended = (mixed / weight_sum).astype(jnp.bfloat16)

    partial = (
        jnp.dot(attended, output_weight, preferred_element_type=jnp.float32) + feedforward
    ).astype(jnp.bfloat16)
    layer_output, incoming = reduce_rows(
        partial.reshape(4, planes, 2, local_rows, width),
        hidden_states,
        outgoing,
        (column_group, column_member),
        (plane_group, plane_member),
        plane_rows,
        planes,
        8,
        2,
    )

    cache_pages = incoming.reshape(1, replica_count, capacity, PAGE, 2 * quarter_width)
    return (layer_output, cache_pages)


def solution(mesh):
    in_specs = (
        P(("dp", "tensor"), None),
        P(),
        P(),
        P(None, "tensor"),
        P("tensor", None),
        P(None, "tensor"),
        P("tensor", None),
        P("dp", None),
        P("dp", None),
    )
    out_specs = (P(("dp", "tensor"), None), P("dp", None, None, None, "tensor"))
    return jax.shard_map(shards, mesh=mesh, in_specs=in_specs, out_specs=out_specs, check_vma=False)
```

```python
import functools
import math

import jax
import jax.numpy as jnp
from jax import lax
from jax.experimental import pallas as pl
from jax.experimental.pallas import tpu as pltpu
from jax.sharding import PartitionSpec as P

H = 8
HD = 256
ROT = 64
PAGE = 16


epsilon = 1e-05
rotary_base = 10000.0


def layer_norm(values, gain):
    floats = values.astype(jnp.float32)
    center = jnp.mean(floats, axis=-1, keepdims=True)
    shifted = floats - center
    spread = jnp.mean(shifted * shifted, axis=-1, keepdims=True)
    return (shifted * lax.rsqrt(spread + epsilon) * gain).astype(jnp.bfloat16)


def positions_of(stream):
    indices = jnp.arange(stream.shape[0], dtype=jnp.int32)
    boundary = jnp.concatenate([jnp.ones((1,), dtype=bool), stream[1:] != stream[:-1]])
    starting = lax.cummax(jnp.where(boundary, indices, jnp.zeros_like(indices)), axis=0)
    return (indices, starting)


def rotate_leading(vectors, offsets, rotary_dims):
    half_dims = rotary_dims // 2
    frequency = jnp.exp(
        jnp.arange(half_dims, dtype=jnp.float32) * (-2.0 * math.log(rotary_base) / rotary_dims)
    )
    angles = offsets.astype(jnp.float32)[:, None] * frequency[None, :]
    cosine = jnp.cos(angles)
    sine = jnp.sin(angles)
    floats = vectors.astype(jnp.float32)
    leading = floats[..., :half_dims]
    trailing = floats[..., half_dims:rotary_dims]
    rotated = jnp.concatenate(
        [
            leading * cosine - trailing * sine,
            trailing * cosine + leading * sine,
            floats[..., rotary_dims:],
        ],
        axis=-1,
    )
    return rotated.astype(jnp.bfloat16)


def _exchange_kernel(plans, work, extra_in, extra_out, *refs):
    count = len(plans)
    sources, refs = refs[:count], refs[count:]
    inputs, refs = refs[:extra_in], refs[extra_in:]
    outs, refs = refs[:count], refs[count:]
    results, semaphores = refs[:extra_out], refs[extra_out:]
    mesh_ids = pl.DeviceIdType.MESH
    barrier = pltpu.get_barrier_semaphore()
    steps = []
    for number, (axis, n, shared, position, member) in enumerate(plans):
        src_ref, out_ref = sources[number], outs[number]
        local_sem, send_sem, recv_sem = semaphores[3 * number : 3 * number + 3]
        index = lax.axis_index(axis)
        pos = position(index)

        def peer_copy(q, slot, src_ref=src_ref, out_ref=out_ref, send_sem=send_sem,
                      recv_sem=recv_sem, axis=axis, member=member, index=index, shared=shared):
            return pltpu.make_async_remote_copy(
                src_ref=src_ref.at[0] if shared else src_ref.at[q],
                dst_ref=out_ref.at[slot],
                send_sem=send_sem.at[q],
                recv_sem=recv_sem.at[slot],
                device_id={axis: member(index, q)},
                device_id_type=mesh_ids,
            )

        def greet(k, carry, n=n, pos=pos, axis=axis, member=member, index=index):
            q = (pos + k) % n
            pl.semaphore_signal(
                barrier, inc=1, device_id={axis: member(index, q)}, device_id_type=mesh_ids
            )
            return carry

        lax.fori_loop(1, n, greet, 0)
        local = pltpu.make_async_copy(
            src_ref.at[0] if shared else src_ref.at[pos], out_ref.at[pos], local_sem
        )
        steps.append((n, pos, peer_copy, local))
    carried = work[0](*inputs) if work is not None else None
    pl.semaphore_wait(barrier, sum(plan[1] - 1 for plan in plans))

    for n, pos, peer_copy, local in steps:
        local.start()

        def send(k, carry, n=n, pos=pos, peer_copy=peer_copy):
            peer_copy((pos + k) % n, pos).start()
            return carry

        lax.fori_loop(1, n, send, 0)

    if work is not None:
        work[1](carried, *inputs, *results)

    for n, pos, peer_copy, local in steps:

        def finish(k, carry, n=n, pos=pos, peer_copy=peer_copy):
            q = (pos + k) % n
            peer_copy(q, pos).wait_send()
            peer_copy(q, q).wait_recv()
            return carry

        lax.fori_loop(1, n, finish, 0)
        local.wait()


def contiguous(n):
    return (lambda index: index % n, lambda index, q: index - index % n + q)


def plane_group(index):
    return (index // 8) * 2 + index % 2


def plane_member(index, q):
    return ((q // 2) * 4 + (index // 2) % 4) * 2 + q % 2


def token_block(zc, p):
    return ((p // 2) * 4 + zc) * 2 + p % 2


def plane_rows(rows_ref, q, z):
    return rows_ref.at[q // 2, z, q % 2]


def column_group(index):
    return (index // 2) % 4


def column_member(index, q):
    return ((index // 8) * 4 + q) * 2 + index % 2


def exchange_all(collective_id, *requests, work=None, inputs=(), results=()):
    plans, blocks, shapes, scratch = [], [], [], []
    for data, axis, n, shared, group in requests:
        position, member = group if group is not None else contiguous(n)
        plans.append((axis, n, shared, position, member))
        blocks.append(data)
        shapes.append(jax.ShapeDtypeStruct((n,) + data.shape[1:], data.dtype))
        scratch += [
            pltpu.SemaphoreType.DMA,
            pltpu.SemaphoreType.DMA((n,)),
            pltpu.SemaphoreType.DMA((n,)),
        ]
    operands = blocks + list(inputs)
    out_shapes = shapes + list(results)
    return pl.pallas_call(
        functools.partial(_exchange_kernel, tuple(plans), work, len(inputs), len(results)),
        out_shape=tuple(out_shapes),
        in_specs=[pl.BlockSpec(memory_space=pltpu.VMEM)] * len(operands),
        out_specs=tuple(pl.BlockSpec(memory_space=pltpu.VMEM) for _ in out_shapes),
        scratch_shapes=scratch,
        compiler_params=pltpu.CompilerParams(collective_id=collective_id, has_side_effects=True),
    )(*operands)


def exchange(blocks, axis, n, shared, collective_id, group=None):
    return exchange_all(collective_id, (blocks, axis, n, shared, group))[0]


def _feedforward_up(normed_ref, upward_ref, downward_ref):
    upward = jnp.dot(normed_ref[...], upward_ref[...], preferred_element_type=jnp.float32)
    return (0.5 * upward * (1.0 + lax.erf(upward * math.sqrt(0.5)))).astype(jnp.bfloat16)


def _feedforward_down(hidden, normed_ref, upward_ref, downward_ref, out_ref):
    out_ref[...] = jnp.dot(hidden, downward_ref[...], preferred_element_type=jnp.float32)


def _greet(barrier, groups, extra=0):
    index = lax.axis_index("tensor")
    total = 0
    for n, position, member in groups:
        pos = position(index)

        def greet(k, carry, n=n, pos=pos, member=member):
            pl.semaphore_signal(
                barrier,
                inc=1,
                device_id={"tensor": member(index, (pos + k) % n)},
                device_id_type=pl.DeviceIdType.MESH,
            )
            return carry

        lax.fori_loop(1, n, greet, 0)
        total += n - 1
    pl.semaphore_wait(barrier, total + extra)


def _gather_kernel(n_col, n_plane, col, plane, slot, count, *refs):
    x_refs, out_refs = refs[:count], refs[count : 2 * count]
    local_sem, send_sem, relay_sem, recv_sem = refs[2 * count :]
    index = lax.axis_index("tensor")
    cpos, ppos = col[0](index), plane[0](index)
    mesh_ids = pl.DeviceIdType.MESH
    _greet(pltpu.get_barrier_semaphore(), [(n_col, *col), (n_plane, *plane)])
    buffers = list(range(count))

    def col_copy(b, q):
        return pltpu.make_async_remote_copy(
            x_refs[b], out_refs[b].at[slot(cpos, ppos)], send_sem.at[b, q], recv_sem.at[b, cpos, ppos],
            device_id={"tensor": col[1](index, q)}, device_id_type=mesh_ids,
        )

    def plane_copy(b, q):
        return pltpu.make_async_remote_copy(
            x_refs[b], out_refs[b].at[slot(cpos, ppos)], send_sem.at[b, n_col + q],
            recv_sem.at[b, cpos, ppos],
            device_id={"tensor": plane[1](index, q)}, device_id_type=mesh_ids,
        )

    def relay_copy(b, zc, q):
        return pltpu.make_async_remote_copy(
            out_refs[b].at[slot(zc, ppos)], out_refs[b].at[slot(zc, ppos)], relay_sem.at[b, zc, q],
            recv_sem.at[b, zc, ppos],
            device_id={"tensor": plane[1](index, q)}, device_id_type=mesh_ids,
        )

    def arrival(b, zc, p):
        return pltpu.make_async_remote_copy(
            x_refs[b], out_refs[b].at[slot(zc, p)], send_sem.at[b, 0], recv_sem.at[b, zc, p],
            device_id={"tensor": index}, device_id_type=mesh_ids,
        )

    locals_ = []
    for b in buffers:
        local = pltpu.make_async_copy(x_refs[b], out_refs[b].at[slot(cpos, ppos)], local_sem.at[b])
        local.start()
        locals_.append(local)

    def send_col(k, carry):
        for b in buffers:
            col_copy(b, (cpos + k) % n_col).start()
        return carry

    def send_plane(k, carry):
        for b in buffers:
            plane_copy(b, (ppos + k) % n_plane).start()
        return carry

    lax.fori_loop(1, n_col, send_col, 0)
    lax.fori_loop(1, n_plane, send_plane, 0)

    def relay(k, carry):
        zc = (cpos + k) % n_col
        for b in buffers:
            arrival(b, zc, ppos).wait_recv()

        def forward(m, inner):
            for b in buffers:
                relay_copy(b, zc, (ppos + m) % n_plane).start()
            return inner

        return lax.fori_loop(1, n_plane, forward, carry)

    lax.fori_loop(1, n_col, relay, 0)

    def finish_col(k, carry):
        for b in buffers:
            col_copy(b, (cpos + k) % n_col).wait_send()
        return carry

    def finish_plane(m, carry):
        q = (ppos + m) % n_plane
        for b in buffers:
            plane_copy(b, q).wait_send()
            arrival(b, cpos, q).wait_recv()
        return carry

    def finish_relay(k, carry):
        zc = (cpos + k) % n_col

        def inner(m, c):
            q = (ppos + m) % n_plane
            for b in buffers:
                relay_copy(b, zc, q).wait_send()
                arrival(b, zc, q).wait_recv()
            return c

        return lax.fori_loop(1, n_plane, inner, carry)

    lax.fori_loop(1, n_col, finish_col, 0)
    lax.fori_loop(1, n_plane, finish_plane, 0)
    lax.fori_loop(1, n_col, finish_relay, 0)
    for local in locals_:
        local.wait()


def gather_tokens(blocks, col, plane, slot, n_col, n_plane, collective_id):
    count = len(blocks)
    return pl.pallas_call(
        functools.partial(_gather_kernel, n_col, n_plane, col, plane, slot, count),
        out_shape=tuple(
            jax.ShapeDtypeStruct((n_col * n_plane,) + x.shape, x.dtype) for x in blocks
        ),
        in_specs=[pl.BlockSpec(memory_space=pltpu.VMEM)] * count,
        out_specs=tuple(pl.BlockSpec(memory_space=pltpu.VMEM) for _ in blocks),
        scratch_shapes=[
            pltpu.SemaphoreType.DMA((count,)),
            pltpu.SemaphoreType.DMA((count, n_col + n_plane)),
            pltpu.SemaphoreType.DMA((count, n_col, n_plane)),
            pltpu.SemaphoreType.DMA((count, n_col, n_plane)),
        ],
        compiler_params=pltpu.CompilerParams(collective_id=collective_id, has_side_effects=True),
    )(*blocks)


def _reduce_kernel(n_col, n_plane, n_dp, col, plane, pick, rows_ref, x_ref, pages_ref, out_ref,
                   pages_out, inbox, stage, inbox2, local_sem, send_sem, recv_sem, send2_sem, recv2_sem,
                   page_local_sem, page_send_sem, page_recv_sem):
    index = lax.axis_index("tensor")
    cpos, ppos = col[0](index), plane[0](index)
    mesh_ids = pl.DeviceIdType.MESH
    barrier = pltpu.get_barrier_semaphore()
    group = lax.axis_index("dp")

    def page_copy(g, slot):
        return pltpu.make_async_remote_copy(
            pages_ref.at[g], pages_out.at[slot], page_send_sem.at[g], page_recv_sem.at[slot],
            device_id={"dp": g}, device_id_type=mesh_ids,
        )

    def greet_group(k, carry):
        pl.semaphore_signal(
            barrier, inc=1, device_id={"dp": (group + k) % n_dp}, device_id_type=mesh_ids
        )
        return carry

    lax.fori_loop(1, n_dp, greet_group, 0)
    _greet(barrier, [(n_col, *col), (n_plane, *plane)], extra=n_dp - 1)
    page_local = pltpu.make_async_copy(pages_ref.at[group], pages_out.at[group], page_local_sem)
    page_local.start()

    def send_pages(k, carry):
        page_copy((group + k) % n_dp, group).start()
        return carry

    lax.fori_loop(1, n_dp, send_pages, 0)

    def plane_copy(q, z, slot):
        return pltpu.make_async_remote_copy(
            pick(rows_ref, q, z), inbox.at[z, slot], send_sem.at[z, q], recv_sem.at[z, slot],
            device_id={"tensor": plane[1](index, q)}, device_id_type=mesh_ids,
        )

    def col_copy(q, slot):
        return pltpu.make_async_remote_copy(
            stage.at[q], inbox2.at[slot], send2_sem.at[q], recv2_sem.at[slot],
            device_id={"tensor": col[1](index, q)}, device_id_type=mesh_ids,
        )

    order = [(cpos + 1 + k) % n_col for k in range(n_col)]
    locals_ = []
    for z in order:
        local = pltpu.make_async_copy(pick(rows_ref, ppos, z), inbox.at[z, ppos], local_sem.at[z])
        local.start()
        locals_.append(local)

        def send_plane(m, carry, z=z):
            plane_copy((ppos + m) % n_plane, z, ppos).start()
            return carry

        lax.fori_loop(1, n_plane, send_plane, 0)

    def plane_sum(z, local):
        def arrive(m, carry):
            plane_copy((ppos + m) % n_plane, z, (ppos + m) % n_plane).wait_recv()
            return carry

        lax.fori_loop(1, n_plane, arrive, 0)
        local.wait()
        total = inbox[z, 0].astype(jnp.float32)
        for sender in range(1, n_plane):
            total = total + inbox[z, sender].astype(jnp.float32)
        return total

    for z, local in zip(order[:-1], locals_[:-1]):
        stage[z] = plane_sum(z, local).astype(stage.dtype)
        col_copy(z, cpos).start()

    result = x_ref[...].astype(jnp.float32) + plane_sum(cpos, locals_[-1])

    def finish_plane(m, carry):
        q = (ppos + m) % n_plane
        for z in order:
            plane_copy(q, z, ppos).wait_send()
        return carry

    lax.fori_loop(1, n_plane, finish_plane, 0)

    for z in order[:-1]:
        col_copy(z, cpos).wait_send()
        col_copy(z, z).wait_recv()
        result = result + inbox2[z].astype(jnp.float32)
    out_ref[...] = result

    def finish_pages(k, carry):
        g = (group + k) % n_dp
        page_copy(g, group).wait_send()
        page_copy(g, g).wait_recv()
        return carry

    lax.fori_loop(1, n_dp, finish_pages, 0)
    page_local.wait()


def reduce_rows(rows, x, pages, col, plane, pick, n_col, n_plane, collective_id):
    block = x.shape
    n_dp = pages.shape[0]
    return pl.pallas_call(
        functools.partial(_reduce_kernel, n_col, n_plane, n_dp, col, plane, pick),
        out_shape=(
            jax.ShapeDtypeStruct(block, jnp.float32),
            jax.ShapeDtypeStruct(pages.shape, pages.dtype),
        ),
        in_specs=[pl.BlockSpec(memory_space=pltpu.VMEM)] * 3,
        out_specs=(pl.BlockSpec(memory_space=pltpu.VMEM), pl.BlockSpec(memory_space=pltpu.VMEM)),
        scratch_shapes=[
            pltpu.VMEM((n_col, n_plane) + block, rows.dtype),
            pltpu.VMEM((n_col,) + block, rows.dtype),
            pltpu.VMEM((n_col,) + block, rows.dtype),
            pltpu.SemaphoreType.DMA((n_col,)),
            pltpu.SemaphoreType.DMA((n_col, n_plane)),
            pltpu.SemaphoreType.DMA((n_col, n_plane)),
            pltpu.SemaphoreType.DMA((n_col,)),
            pltpu.SemaphoreType.DMA((n_col,)),
            pltpu.SemaphoreType.DMA,
            pltpu.SemaphoreType.DMA((n_dp,)),
            pltpu.SemaphoreType.DMA((n_dp,)),
        ],
        compiler_params=pltpu.CompilerParams(collective_id=collective_id, has_side_effects=True),
    )(rows, x, pages)


def shards(
    hidden_states,
    attention_gain,
    feedforward_gain,
    heads_weight,
    output_weight,
    upward_weight,
    downward_weight,
    segments,
    page_targets,
):
    tensor_count = lax.axis_size("tensor")
    replica_count = lax.axis_size("dp")
    tensor_index = lax.axis_index("tensor")
    quarters = tensor_count // H
    quarter_width = HD // quarters
    quarter_index = tensor_index % quarters
    stream = segments[0]
    tokens_total = stream.shape[0]
    local_rows = hidden_states.shape[0]

    width = hidden_states.shape[1]
    planes = tensor_count // 8
    own = hidden_states.astype(jnp.float32)
    own_center = jnp.mean(own, axis=-1, keepdims=True)
    own_shifted = own - own_center
    own_scale = lax.rsqrt(jnp.mean(own_shifted * own_shifted, axis=-1, keepdims=True) + epsilon)
    gathered, statistics = gather_tokens(
        (hidden_states, jnp.concatenate([own_center, own_scale], 1)),
        (column_group, column_member),
        (plane_group, plane_member),
        token_block,
        planes,
        8,
        0,
    )
    tokens = gathered.reshape(tokens_total, width)
    statistics = statistics.reshape(tokens_total, 2)
    shifted = tokens.astype(jnp.float32) - statistics[:, :1]
    scaled = shifted * statistics[:, 1:]
    normed_attention = (scaled * attention_gain).astype(jnp.bfloat16)
    normed_feedforward = (scaled * feedforward_gain).astype(jnp.bfloat16)
    joined = jnp.dot(normed_attention, heads_weight, preferred_element_type=jnp.float32).astype(
        jnp.bfloat16
    )

    indices, starting = positions_of(stream)
    offsets = indices - starting
    query_piece = joined[:, :quarter_width]
    key_piece = joined[:, quarter_width : 2 * quarter_width]
    value_piece = joined[:, 2 * quarter_width :]
    leading = quarter_index == 0
    query_piece = jnp.where(leading, rotate_leading(query_piece, offsets, ROT), query_piece)
    key_piece = jnp.where(leading, rotate_leading(key_piece, offsets, ROT), key_piece)

    page_count = tokens_total // PAGE
    page_rows = jnp.concatenate([key_piece, value_piece], 1).reshape(
        page_count, PAGE * 2 * quarter_width
    )
    targets = page_targets[:, 0]
    page_numbers = jnp.arange(page_count, dtype=jnp.int32)
    earlier = jnp.sum(
        (
            (targets[None, :] == targets[:, None]) & (page_numbers[None, :] < page_numbers[:, None])
        ).astype(jnp.int32),
        axis=1,
    )
    capacity = 2 * page_count // replica_count
    slot_numbers = targets * capacity + earlier
    placing = (
        jnp.arange(replica_count * capacity, dtype=jnp.int32)[:, None] == slot_numbers[None, :]
    ).astype(jnp.bfloat16)
    outgoing = jnp.dot(placing, page_rows, preferred_element_type=jnp.float32).astype(jnp.bfloat16)
    outgoing = outgoing.reshape(replica_count, capacity * PAGE, 2 * quarter_width)
    head_pieces, feedforward = exchange_all(
        1,
        (jnp.concatenate([query_piece, key_piece], 1)[None], "tensor", quarters, True, None),
        work=(_feedforward_up, _feedforward_down),
        inputs=(normed_feedforward, upward_weight, downward_weight),
        results=(jax.ShapeDtypeStruct((tokens_total, width), jnp.float32),),
    )
    queries = head_pieces[:, :, :quarter_width].transpose(1, 0, 2).reshape(tokens_total, HD)
    keys = head_pieces[:, :, quarter_width:].transpose(1, 0, 2).reshape(tokens_total, HD)

    scores = jnp.dot(queries, keys.T, preferred_element_type=jnp.float32) * HD ** (-0.5)
    allowed = (stream[None, :] == stream[:, None]) & (indices[None, :] <= indices[:, None])
    peak = jnp.max(jnp.where(allowed, scores, -jnp.inf), axis=1, keepdims=True)
    weights = jnp.where(allowed, jnp.exp(scores - peak), 0.0)
    weight_sum = jnp.sum(weights, axis=1, keepdims=True)
    mixed = jnp.dot(weights.astype(jnp.bfloat16), value_piece, preferred_element_type=jnp.float32)
    attended = (mixed / weight_sum).astype(jnp.bfloat16)

    partial = (
        jnp.dot(attended, output_weight, preferred_element_type=jnp.float32) + feedforward
    ).astype(jnp.bfloat16)
    layer_output, incoming = reduce_rows(
        partial.reshape(4, planes, 2, local_rows, width),
        hidden_states,
        outgoing,
        (column_group, column_member),
        (plane_group, plane_member),
        plane_rows,
        planes,
        8,
        2,
    )

    cache_pages = incoming.reshape(1, replica_count, capacity, PAGE, 2 * quarter_width)
    return (layer_output, cache_pages)


def solution(mesh):
    in_specs = (
        P(("dp", "tensor"), None),
        P(),
        P(),
        P(None, "tensor"),
        P("tensor", None),
        P(None, "tensor"),
        P("tensor", None),
        P("dp", None),
        P("dp", None),
    )
    out_specs = (P(("dp", "tensor"), None), P("dp", None, None, None, "tensor"))
    return jax.shard_map(shards, mesh=mesh, in_specs=in_specs, out_specs=out_specs, check_vma=False)
```

```python
import functools
import math

import jax
import jax.numpy as jnp
from jax import lax
from jax.experimental import pallas as pl
from jax.experimental.pallas import tpu as pltpu
from jax.sharding import PartitionSpec as P

H = 8
HD = 256
ROT = 64
PAGE = 16


epsilon = 1e-05
rotary_base = 10000.0


def layer_norm(values, gain):
    floats = values.astype(jnp.float32)
    center = jnp.mean(floats, axis=-1, keepdims=True)
    shifted = floats - center
    spread = jnp.mean(shifted * shifted, axis=-1, keepdims=True)
    return (shifted * lax.rsqrt(spread + epsilon) * gain).astype(jnp.bfloat16)


def positions_of(stream):
    indices = jnp.arange(stream.shape[0], dtype=jnp.int32)
    boundary = jnp.concatenate([jnp.ones((1,), dtype=bool), stream[1:] != stream[:-1]])
    starting = lax.cummax(jnp.where(boundary, indices, jnp.zeros_like(indices)), axis=0)
    return (indices, starting)


def rotate_leading(vectors, offsets, rotary_dims):
    half_dims = rotary_dims // 2
    frequency = jnp.exp(
        jnp.arange(half_dims, dtype=jnp.float32) * (-2.0 * math.log(rotary_base) / rotary_dims)
    )
    angles = offsets.astype(jnp.float32)[:, None] * frequency[None, :]
    cosine = jnp.cos(angles)
    sine = jnp.sin(angles)
    floats = vectors.astype(jnp.float32)
    leading = floats[..., :half_dims]
    trailing = floats[..., half_dims:rotary_dims]
    rotated = jnp.concatenate(
        [
            leading * cosine - trailing * sine,
            trailing * cosine + leading * sine,
            floats[..., rotary_dims:],
        ],
        axis=-1,
    )
    return rotated.astype(jnp.bfloat16)


def _exchange_kernel(plans, work, extra_in, extra_out, *refs):
    count = len(plans)
    sources, refs = refs[:count], refs[count:]
    inputs, refs = refs[:extra_in], refs[extra_in:]
    outs, refs = refs[:count], refs[count:]
    results, semaphores = refs[:extra_out], refs[extra_out:]
    mesh_ids = pl.DeviceIdType.MESH
    barrier = pltpu.get_barrier_semaphore()
    steps = []
    for number, (axis, n, shared, position, member) in enumerate(plans):
        src_ref, out_ref = sources[number], outs[number]
        local_sem, send_sem, recv_sem = semaphores[3 * number : 3 * number + 3]
        index = lax.axis_index(axis)
        pos = position(index)

        def peer_copy(q, slot, src_ref=src_ref, out_ref=out_ref, send_sem=send_sem,
                      recv_sem=recv_sem, axis=axis, member=member, index=index, shared=shared):
            return pltpu.make_async_remote_copy(
                src_ref=src_ref.at[0] if shared else src_ref.at[q],
                dst_ref=out_ref.at[slot],
                send_sem=send_sem.at[q],
                recv_sem=recv_sem.at[slot],
                device_id={axis: member(index, q)},
                device_id_type=mesh_ids,
            )

        def greet(k, carry, n=n, pos=pos, axis=axis, member=member, index=index):
            q = (pos + k) % n
            pl.semaphore_signal(
                barrier, inc=1, device_id={axis: member(index, q)}, device_id_type=mesh_ids
            )
            return carry

        lax.fori_loop(1, n, greet, 0)
        local = pltpu.make_async_copy(
            src_ref.at[0] if shared else src_ref.at[pos], out_ref.at[pos], local_sem
        )
        steps.append((n, pos, peer_copy, local))
    carried = work[0](*inputs) if work is not None else None
    pl.semaphore_wait(barrier, sum(plan[1] - 1 for plan in plans))

    for n, pos, peer_copy, local in steps:
        local.start()

        def send(k, carry, n=n, pos=pos, peer_copy=peer_copy):
            peer_copy((pos + k) % n, pos).start()
            return carry

        lax.fori_loop(1, n, send, 0)

    if work is not None:
        work[1](carried, *inputs, *results)

    for n, pos, peer_copy, local in steps:

        def finish(k, carry, n=n, pos=pos, peer_copy=peer_copy):
            q = (pos + k) % n
            peer_copy(q, pos).wait_send()
            peer_copy(q, q).wait_recv()
            return carry

        lax.fori_loop(1, n, finish, 0)
        local.wait()


def contiguous(n):
    return (lambda index: index % n, lambda index, q: index - index % n + q)


def plane_group(index):
    return (index // 8) * 2 + index % 2


def plane_member(index, q):
    return ((q // 2) * 4 + (index // 2) % 4) * 2 + q % 2


def token_block(zc, p):
    return ((p // 2) * 4 + zc) * 2 + p % 2


def plane_rows(rows_ref, q, z):
    return rows_ref.at[q // 2, z, q % 2]


def column_group(index):
    return (index // 2) % 4


def column_member(index, q):
    return ((index // 8) * 4 + q) * 2 + index % 2


def exchange_all(collective_id, *requests, work=None, inputs=(), results=()):
    plans, blocks, shapes, scratch = [], [], [], []
    for data, axis, n, shared, group in requests:
        position, member = group if group is not None else contiguous(n)
        plans.append((axis, n, shared, position, member))
        blocks.append(data)
        shapes.append(jax.ShapeDtypeStruct((n,) + data.shape[1:], data.dtype))
        scratch += [
            pltpu.SemaphoreType.DMA,
            pltpu.SemaphoreType.DMA((n,)),
            pltpu.SemaphoreType.DMA((n,)),
        ]
    operands = blocks + list(inputs)
    out_shapes = shapes + list(results)
    return pl.pallas_call(
        functools.partial(_exchange_kernel, tuple(plans), work, len(inputs), len(results)),
        out_shape=tuple(out_shapes),
        in_specs=[pl.BlockSpec(memory_space=pltpu.VMEM)] * len(operands),
        out_specs=tuple(pl.BlockSpec(memory_space=pltpu.VMEM) for _ in out_shapes),
        scratch_shapes=scratch,
        compiler_params=pltpu.CompilerParams(collective_id=collective_id, has_side_effects=True),
    )(*operands)


def exchange(blocks, axis, n, shared, collective_id, group=None):
    return exchange_all(collective_id, (blocks, axis, n, shared, group))[0]


def _feedforward_up(normed_ref, upward_ref, downward_ref):
    upward = jnp.dot(normed_ref[...], upward_ref[...], preferred_element_type=jnp.float32)
    return (0.5 * upward * (1.0 + lax.erf(upward * math.sqrt(0.5)))).astype(jnp.bfloat16)


def _feedforward_down(hidden, normed_ref, upward_ref, downward_ref, out_ref):
    out_ref[...] = jnp.dot(hidden, downward_ref[...], preferred_element_type=jnp.float32)


def _greet(barrier, groups, extra=0):
    index = lax.axis_index("tensor")
    total = 0
    for n, position, member in groups:
        pos = position(index)

        def greet(k, carry, n=n, pos=pos, member=member):
            pl.semaphore_signal(
                barrier,
                inc=1,
                device_id={"tensor": member(index, (pos + k) % n)},
                device_id_type=pl.DeviceIdType.MESH,
            )
            return carry

        lax.fori_loop(1, n, greet, 0)
        total += n - 1
    pl.semaphore_wait(barrier, total + extra)


def _gather_kernel(n_col, n_plane, col, plane, slot, x_ref, out_ref, local_sem, send_sem, relay_sem, recv_sem):
    index = lax.axis_index("tensor")
    cpos, ppos = col[0](index), plane[0](index)
    mesh_ids = pl.DeviceIdType.MESH
    _greet(pltpu.get_barrier_semaphore(), [(n_col, *col), (n_plane, *plane)])

    def col_copy(q):
        return pltpu.make_async_remote_copy(
            x_ref, out_ref.at[slot(cpos, ppos)], send_sem.at[q], recv_sem.at[cpos, ppos],
            device_id={"tensor": col[1](index, q)}, device_id_type=mesh_ids,
        )

    def plane_copy(q):
        return pltpu.make_async_remote_copy(
            x_ref, out_ref.at[slot(cpos, ppos)], send_sem.at[n_col + q], recv_sem.at[cpos, ppos],
            device_id={"tensor": plane[1](index, q)}, device_id_type=mesh_ids,
        )

    def relay_copy(zc, q):
        return pltpu.make_async_remote_copy(
            out_ref.at[slot(zc, ppos)], out_ref.at[slot(zc, ppos)], relay_sem.at[zc, q], recv_sem.at[zc, ppos],
            device_id={"tensor": plane[1](index, q)}, device_id_type=mesh_ids,
        )

    def arrival(zc, p):
        return pltpu.make_async_remote_copy(
            x_ref, out_ref.at[slot(zc, p)], send_sem.at[0], recv_sem.at[zc, p],
            device_id={"tensor": index}, device_id_type=mesh_ids,
        )

    local = pltpu.make_async_copy(x_ref, out_ref.at[slot(cpos, ppos)], local_sem)
    local.start()

    def send_col(k, carry):
        col_copy((cpos + k) % n_col).start()
        return carry

    def send_plane(k, carry):
        plane_copy((ppos + k) % n_plane).start()
        return carry

    lax.fori_loop(1, n_col, send_col, 0)
    lax.fori_loop(1, n_plane, send_plane, 0)

    def relay(k, carry):
        zc = (cpos + k) % n_col
        arrival(zc, ppos).wait_recv()

        def forward(m, inner):
            relay_copy(zc, (ppos + m) % n_plane).start()
            return inner

        return lax.fori_loop(1, n_plane, forward, carry)

    lax.fori_loop(1, n_col, relay, 0)

    def finish_col(k, carry):
        col_copy((cpos + k) % n_col).wait_send()
        return carry

    def finish_plane(m, carry):
        q = (ppos + m) % n_plane
        plane_copy(q).wait_send()
        arrival(cpos, q).wait_recv()
        return carry

    def finish_relay(k, carry):
        zc = (cpos + k) % n_col

        def inner(m, c):
            q = (ppos + m) % n_plane
            relay_copy(zc, q).wait_send()
            arrival(zc, q).wait_recv()
            return c

        return lax.fori_loop(1, n_plane, inner, carry)

    lax.fori_loop(1, n_col, finish_col, 0)
    lax.fori_loop(1, n_plane, finish_plane, 0)
    lax.fori_loop(1, n_col, finish_relay, 0)
    local.wait()


def gather_tokens(x, col, plane, slot, n_col, n_plane, collective_id):
    return pl.pallas_call(
        functools.partial(_gather_kernel, n_col, n_plane, col, plane, slot),
        out_shape=jax.ShapeDtypeStruct((n_col * n_plane,) + x.shape, x.dtype),
        in_specs=[pl.BlockSpec(memory_space=pltpu.VMEM)],
        out_specs=pl.BlockSpec(memory_space=pltpu.VMEM),
        scratch_shapes=[
            pltpu.SemaphoreType.DMA,
            pltpu.SemaphoreType.DMA((n_col + n_plane,)),
            pltpu.SemaphoreType.DMA((n_col, n_plane)),
            pltpu.SemaphoreType.DMA((n_col, n_plane)),
        ],
        compiler_params=pltpu.CompilerParams(collective_id=collective_id, has_side_effects=True),
    )(x)


def _reduce_kernel(n_col, n_y, n_dp, col, ygroup, rows_ref, x_ref, pages_ref, out_ref, pages_out,
                   inbox0, chip, inbox1, stage, inbox2, sem0, local_sem, send_sem, recv_sem,
                   send2_sem, recv2_sem, page_local_sem, page_send_sem, page_recv_sem):
    index = lax.axis_index("tensor")
    cpos, ypos, core = col[0](index), ygroup[0](index), index % 2
    mesh_ids = pl.DeviceIdType.MESH
    barrier = pltpu.get_barrier_semaphore()
    group = lax.axis_index("dp")

    def page_copy(g, slot):
        return pltpu.make_async_remote_copy(
            pages_ref.at[g], pages_out.at[slot], page_send_sem.at[g], page_recv_sem.at[slot],
            device_id={"dp": g}, device_id_type=mesh_ids,
        )

    def greet_group(k, carry):
        pl.semaphore_signal(
            barrier, inc=1, device_id={"dp": (group + k) % n_dp}, device_id_type=mesh_ids
        )
        return carry

    lax.fori_loop(1, n_dp, greet_group, 0)
    sibling = (2, lambda t: t % 2, lambda t, q: t - t % 2 + q)
    _greet(barrier, [sibling, (n_y, *ygroup), (n_col, *col)], extra=n_dp - 1)
    page_local = pltpu.make_async_copy(pages_ref.at[group], pages_out.at[group], page_local_sem)
    page_local.start()

    def send_pages(k, carry):
        page_copy((group + k) % n_dp, group).start()
        return carry

    lax.fori_loop(1, n_dp, send_pages, 0)

    pair = pltpu.make_async_remote_copy(
        rows_ref.at[:, :, 1 - core], inbox0, sem0.at[0], sem0.at[1],
        device_id={"tensor": index - core + 1 - core}, device_id_type=mesh_ids,
    )
    pair.start()
    pair.wait_send()
    pair.wait_recv()
    for y in range(n_y):
        for z in range(n_col):
            chip[y, z] = (
                rows_ref[y, z, core].astype(jnp.float32) + inbox0[y, z].astype(jnp.float32)
            ).astype(chip.dtype)

    def plane_copy(q, z, slot):
        return pltpu.make_async_remote_copy(
            chip.at[q, z], inbox1.at[z, slot], send_sem.at[z, q], recv_sem.at[z, slot],
            device_id={"tensor": ygroup[1](index, q)}, device_id_type=mesh_ids,
        )

    def col_copy(q, slot):
        return pltpu.make_async_remote_copy(
            stage.at[q], inbox2.at[slot], send2_sem.at[q], recv2_sem.at[slot],
            device_id={"tensor": col[1](index, q)}, device_id_type=mesh_ids,
        )

    order = [(cpos + 1 + k) % n_col for k in range(n_col)]
    locals_ = []
    for z in order:
        local = pltpu.make_async_copy(chip.at[ypos, z], inbox1.at[z, ypos], local_sem.at[z])
        local.start()
        locals_.append(local)

        def send_plane(m, carry, z=z):
            plane_copy((ypos + m) % n_y, z, ypos).start()
            return carry

        lax.fori_loop(1, n_y, send_plane, 0)

    def plane_sum(z, local):
        def arrive(m, carry):
            plane_copy((ypos + m) % n_y, z, (ypos + m) % n_y).wait_recv()
            return carry

        lax.fori_loop(1, n_y, arrive, 0)
        local.wait()
        total = inbox1[z, 0].astype(jnp.float32)
        for sender in range(1, n_y):
            total = total + inbox1[z, sender].astype(jnp.float32)
        return total

    for z, local in zip(order[:-1], locals_[:-1]):
        stage[z] = plane_sum(z, local).astype(stage.dtype)
        col_copy(z, cpos).start()

    result = x_ref[...].astype(jnp.float32) + plane_sum(cpos, locals_[-1])

    def finish_plane(m, carry):
        q = (ypos + m) % n_y
        for z in order:
            plane_copy(q, z, ypos).wait_send()
        return carry

    lax.fori_loop(1, n_y, finish_plane, 0)

    for z in order[:-1]:
        col_copy(z, cpos).wait_send()
        col_copy(z, z).wait_recv()
        result = result + inbox2[z].astype(jnp.float32)
    out_ref[...] = result

    def finish_pages(k, carry):
        g = (group + k) % n_dp
        page_copy(g, group).wait_send()
        page_copy(g, g).wait_recv()
        return carry

    lax.fori_loop(1, n_dp, finish_pages, 0)
    page_local.wait()


def reduce_rows(rows, x, pages, col, ygroup, collective_id):
    n_y, n_col = rows.shape[0], rows.shape[1]
    block = x.shape
    n_dp = pages.shape[0]
    return pl.pallas_call(
        functools.partial(_reduce_kernel, n_col, n_y, n_dp, col, ygroup),
        out_shape=(
            jax.ShapeDtypeStruct(block, jnp.float32),
            jax.ShapeDtypeStruct(pages.shape, pages.dtype),
        ),
        in_specs=[pl.BlockSpec(memory_space=pltpu.VMEM)] * 3,
        out_specs=(pl.BlockSpec(memory_space=pltpu.VMEM), pl.BlockSpec(memory_space=pltpu.VMEM)),
        scratch_shapes=[
            pltpu.VMEM((n_y, n_col) + block, rows.dtype),
            pltpu.VMEM((n_y, n_col) + block, rows.dtype),
            pltpu.VMEM((n_col, n_y) + block, rows.dtype),
            pltpu.VMEM((n_col,) + block, rows.dtype),
            pltpu.VMEM((n_col,) + block, rows.dtype),
            pltpu.SemaphoreType.DMA((2,)),
            pltpu.SemaphoreType.DMA((n_col,)),
            pltpu.SemaphoreType.DMA((n_col, n_y)),
            pltpu.SemaphoreType.DMA((n_col, n_y)),
            pltpu.SemaphoreType.DMA((n_col,)),
            pltpu.SemaphoreType.DMA((n_col,)),
            pltpu.SemaphoreType.DMA,
            pltpu.SemaphoreType.DMA((n_dp,)),
            pltpu.SemaphoreType.DMA((n_dp,)),
        ],
        compiler_params=pltpu.CompilerParams(collective_id=collective_id, has_side_effects=True),
    )(rows, x, pages)


def same_core_group(index):
    return index // 8


def same_core_member(index, q):
    return q * 8 + index % 8


def shards(
    hidden_states,
    attention_gain,
    feedforward_gain,
    heads_weight,
    output_weight,
    upward_weight,
    downward_weight,
    segments,
    page_targets,
):
    tensor_count = lax.axis_size("tensor")
    replica_count = lax.axis_size("dp")
    tensor_index = lax.axis_index("tensor")
    quarters = tensor_count // H
    quarter_width = HD // quarters
    quarter_index = tensor_index % quarters
    stream = segments[0]
    tokens_total = stream.shape[0]
    local_rows = hidden_states.shape[0]

    width = hidden_states.shape[1]
    planes = tensor_count // 8
    gathered = gather_tokens(
        hidden_states,
        (column_group, column_member),
        (plane_group, plane_member),
        token_block,
        planes,
        8,
        0,
    )
    tokens = gathered.reshape(tokens_total, width)
    normed_attention = layer_norm(tokens, attention_gain)
    normed_feedforward = layer_norm(tokens, feedforward_gain)
    joined = jnp.dot(normed_attention, heads_weight, preferred_element_type=jnp.float32).astype(
        jnp.bfloat16
    )

    indices, starting = positions_of(stream)
    offsets = indices - starting
    query_piece = joined[:, :quarter_width]
    key_piece = joined[:, quarter_width : 2 * quarter_width]
    value_piece = joined[:, 2 * quarter_width :]
    leading = quarter_index == 0
    query_piece = jnp.where(leading, rotate_leading(query_piece, offsets, ROT), query_piece)
    key_piece = jnp.where(leading, rotate_leading(key_piece, offsets, ROT), key_piece)

    page_count = tokens_total // PAGE
    page_rows = jnp.concatenate([key_piece, value_piece], 1).reshape(
        page_count, PAGE * 2 * quarter_width
    )
    targets = page_targets[:, 0]
    page_numbers = jnp.arange(page_count, dtype=jnp.int32)
    earlier = jnp.sum(
        (
            (targets[None, :] == targets[:, None]) & (page_numbers[None, :] < page_numbers[:, None])
        ).astype(jnp.int32),
        axis=1,
    )
    capacity = 2 * page_count // replica_count
    slot_numbers = targets * capacity + earlier
    placing = (
        jnp.arange(replica_count * capacity, dtype=jnp.int32)[:, None] == slot_numbers[None, :]
    ).astype(jnp.bfloat16)
    outgoing = jnp.dot(placing, page_rows, preferred_element_type=jnp.float32).astype(jnp.bfloat16)
    outgoing = outgoing.reshape(replica_count, capacity * PAGE, 2 * quarter_width)
    head_pieces, feedforward = exchange_all(
        1,
        (jnp.concatenate([query_piece, key_piece], 1)[None], "tensor", quarters, True, None),
        work=(_feedforward_up, _feedforward_down),
        inputs=(normed_feedforward, upward_weight, downward_weight),
        results=(jax.ShapeDtypeStruct((tokens_total, width), jnp.float32),),
    )
    queries = head_pieces[:, :, :quarter_width].transpose(1, 0, 2).reshape(tokens_total, HD)
    keys = head_pieces[:, :, quarter_width:].transpose(1, 0, 2).reshape(tokens_total, HD)

    scores = jnp.dot(queries, keys.T, preferred_element_type=jnp.float32) * HD ** (-0.5)
    allowed = (stream[None, :] == stream[:, None]) & (indices[None, :] <= indices[:, None])
    peak = jnp.max(jnp.where(allowed, scores, -jnp.inf), axis=1, keepdims=True)
    weights = jnp.where(allowed, jnp.exp(scores - peak), 0.0)
    weight_sum = jnp.sum(weights, axis=1, keepdims=True)
    mixed = jnp.dot(weights.astype(jnp.bfloat16), value_piece, preferred_element_type=jnp.float32)
    attended = (mixed / weight_sum).astype(jnp.bfloat16)

    partial = (
        jnp.dot(attended, output_weight, preferred_element_type=jnp.float32) + feedforward
    ).astype(jnp.bfloat16)
    layer_output, incoming = reduce_rows(
        partial.reshape(4, planes, 2, local_rows, width),
        hidden_states,
        outgoing,
        (column_group, column_member),
        (same_core_group, same_core_member),
        2,
    )

    cache_pages = incoming.reshape(1, replica_count, capacity, PAGE, 2 * quarter_width)
    return (layer_output, cache_pages)


def solution(mesh):
    in_specs = (
        P(("dp", "tensor"), None),
        P(),
        P(),
        P(None, "tensor"),
        P("tensor", None),
        P(None, "tensor"),
        P("tensor", None),
        P("dp", None),
        P("dp", None),
    )
    out_specs = (P(("dp", "tensor"), None), P("dp", None, None, None, "tensor"))
    return jax.shard_map(shards, mesh=mesh, in_specs=in_specs, out_specs=out_specs, check_vma=False)
```

```python
import functools
import math

import jax
import jax.numpy as jnp
from jax import lax
from jax.experimental import pallas as pl
from jax.experimental.pallas import tpu as pltpu
from jax.sharding import PartitionSpec as P

H = 8
HD = 256
ROT = 64
PAGE = 16


epsilon = 1e-05
rotary_base = 10000.0


def layer_norm(values, gain):
    floats = values.astype(jnp.float32)
    center = jnp.mean(floats, axis=-1, keepdims=True)
    shifted = floats - center
    spread = jnp.mean(shifted * shifted, axis=-1, keepdims=True)
    return (shifted * lax.rsqrt(spread + epsilon) * gain).astype(jnp.bfloat16)


def positions_of(stream):
    indices = jnp.arange(stream.shape[0], dtype=jnp.int32)
    boundary = jnp.concatenate([jnp.ones((1,), dtype=bool), stream[1:] != stream[:-1]])
    starting = lax.cummax(jnp.where(boundary, indices, jnp.zeros_like(indices)), axis=0)
    return (indices, starting)


def rotate_leading(vectors, offsets, rotary_dims):
    half_dims = rotary_dims // 2
    frequency = jnp.exp(
        jnp.arange(half_dims, dtype=jnp.float32) * (-2.0 * math.log(rotary_base) / rotary_dims)
    )
    angles = offsets.astype(jnp.float32)[:, None] * frequency[None, :]
    cosine = jnp.cos(angles)
    sine = jnp.sin(angles)
    floats = vectors.astype(jnp.float32)
    leading = floats[..., :half_dims]
    trailing = floats[..., half_dims:rotary_dims]
    rotated = jnp.concatenate(
        [
            leading * cosine - trailing * sine,
            trailing * cosine + leading * sine,
            floats[..., rotary_dims:],
        ],
        axis=-1,
    )
    return rotated.astype(jnp.bfloat16)


def _exchange_kernel(plans, work, extra_in, extra_out, *refs):
    count = len(plans)
    sources, refs = refs[:count], refs[count:]
    inputs, refs = refs[:extra_in], refs[extra_in:]
    outs, refs = refs[:count], refs[count:]
    results, semaphores = refs[:extra_out], refs[extra_out:]
    mesh_ids = pl.DeviceIdType.MESH
    barrier = pltpu.get_barrier_semaphore()
    steps = []
    for number, (axis, n, shared, position, member) in enumerate(plans):
        src_ref, out_ref = sources[number], outs[number]
        local_sem, send_sem, recv_sem = semaphores[3 * number : 3 * number + 3]
        index = lax.axis_index(axis)
        pos = position(index)

        def peer_copy(q, slot, src_ref=src_ref, out_ref=out_ref, send_sem=send_sem,
                      recv_sem=recv_sem, axis=axis, member=member, index=index, shared=shared):
            return pltpu.make_async_remote_copy(
                src_ref=src_ref.at[0] if shared else src_ref.at[q],
                dst_ref=out_ref.at[slot],
                send_sem=send_sem.at[q],
                recv_sem=recv_sem.at[slot],
                device_id={axis: member(index, q)},
                device_id_type=mesh_ids,
            )

        def greet(k, carry, n=n, pos=pos, axis=axis, member=member, index=index):
            q = (pos + k) % n
            pl.semaphore_signal(
                barrier, inc=1, device_id={axis: member(index, q)}, device_id_type=mesh_ids
            )
            return carry

        lax.fori_loop(1, n, greet, 0)
        local = pltpu.make_async_copy(
            src_ref.at[0] if shared else src_ref.at[pos], out_ref.at[pos], local_sem
        )
        steps.append((n, pos, peer_copy, local))
    carried = work[0](*inputs) if work is not None else None
    pl.semaphore_wait(barrier, sum(plan[1] - 1 for plan in plans))

    for n, pos, peer_copy, local in steps:
        local.start()

        def send(k, carry, n=n, pos=pos, peer_copy=peer_copy):
            peer_copy((pos + k) % n, pos).start()
            return carry

        lax.fori_loop(1, n, send, 0)

    if work is not None:
        work[1](carried, *inputs, *results)

    for n, pos, peer_copy, local in steps:

        def finish(k, carry, n=n, pos=pos, peer_copy=peer_copy):
            q = (pos + k) % n
            peer_copy(q, pos).wait_send()
            peer_copy(q, q).wait_recv()
            return carry

        lax.fori_loop(1, n, finish, 0)
        local.wait()


def contiguous(n):
    return (lambda index: index % n, lambda index, q: index - index % n + q)


def plane_group(index):
    return (index // 8) * 2 + index % 2


def plane_member(index, q):
    return ((q // 2) * 4 + (index // 2) % 4) * 2 + q % 2


def token_block(zc, p):
    return ((p // 2) * 4 + zc) * 2 + p % 2


def plane_rows(rows_ref, q, z):
    return rows_ref.at[q // 2, z, q % 2]


def column_group(index):
    return (index // 2) % 4


def column_member(index, q):
    return ((index // 8) * 4 + q) * 2 + index % 2


def exchange_all(collective_id, *requests, work=None, inputs=(), results=()):
    plans, blocks, shapes, scratch = [], [], [], []
    for data, axis, n, shared, group in requests:
        position, member = group if group is not None else contiguous(n)
        plans.append((axis, n, shared, position, member))
        blocks.append(data)
        shapes.append(jax.ShapeDtypeStruct((n,) + data.shape[1:], data.dtype))
        scratch += [
            pltpu.SemaphoreType.DMA,
            pltpu.SemaphoreType.DMA((n,)),
            pltpu.SemaphoreType.DMA((n,)),
        ]
    operands = blocks + list(inputs)
    out_shapes = shapes + list(results)
    return pl.pallas_call(
        functools.partial(_exchange_kernel, tuple(plans), work, len(inputs), len(results)),
        out_shape=tuple(out_shapes),
        in_specs=[pl.BlockSpec(memory_space=pltpu.VMEM)] * len(operands),
        out_specs=tuple(pl.BlockSpec(memory_space=pltpu.VMEM) for _ in out_shapes),
        scratch_shapes=scratch,
        compiler_params=pltpu.CompilerParams(collective_id=collective_id, has_side_effects=True),
    )(*operands)


def exchange(blocks, axis, n, shared, collective_id, group=None):
    return exchange_all(collective_id, (blocks, axis, n, shared, group))[0]


def _feedforward_up(normed_ref, upward_ref, downward_ref):
    upward = jnp.dot(normed_ref[...], upward_ref[...], preferred_element_type=jnp.float32)
    return (0.5 * upward * (1.0 + lax.erf(upward * math.sqrt(0.5)))).astype(jnp.bfloat16)


def _feedforward_down(hidden, normed_ref, upward_ref, downward_ref, out_ref):
    out_ref[...] = jnp.dot(hidden, downward_ref[...], preferred_element_type=jnp.float32)


def _greet(barrier, groups, extra=0):
    index = lax.axis_index("tensor")
    total = 0
    for n, position, member in groups:
        pos = position(index)

        def greet(k, carry, n=n, pos=pos, member=member):
            pl.semaphore_signal(
                barrier,
                inc=1,
                device_id={"tensor": member(index, (pos + k) % n)},
                device_id_type=pl.DeviceIdType.MESH,
            )
            return carry

        lax.fori_loop(1, n, greet, 0)
        total += n - 1
    pl.semaphore_wait(barrier, total + extra)


def _gather_kernel(n_col, n_y, col, ygroup, slot, x_ref, out_ref, local_sem, col_sem, y_sem, pair_sem,
                   recv_sem):
    index = lax.axis_index("tensor")
    z0, y0, c0 = col[0](index), ygroup[0](index), index % 2
    mesh_ids = pl.DeviceIdType.MESH
    sibling = (2, lambda t: t % 2, lambda t, q: t - t % 2 + q)
    _greet(pltpu.get_barrier_semaphore(), [(n_col, *col), (n_y, *ygroup), sibling])
    partner = index - c0 + 1 - c0

    def block(y, z, c):
        return out_ref.at[slot(y, z, c)]

    def col_copy(q):
        return pltpu.make_async_remote_copy(
            x_ref, block(y0, z0, c0), col_sem.at[q], recv_sem.at[y0, z0, c0],
            device_id={"tensor": col[1](index, q)}, device_id_type=mesh_ids,
        )

    def y_copy(z, q):
        return pltpu.make_async_remote_copy(
            block(y0, z, c0), block(y0, z, c0), y_sem.at[z, q], recv_sem.at[y0, z, c0],
            device_id={"tensor": ygroup[1](index, q)}, device_id_type=mesh_ids,
        )

    def pair_copy(y, z):
        return pltpu.make_async_remote_copy(
            block(y, z, c0), block(y, z, c0), pair_sem.at[y, z], recv_sem.at[y, z, c0],
            device_id={"tensor": partner}, device_id_type=mesh_ids,
        )

    def arrival(y, z, c):
        return pltpu.make_async_remote_copy(
            x_ref, block(y, z, c), col_sem.at[0], recv_sem.at[y, z, c],
            device_id={"tensor": index}, device_id_type=mesh_ids,
        )

    def spread(z):
        def send_y(m, carry):
            y_copy(z, (y0 + m) % n_y).start()
            return carry

        lax.fori_loop(1, n_y, send_y, 0)
        pair_copy(y0, z).start()

    local = pltpu.make_async_copy(x_ref, block(y0, z0, c0), local_sem)
    local.start()

    def send_col(k, carry):
        col_copy((z0 + k) % n_col).start()
        return carry

    lax.fori_loop(1, n_col, send_col, 0)
    local.wait()
    spread(z0)

    def relay_col(k, carry):
        z = (z0 + k) % n_col
        arrival(y0, z, c0).wait_recv()
        spread(z)
        return carry

    lax.fori_loop(1, n_col, relay_col, 0)

    def relay_y(m, carry):
        y = (y0 + m) % n_y

        def each(k, inner):
            z = (z0 + k) % n_col
            arrival(y, z, c0).wait_recv()
            pair_copy(y, z).start()
            return inner

        return lax.fori_loop(0, n_col, each, carry)

    lax.fori_loop(1, n_y, relay_y, 0)

    def finish_col(k, carry):
        col_copy((z0 + k) % n_col).wait_send()
        return carry

    lax.fori_loop(1, n_col, finish_col, 0)

    def finish_y(k, carry):
        z = (z0 + k) % n_col

        def each(m, inner):
            y_copy(z, (y0 + m) % n_y).wait_send()
            return inner

        return lax.fori_loop(1, n_y, each, carry)

    lax.fori_loop(0, n_col, finish_y, 0)

    def finish_pair(m, carry):
        y = (y0 + m) % n_y

        def each(k, inner):
            z = (z0 + k) % n_col
            pair_copy(y, z).wait_send()
            arrival(y, z, 1 - c0).wait_recv()
            return inner

        return lax.fori_loop(0, n_col, each, carry)

    lax.fori_loop(0, n_y, finish_pair, 0)


def gather_tokens(x, col, ygroup, slot, n_col, n_y, collective_id):
    return pl.pallas_call(
        functools.partial(_gather_kernel, n_col, n_y, col, ygroup, slot),
        out_shape=jax.ShapeDtypeStruct((n_col * n_y * 2,) + x.shape, x.dtype),
        in_specs=[pl.BlockSpec(memory_space=pltpu.VMEM)],
        out_specs=pl.BlockSpec(memory_space=pltpu.VMEM),
        scratch_shapes=[
            pltpu.SemaphoreType.DMA,
            pltpu.SemaphoreType.DMA((n_col,)),
            pltpu.SemaphoreType.DMA((n_col, n_y)),
            pltpu.SemaphoreType.DMA((n_y, n_col)),
            pltpu.SemaphoreType.DMA((n_y, n_col, 2)),
        ],
        compiler_params=pltpu.CompilerParams(collective_id=collective_id, has_side_effects=True),
    )(x)


def token_slot(y, z, c):
    return (y * 4 + z) * 2 + c


def _reduce_kernel(n_col, n_y, n_dp, col, ygroup, rows_ref, x_ref, pages_ref, out_ref, pages_out,
                   inbox0, chip, inbox1, stage, inbox2, sem0, local_sem, send_sem, recv_sem,
                   send2_sem, recv2_sem, page_local_sem, page_send_sem, page_recv_sem):
    index = lax.axis_index("tensor")
    cpos, ypos, core = col[0](index), ygroup[0](index), index % 2
    mesh_ids = pl.DeviceIdType.MESH
    barrier = pltpu.get_barrier_semaphore()
    group = lax.axis_index("dp")

    def page_copy(g, slot):
        return pltpu.make_async_remote_copy(
            pages_ref.at[g], pages_out.at[slot], page_send_sem.at[g], page_recv_sem.at[slot],
            device_id={"dp": g}, device_id_type=mesh_ids,
        )

    def greet_group(k, carry):
        pl.semaphore_signal(
            barrier, inc=1, device_id={"dp": (group + k) % n_dp}, device_id_type=mesh_ids
        )
        return carry

    lax.fori_loop(1, n_dp, greet_group, 0)
    sibling = (2, lambda t: t % 2, lambda t, q: t - t % 2 + q)
    _greet(barrier, [sibling, (n_y, *ygroup), (n_col, *col)], extra=n_dp - 1)
    page_local = pltpu.make_async_copy(pages_ref.at[group], pages_out.at[group], page_local_sem)
    page_local.start()

    def send_pages(k, carry):
        page_copy((group + k) % n_dp, group).start()
        return carry

    lax.fori_loop(1, n_dp, send_pages, 0)

    pair = pltpu.make_async_remote_copy(
        rows_ref.at[:, :, 1 - core], inbox0, sem0.at[0], sem0.at[1],
        device_id={"tensor": index - core + 1 - core}, device_id_type=mesh_ids,
    )
    pair.start()
    pair.wait_send()
    pair.wait_recv()
    for y in range(n_y):
        for z in range(n_col):
            chip[y, z] = (
                rows_ref[y, z, core].astype(jnp.float32) + inbox0[y, z].astype(jnp.float32)
            ).astype(chip.dtype)

    def plane_copy(q, z, slot):
        return pltpu.make_async_remote_copy(
            chip.at[q, z], inbox1.at[z, slot], send_sem.at[z, q], recv_sem.at[z, slot],
            device_id={"tensor": ygroup[1](index, q)}, device_id_type=mesh_ids,
        )

    def col_copy(q, slot):
        return pltpu.make_async_remote_copy(
            stage.at[q], inbox2.at[slot], send2_sem.at[q], recv2_sem.at[slot],
            device_id={"tensor": col[1](index, q)}, device_id_type=mesh_ids,
        )

    order = [(cpos + 1 + k) % n_col for k in range(n_col)]
    locals_ = []
    for z in order:
        local = pltpu.make_async_copy(chip.at[ypos, z], inbox1.at[z, ypos], local_sem.at[z])
        local.start()
        locals_.append(local)

        def send_plane(m, carry, z=z):
            plane_copy((ypos + m) % n_y, z, ypos).start()
            return carry

        lax.fori_loop(1, n_y, send_plane, 0)

    def plane_sum(z, local):
        def arrive(m, carry):
            plane_copy((ypos + m) % n_y, z, (ypos + m) % n_y).wait_recv()
            return carry

        lax.fori_loop(1, n_y, arrive, 0)
        local.wait()
        total = inbox1[z, 0].astype(jnp.float32)
        for sender in range(1, n_y):
            total = total + inbox1[z, sender].astype(jnp.float32)
        return total

    for z, local in zip(order[:-1], locals_[:-1]):
        stage[z] = plane_sum(z, local).astype(stage.dtype)
        col_copy(z, cpos).start()

    result = x_ref[...].astype(jnp.float32) + plane_sum(cpos, locals_[-1])

    def finish_plane(m, carry):
        q = (ypos + m) % n_y
        for z in order:
            plane_copy(q, z, ypos).wait_send()
        return carry

    lax.fori_loop(1, n_y, finish_plane, 0)

    for z in order[:-1]:
        col_copy(z, cpos).wait_send()
        col_copy(z, z).wait_recv()
        result = result + inbox2[z].astype(jnp.float32)
    out_ref[...] = result

    def finish_pages(k, carry):
        g = (group + k) % n_dp
        page_copy(g, group).wait_send()
        page_copy(g, g).wait_recv()
        return carry

    lax.fori_loop(1, n_dp, finish_pages, 0)
    page_local.wait()


def reduce_rows(rows, x, pages, col, ygroup, collective_id):
    n_y, n_col = rows.shape[0], rows.shape[1]
    block = x.shape
    n_dp = pages.shape[0]
    return pl.pallas_call(
        functools.partial(_reduce_kernel, n_col, n_y, n_dp, col, ygroup),
        out_shape=(
            jax.ShapeDtypeStruct(block, jnp.float32),
            jax.ShapeDtypeStruct(pages.shape, pages.dtype),
        ),
        in_specs=[pl.BlockSpec(memory_space=pltpu.VMEM)] * 3,
        out_specs=(pl.BlockSpec(memory_space=pltpu.VMEM), pl.BlockSpec(memory_space=pltpu.VMEM)),
        scratch_shapes=[
            pltpu.VMEM((n_y, n_col) + block, rows.dtype),
            pltpu.VMEM((n_y, n_col) + block, rows.dtype),
            pltpu.VMEM((n_col, n_y) + block, rows.dtype),
            pltpu.VMEM((n_col,) + block, rows.dtype),
            pltpu.VMEM((n_col,) + block, rows.dtype),
            pltpu.SemaphoreType.DMA((2,)),
            pltpu.SemaphoreType.DMA((n_col,)),
            pltpu.SemaphoreType.DMA((n_col, n_y)),
            pltpu.SemaphoreType.DMA((n_col, n_y)),
            pltpu.SemaphoreType.DMA((n_col,)),
            pltpu.SemaphoreType.DMA((n_col,)),
            pltpu.SemaphoreType.DMA,
            pltpu.SemaphoreType.DMA((n_dp,)),
            pltpu.SemaphoreType.DMA((n_dp,)),
        ],
        compiler_params=pltpu.CompilerParams(collective_id=collective_id, has_side_effects=True),
    )(rows, x, pages)


def same_core_group(index):
    return index // 8


def same_core_member(index, q):
    return q * 8 + index % 8


def shards(
    hidden_states,
    attention_gain,
    feedforward_gain,
    heads_weight,
    output_weight,
    upward_weight,
    downward_weight,
    segments,
    page_targets,
):
    tensor_count = lax.axis_size("tensor")
    replica_count = lax.axis_size("dp")
    tensor_index = lax.axis_index("tensor")
    quarters = tensor_count // H
    quarter_width = HD // quarters
    quarter_index = tensor_index % quarters
    stream = segments[0]
    tokens_total = stream.shape[0]
    local_rows = hidden_states.shape[0]

    width = hidden_states.shape[1]
    planes = tensor_count // 8
    gathered = gather_tokens(
        hidden_states,
        (column_group, column_member),
        (same_core_group, same_core_member),
        token_slot,
        planes,
        4,
        0,
    )
    tokens = gathered.reshape(tokens_total, width)
    normed_attention = layer_norm(tokens, attention_gain)
    normed_feedforward = layer_norm(tokens, feedforward_gain)
    joined = jnp.dot(normed_attention, heads_weight, preferred_element_type=jnp.float32).astype(
        jnp.bfloat16
    )

    indices, starting = positions_of(stream)
    offsets = indices - starting
    query_piece = joined[:, :quarter_width]
    key_piece = joined[:, quarter_width : 2 * quarter_width]
    value_piece = joined[:, 2 * quarter_width :]
    leading = quarter_index == 0
    query_piece = jnp.where(leading, rotate_leading(query_piece, offsets, ROT), query_piece)
    key_piece = jnp.where(leading, rotate_leading(key_piece, offsets, ROT), key_piece)

    page_count = tokens_total // PAGE
    page_rows = jnp.concatenate([key_piece, value_piece], 1).reshape(
        page_count, PAGE * 2 * quarter_width
    )
    targets = page_targets[:, 0]
    page_numbers = jnp.arange(page_count, dtype=jnp.int32)
    earlier = jnp.sum(
        (
            (targets[None, :] == targets[:, None]) & (page_numbers[None, :] < page_numbers[:, None])
        ).astype(jnp.int32),
        axis=1,
    )
    capacity = 2 * page_count // replica_count
    slot_numbers = targets * capacity + earlier
    placing = (
        jnp.arange(replica_count * capacity, dtype=jnp.int32)[:, None] == slot_numbers[None, :]
    ).astype(jnp.bfloat16)
    outgoing = jnp.dot(placing, page_rows, preferred_element_type=jnp.float32).astype(jnp.bfloat16)
    outgoing = outgoing.reshape(replica_count, capacity * PAGE, 2 * quarter_width)
    head_pieces, feedforward = exchange_all(
        1,
        (jnp.concatenate([query_piece, key_piece], 1)[None], "tensor", quarters, True, None),
        work=(_feedforward_up, _feedforward_down),
        inputs=(normed_feedforward, upward_weight, downward_weight),
        results=(jax.ShapeDtypeStruct((tokens_total, width), jnp.float32),),
    )
    queries = head_pieces[:, :, :quarter_width].transpose(1, 0, 2).reshape(tokens_total, HD)
    keys = head_pieces[:, :, quarter_width:].transpose(1, 0, 2).reshape(tokens_total, HD)

    scores = jnp.dot(queries, keys.T, preferred_element_type=jnp.float32) * HD ** (-0.5)
    allowed = (stream[None, :] == stream[:, None]) & (indices[None, :] <= indices[:, None])
    peak = jnp.max(jnp.where(allowed, scores, -jnp.inf), axis=1, keepdims=True)
    weights = jnp.where(allowed, jnp.exp(scores - peak), 0.0)
    weight_sum = jnp.sum(weights, axis=1, keepdims=True)
    mixed = jnp.dot(weights.astype(jnp.bfloat16), value_piece, preferred_element_type=jnp.float32)
    attended = (mixed / weight_sum).astype(jnp.bfloat16)

    partial = (
        jnp.dot(attended, output_weight, preferred_element_type=jnp.float32) + feedforward
    ).astype(jnp.bfloat16)
    layer_output, incoming = reduce_rows(
        partial.reshape(4, planes, 2, local_rows, width),
        hidden_states,
        outgoing,
        (column_group, column_member),
        (same_core_group, same_core_member),
        2,
    )

    cache_pages = incoming.reshape(1, replica_count, capacity, PAGE, 2 * quarter_width)
    return (layer_output, cache_pages)


def solution(mesh):
    in_specs = (
        P(("dp", "tensor"), None),
        P(),
        P(),
        P(None, "tensor"),
        P("tensor", None),
        P(None, "tensor"),
        P("tensor", None),
        P("dp", None),
        P("dp", None),
    )
    out_specs = (P(("dp", "tensor"), None), P("dp", None, None, None, "tensor"))
    return jax.shard_map(shards, mesh=mesh, in_specs=in_specs, out_specs=out_specs, check_vma=False)
```

```python
import functools
import math

import jax
import jax.numpy as jnp
from jax import lax
from jax.experimental import pallas as pl
from jax.experimental.pallas import tpu as pltpu
from jax.sharding import PartitionSpec as P

H = 8
HD = 256
ROT = 64
PAGE = 16


epsilon = 1e-05
rotary_base = 10000.0


def layer_norm(values, gain):
    floats = values.astype(jnp.float32)
    center = jnp.mean(floats, axis=-1, keepdims=True)
    shifted = floats - center
    spread = jnp.mean(shifted * shifted, axis=-1, keepdims=True)
    return (shifted * lax.rsqrt(spread + epsilon) * gain).astype(jnp.bfloat16)


def positions_of(stream):
    indices = jnp.arange(stream.shape[0], dtype=jnp.int32)
    boundary = jnp.concatenate([jnp.ones((1,), dtype=bool), stream[1:] != stream[:-1]])
    starting = lax.cummax(jnp.where(boundary, indices, jnp.zeros_like(indices)), axis=0)
    return (indices, starting)


def rotate_leading(vectors, offsets, rotary_dims):
    half_dims = rotary_dims // 2
    frequency = jnp.exp(
        jnp.arange(half_dims, dtype=jnp.float32) * (-2.0 * math.log(rotary_base) / rotary_dims)
    )
    angles = offsets.astype(jnp.float32)[:, None] * frequency[None, :]
    cosine = jnp.cos(angles)
    sine = jnp.sin(angles)
    floats = vectors.astype(jnp.float32)
    leading = floats[..., :half_dims]
    trailing = floats[..., half_dims:rotary_dims]
    rotated = jnp.concatenate(
        [
            leading * cosine - trailing * sine,
            trailing * cosine + leading * sine,
            floats[..., rotary_dims:],
        ],
        axis=-1,
    )
    return rotated.astype(jnp.bfloat16)


def _exchange_kernel(plans, work, extra_in, extra_out, *refs):
    count = len(plans)
    sources, refs = refs[:count], refs[count:]
    inputs, refs = refs[:extra_in], refs[extra_in:]
    outs, refs = refs[:count], refs[count:]
    results, semaphores = refs[:extra_out], refs[extra_out:]
    mesh_ids = pl.DeviceIdType.MESH
    barrier = pltpu.get_barrier_semaphore()
    steps = []
    for number, (axis, n, shared, position, member) in enumerate(plans):
        src_ref, out_ref = sources[number], outs[number]
        local_sem, send_sem, recv_sem = semaphores[3 * number : 3 * number + 3]
        index = lax.axis_index(axis)
        pos = position(index)

        def peer_copy(q, slot, src_ref=src_ref, out_ref=out_ref, send_sem=send_sem,
                      recv_sem=recv_sem, axis=axis, member=member, index=index, shared=shared):
            return pltpu.make_async_remote_copy(
                src_ref=src_ref.at[0] if shared else src_ref.at[q],
                dst_ref=out_ref.at[slot],
                send_sem=send_sem.at[q],
                recv_sem=recv_sem.at[slot],
                device_id={axis: member(index, q)},
                device_id_type=mesh_ids,
            )

        def greet(k, carry, n=n, pos=pos, axis=axis, member=member, index=index):
            q = (pos + k) % n
            pl.semaphore_signal(
                barrier, inc=1, device_id={axis: member(index, q)}, device_id_type=mesh_ids
            )
            return carry

        lax.fori_loop(1, n, greet, 0)
        local = pltpu.make_async_copy(
            src_ref.at[0] if shared else src_ref.at[pos], out_ref.at[pos], local_sem
        )
        steps.append((n, pos, peer_copy, local))
    carried = work[0](*inputs) if work is not None else None
    pl.semaphore_wait(barrier, sum(plan[1] - 1 for plan in plans))

    for n, pos, peer_copy, local in steps:
        local.start()

        def send(k, carry, n=n, pos=pos, peer_copy=peer_copy):
            peer_copy((pos + k) % n, pos).start()
            return carry

        lax.fori_loop(1, n, send, 0)

    if work is not None:
        work[1](carried, *inputs, *results)

    for n, pos, peer_copy, local in steps:

        def finish(k, carry, n=n, pos=pos, peer_copy=peer_copy):
            q = (pos + k) % n
            peer_copy(q, pos).wait_send()
            peer_copy(q, q).wait_recv()
            return carry

        lax.fori_loop(1, n, finish, 0)
        local.wait()


def contiguous(n):
    return (lambda index: index % n, lambda index, q: index - index % n + q)


def plane_group(index):
    return (index // 8) * 2 + index % 2


def plane_member(index, q):
    return ((q // 2) * 4 + (index // 2) % 4) * 2 + q % 2


def token_block(zc, p):
    return ((p // 2) * 4 + zc) * 2 + p % 2


def plane_rows(rows_ref, q, z):
    return rows_ref.at[q // 2, z, q % 2]


def column_group(index):
    return (index // 2) % 4


def column_member(index, q):
    return ((index // 8) * 4 + q) * 2 + index % 2


def exchange_all(collective_id, *requests, work=None, inputs=(), results=()):
    plans, blocks, shapes, scratch = [], [], [], []
    for data, axis, n, shared, group in requests:
        position, member = group if group is not None else contiguous(n)
        plans.append((axis, n, shared, position, member))
        blocks.append(data)
        shapes.append(jax.ShapeDtypeStruct((n,) + data.shape[1:], data.dtype))
        scratch += [
            pltpu.SemaphoreType.DMA,
            pltpu.SemaphoreType.DMA((n,)),
            pltpu.SemaphoreType.DMA((n,)),
        ]
    operands = blocks + list(inputs)
    out_shapes = shapes + list(results)
    return pl.pallas_call(
        functools.partial(_exchange_kernel, tuple(plans), work, len(inputs), len(results)),
        out_shape=tuple(out_shapes),
        in_specs=[pl.BlockSpec(memory_space=pltpu.VMEM)] * len(operands),
        out_specs=tuple(pl.BlockSpec(memory_space=pltpu.VMEM) for _ in out_shapes),
        scratch_shapes=scratch,
        compiler_params=pltpu.CompilerParams(collective_id=collective_id, has_side_effects=True),
    )(*operands)


def exchange(blocks, axis, n, shared, collective_id, group=None):
    return exchange_all(collective_id, (blocks, axis, n, shared, group))[0]


def _feedforward_up(normed_ref, upward_ref, downward_ref):
    upward = jnp.dot(normed_ref[...], upward_ref[...], preferred_element_type=jnp.float32)
    return (0.5 * upward * (1.0 + lax.erf(upward * math.sqrt(0.5)))).astype(jnp.bfloat16)


def _feedforward_down(hidden, normed_ref, upward_ref, downward_ref, out_ref):
    out_ref[...] = jnp.dot(hidden, downward_ref[...], preferred_element_type=jnp.float32)


def _signal(barrier, groups):
    index = lax.axis_index("tensor")
    total = 0
    for n, position, member in groups:
        pos = position(index)

        def greet(k, carry, n=n, pos=pos, member=member):
            pl.semaphore_signal(
                barrier,
                inc=1,
                device_id={"tensor": member(index, (pos + k) % n)},
                device_id_type=pl.DeviceIdType.MESH,
            )
            return carry

        lax.fori_loop(1, n, greet, 0)
        total += n - 1
    return total


def _greet(barrier, groups, extra=0):
    index = lax.axis_index("tensor")
    total = 0
    for n, position, member in groups:
        pos = position(index)

        def greet(k, carry, n=n, pos=pos, member=member):
            pl.semaphore_signal(
                barrier,
                inc=1,
                device_id={"tensor": member(index, (pos + k) % n)},
                device_id_type=pl.DeviceIdType.MESH,
            )
            return carry

        lax.fori_loop(1, n, greet, 0)
        total += n - 1
    pl.semaphore_wait(barrier, total + extra)


def _gather_kernel(n_col, n_y, col, ygroup, slot, x_ref, out_ref, local_sem, col_sem, y_sem, pair_sem,
                   recv_sem):
    index = lax.axis_index("tensor")
    z0, y0, c0 = col[0](index), ygroup[0](index), index % 2
    mesh_ids = pl.DeviceIdType.MESH
    sibling = (2, lambda t: t % 2, lambda t, q: t - t % 2 + q)
    _greet(pltpu.get_barrier_semaphore(), [(n_col, *col), (n_y, *ygroup), sibling])
    partner = index - c0 + 1 - c0

    def block(y, z, c):
        return out_ref.at[slot(y, z, c)]

    def col_copy(q):
        return pltpu.make_async_remote_copy(
            x_ref, block(y0, z0, c0), col_sem.at[q], recv_sem.at[y0, z0, c0],
            device_id={"tensor": col[1](index, q)}, device_id_type=mesh_ids,
        )

    def y_copy(z, q):
        return pltpu.make_async_remote_copy(
            block(y0, z, c0), block(y0, z, c0), y_sem.at[z, q], recv_sem.at[y0, z, c0],
            device_id={"tensor": ygroup[1](index, q)}, device_id_type=mesh_ids,
        )

    def pair_copy(y, z):
        return pltpu.make_async_remote_copy(
            block(y, z, c0), block(y, z, c0), pair_sem.at[y, z], recv_sem.at[y, z, c0],
            device_id={"tensor": partner}, device_id_type=mesh_ids,
        )

    def arrival(y, z, c):
        return pltpu.make_async_remote_copy(
            x_ref, block(y, z, c), col_sem.at[0], recv_sem.at[y, z, c],
            device_id={"tensor": index}, device_id_type=mesh_ids,
        )

    def spread(z):
        def send_y(m, carry):
            y_copy(z, (y0 + m) % n_y).start()
            return carry

        lax.fori_loop(1, n_y, send_y, 0)
        pair_copy(y0, z).start()

    local = pltpu.make_async_copy(x_ref, block(y0, z0, c0), local_sem)
    local.start()

    def send_col(k, carry):
        col_copy((z0 + k) % n_col).start()
        return carry

    lax.fori_loop(1, n_col, send_col, 0)
    local.wait()
    spread(z0)

    def relay_col(k, carry):
        z = (z0 + k) % n_col
        arrival(y0, z, c0).wait_recv()
        spread(z)
        return carry

    lax.fori_loop(1, n_col, relay_col, 0)

    def relay_y(m, carry):
        y = (y0 + m) % n_y

        def each(k, inner):
            z = (z0 + k) % n_col
            arrival(y, z, c0).wait_recv()
            pair_copy(y, z).start()
            return inner

        return lax.fori_loop(0, n_col, each, carry)

    lax.fori_loop(1, n_y, relay_y, 0)

    def finish_col(k, carry):
        col_copy((z0 + k) % n_col).wait_send()
        return carry

    lax.fori_loop(1, n_col, finish_col, 0)

    def finish_y(k, carry):
        z = (z0 + k) % n_col

        def each(m, inner):
            y_copy(z, (y0 + m) % n_y).wait_send()
            return inner

        return lax.fori_loop(1, n_y, each, carry)

    lax.fori_loop(0, n_col, finish_y, 0)

    def finish_pair(m, carry):
        y = (y0 + m) % n_y

        def each(k, inner):
            z = (z0 + k) % n_col
            pair_copy(y, z).wait_send()
            arrival(y, z, 1 - c0).wait_recv()
            return inner

        return lax.fori_loop(0, n_col, each, carry)

    lax.fori_loop(0, n_y, finish_pair, 0)


def gather_tokens(x, col, ygroup, slot, n_col, n_y, collective_id):
    return pl.pallas_call(
        functools.partial(_gather_kernel, n_col, n_y, col, ygroup, slot),
        out_shape=jax.ShapeDtypeStruct((n_col * n_y * 2,) + x.shape, x.dtype),
        in_specs=[pl.BlockSpec(memory_space=pltpu.VMEM)],
        out_specs=pl.BlockSpec(memory_space=pltpu.VMEM),
        scratch_shapes=[
            pltpu.SemaphoreType.DMA,
            pltpu.SemaphoreType.DMA((n_col,)),
            pltpu.SemaphoreType.DMA((n_col, n_y)),
            pltpu.SemaphoreType.DMA((n_y, n_col)),
            pltpu.SemaphoreType.DMA((n_y, n_col, 2)),
        ],
        compiler_params=pltpu.CompilerParams(collective_id=collective_id, has_side_effects=True),
    )(x)


def token_slot(y, z, c):
    return (y * 4 + z) * 2 + c


def _reduce_kernel(n_col, n_y, n_dp, col, ygroup, attended_ref, output_ref, feedforward_ref, x_ref,
                   pages_ref, out_ref, pages_out, rows_ref, inbox0, chip, inbox1, stage, inbox2, sem0,
                   local_sem, send_sem, recv_sem, send2_sem, recv2_sem, page_local_sem, page_send_sem,
                   page_recv_sem):
    index = lax.axis_index("tensor")
    cpos, ypos, core = col[0](index), ygroup[0](index), index % 2
    mesh_ids = pl.DeviceIdType.MESH
    barrier = pltpu.get_barrier_semaphore()
    group = lax.axis_index("dp")

    def page_copy(g, slot):
        return pltpu.make_async_remote_copy(
            pages_ref.at[g], pages_out.at[slot], page_send_sem.at[g], page_recv_sem.at[slot],
            device_id={"dp": g}, device_id_type=mesh_ids,
        )

    def greet_group(k, carry):
        pl.semaphore_signal(
            barrier, inc=1, device_id={"dp": (group + k) % n_dp}, device_id_type=mesh_ids
        )
        return carry

    lax.fori_loop(1, n_dp, greet_group, 0)
    sibling = (2, lambda t: t % 2, lambda t, q: t - t % 2 + q)
    total = _signal(barrier, [sibling, (n_y, *ygroup), (n_col, *col)])

    product = (
        jnp.dot(attended_ref[...], output_ref[...], preferred_element_type=jnp.float32)
        + feedforward_ref[...]
    )
    rows = x_ref.shape[0]
    for owner in range(n_y * n_col * 2):
        rows_ref[owner // (2 * n_col), (owner // 2) % n_col, owner % 2] = product[
            owner * rows : (owner + 1) * rows
        ].astype(rows_ref.dtype)
    pl.semaphore_wait(barrier, total + n_dp - 1)
    page_local = pltpu.make_async_copy(pages_ref.at[group], pages_out.at[group], page_local_sem)
    page_local.start()

    def send_pages(k, carry):
        page_copy((group + k) % n_dp, group).start()
        return carry

    lax.fori_loop(1, n_dp, send_pages, 0)

    pair = pltpu.make_async_remote_copy(
        rows_ref.at[:, :, 1 - core], inbox0, sem0.at[0], sem0.at[1],
        device_id={"tensor": index - core + 1 - core}, device_id_type=mesh_ids,
    )
    pair.start()
    pair.wait_send()
    pair.wait_recv()
    for y in range(n_y):
        for z in range(n_col):
            chip[y, z] = (
                rows_ref[y, z, core].astype(jnp.float32) + inbox0[y, z].astype(jnp.float32)
            ).astype(chip.dtype)

    def plane_copy(q, z, slot):
        return pltpu.make_async_remote_copy(
            chip.at[q, z], inbox1.at[z, slot], send_sem.at[z, q], recv_sem.at[z, slot],
            device_id={"tensor": ygroup[1](index, q)}, device_id_type=mesh_ids,
        )

    def col_copy(q, slot):
        return pltpu.make_async_remote_copy(
            stage.at[q], inbox2.at[slot], send2_sem.at[q], recv2_sem.at[slot],
            device_id={"tensor": col[1](index, q)}, device_id_type=mesh_ids,
        )

    order = [(cpos + 1 + k) % n_col for k in range(n_col)]
    locals_ = []
    for z in order:
        local = pltpu.make_async_copy(chip.at[ypos, z], inbox1.at[z, ypos], local_sem.at[z])
        local.start()
        locals_.append(local)

        def send_plane(m, carry, z=z):
            plane_copy((ypos + m) % n_y, z, ypos).start()
            return carry

        lax.fori_loop(1, n_y, send_plane, 0)

    def plane_sum(z, local):
        def arrive(m, carry):
            plane_copy((ypos + m) % n_y, z, (ypos + m) % n_y).wait_recv()
            return carry

        lax.fori_loop(1, n_y, arrive, 0)
        local.wait()
        total = inbox1[z, 0].astype(jnp.float32)
        for sender in range(1, n_y):
            total = total + inbox1[z, sender].astype(jnp.float32)
        return total

    for z, local in zip(order[:-1], locals_[:-1]):
        stage[z] = plane_sum(z, local).astype(stage.dtype)
        col_copy(z, cpos).start()

    result = x_ref[...].astype(jnp.float32) + plane_sum(cpos, locals_[-1])

    def finish_plane(m, carry):
        q = (ypos + m) % n_y
        for z in order:
            plane_copy(q, z, ypos).wait_send()
        return carry

    lax.fori_loop(1, n_y, finish_plane, 0)

    for z in order[:-1]:
        col_copy(z, cpos).wait_send()
        col_copy(z, z).wait_recv()
        result = result + inbox2[z].astype(jnp.float32)
    out_ref[...] = result

    def finish_pages(k, carry):
        g = (group + k) % n_dp
        page_copy(g, group).wait_send()
        page_copy(g, g).wait_recv()
        return carry

    lax.fori_loop(1, n_dp, finish_pages, 0)
    page_local.wait()


def reduce_rows(attended, output_weight, feedforward, x, pages, col, ygroup, n_y, n_col, collective_id):
    block = x.shape
    n_dp = pages.shape[0]
    operands = (attended, output_weight, feedforward, x, pages)
    return pl.pallas_call(
        functools.partial(_reduce_kernel, n_col, n_y, n_dp, col, ygroup),
        out_shape=(
            jax.ShapeDtypeStruct(block, jnp.float32),
            jax.ShapeDtypeStruct(pages.shape, pages.dtype),
        ),
        in_specs=[pl.BlockSpec(memory_space=pltpu.VMEM)] * len(operands),
        out_specs=(pl.BlockSpec(memory_space=pltpu.VMEM), pl.BlockSpec(memory_space=pltpu.VMEM)),
        scratch_shapes=[
            pltpu.VMEM((n_y, n_col, 2) + block, x.dtype),
            pltpu.VMEM((n_y, n_col) + block, x.dtype),
            pltpu.VMEM((n_y, n_col) + block, x.dtype),
            pltpu.VMEM((n_col, n_y) + block, x.dtype),
            pltpu.VMEM((n_col,) + block, x.dtype),
            pltpu.VMEM((n_col,) + block, x.dtype),
            pltpu.SemaphoreType.DMA((2,)),
            pltpu.SemaphoreType.DMA((n_col,)),
            pltpu.SemaphoreType.DMA((n_col, n_y)),
            pltpu.SemaphoreType.DMA((n_col, n_y)),
            pltpu.SemaphoreType.DMA((n_col,)),
            pltpu.SemaphoreType.DMA((n_col,)),
            pltpu.SemaphoreType.DMA,
            pltpu.SemaphoreType.DMA((n_dp,)),
            pltpu.SemaphoreType.DMA((n_dp,)),
        ],
        compiler_params=pltpu.CompilerParams(collective_id=collective_id, has_side_effects=True),
    )(*operands)


def same_core_group(index):
    return index // 8


def same_core_member(index, q):
    return q * 8 + index % 8


def shards(
    hidden_states,
    attention_gain,
    feedforward_gain,
    heads_weight,
    output_weight,
    upward_weight,
    downward_weight,
    segments,
    page_targets,
):
    tensor_count = lax.axis_size("tensor")
    replica_count = lax.axis_size("dp")
    tensor_index = lax.axis_index("tensor")
    quarters = tensor_count // H
    quarter_width = HD // quarters
    quarter_index = tensor_index % quarters
    stream = segments[0]
    tokens_total = stream.shape[0]
    local_rows = hidden_states.shape[0]

    width = hidden_states.shape[1]
    planes = tensor_count // 8
    gathered = gather_tokens(
        hidden_states,
        (column_group, column_member),
        (same_core_group, same_core_member),
        token_slot,
        planes,
        4,
        0,
    )
    tokens = gathered.reshape(tokens_total, width)
    normed_attention = layer_norm(tokens, attention_gain)
    normed_feedforward = layer_norm(tokens, feedforward_gain)
    joined = jnp.dot(normed_attention, heads_weight, preferred_element_type=jnp.float32).astype(
        jnp.bfloat16
    )

    indices, starting = positions_of(stream)
    offsets = indices - starting
    query_piece = joined[:, :quarter_width]
    key_piece = joined[:, quarter_width : 2 * quarter_width]
    value_piece = joined[:, 2 * quarter_width :]
    leading = quarter_index == 0
    query_piece = jnp.where(leading, rotate_leading(query_piece, offsets, ROT), query_piece)
    key_piece = jnp.where(leading, rotate_leading(key_piece, offsets, ROT), key_piece)

    page_count = tokens_total // PAGE
    page_rows = jnp.concatenate([key_piece, value_piece], 1).reshape(
        page_count, PAGE * 2 * quarter_width
    )
    targets = page_targets[:, 0]
    page_numbers = jnp.arange(page_count, dtype=jnp.int32)
    earlier = jnp.sum(
        (
            (targets[None, :] == targets[:, None]) & (page_numbers[None, :] < page_numbers[:, None])
        ).astype(jnp.int32),
        axis=1,
    )
    capacity = 2 * page_count // replica_count
    slot_numbers = targets * capacity + earlier
    placing = (
        jnp.arange(replica_count * capacity, dtype=jnp.int32)[:, None] == slot_numbers[None, :]
    ).astype(jnp.bfloat16)
    outgoing = jnp.dot(placing, page_rows, preferred_element_type=jnp.float32).astype(jnp.bfloat16)
    outgoing = outgoing.reshape(replica_count, capacity * PAGE, 2 * quarter_width)
    head_pieces, feedforward = exchange_all(
        1,
        (jnp.concatenate([query_piece, key_piece], 1)[None], "tensor", quarters, True, None),
        work=(_feedforward_up, _feedforward_down),
        inputs=(normed_feedforward, upward_weight, downward_weight),
        results=(jax.ShapeDtypeStruct((tokens_total, width), jnp.float32),),
    )
    queries = head_pieces[:, :, :quarter_width].transpose(1, 0, 2).reshape(tokens_total, HD)
    keys = head_pieces[:, :, quarter_width:].transpose(1, 0, 2).reshape(tokens_total, HD)

    scores = jnp.dot(queries, keys.T, preferred_element_type=jnp.float32) * HD ** (-0.5)
    allowed = (stream[None, :] == stream[:, None]) & (indices[None, :] <= indices[:, None])
    peak = jnp.max(jnp.where(allowed, scores, -jnp.inf), axis=1, keepdims=True)
    weights = jnp.where(allowed, jnp.exp(scores - peak), 0.0)
    weight_sum = jnp.sum(weights, axis=1, keepdims=True)
    mixed = jnp.dot(weights.astype(jnp.bfloat16), value_piece, preferred_element_type=jnp.float32)
    attended = (mixed / weight_sum).astype(jnp.bfloat16)

    layer_output, incoming = reduce_rows(
        attended,
        output_weight,
        feedforward,
        hidden_states,
        outgoing,
        (column_group, column_member),
        (same_core_group, same_core_member),
        4,
        planes,
        2,
    )

    cache_pages = incoming.reshape(1, replica_count, capacity, PAGE, 2 * quarter_width)
    return (layer_output, cache_pages)


def solution(mesh):
    in_specs = (
        P(("dp", "tensor"), None),
        P(),
        P(),
        P(None, "tensor"),
        P("tensor", None),
        P(None, "tensor"),
        P("tensor", None),
        P("dp", None),
        P("dp", None),
    )
    out_specs = (P(("dp", "tensor"), None), P("dp", None, None, None, "tensor"))
    return jax.shard_map(shards, mesh=mesh, in_specs=in_specs, out_specs=out_specs, check_vma=False)
```

```python
import functools
import math

import jax
import jax.numpy as jnp
from jax import lax
from jax.experimental import pallas as pl
from jax.experimental.pallas import tpu as pltpu
from jax.sharding import PartitionSpec as P

H = 8
HD = 256
ROT = 64
PAGE = 16


epsilon = 1e-05
rotary_base = 10000.0


def layer_norm(values, gain):
    floats = values.astype(jnp.float32)
    center = jnp.mean(floats, axis=-1, keepdims=True)
    shifted = floats - center
    spread = jnp.mean(shifted * shifted, axis=-1, keepdims=True)
    return (shifted * lax.rsqrt(spread + epsilon) * gain).astype(jnp.bfloat16)


def positions_of(stream):
    indices = jnp.arange(stream.shape[0], dtype=jnp.int32)
    boundary = jnp.concatenate([jnp.ones((1,), dtype=bool), stream[1:] != stream[:-1]])
    starting = lax.cummax(jnp.where(boundary, indices, jnp.zeros_like(indices)), axis=0)
    return (indices, starting)


def rotate_leading(vectors, offsets, rotary_dims):
    half_dims = rotary_dims // 2
    frequency = jnp.exp(
        jnp.arange(half_dims, dtype=jnp.float32) * (-2.0 * math.log(rotary_base) / rotary_dims)
    )
    angles = offsets.astype(jnp.float32)[:, None] * frequency[None, :]
    cosine = jnp.cos(angles)
    sine = jnp.sin(angles)
    floats = vectors.astype(jnp.float32)
    leading = floats[..., :half_dims]
    trailing = floats[..., half_dims:rotary_dims]
    rotated = jnp.concatenate(
        [
            leading * cosine - trailing * sine,
            trailing * cosine + leading * sine,
            floats[..., rotary_dims:],
        ],
        axis=-1,
    )
    return rotated.astype(jnp.bfloat16)


def _exchange_kernel(plans, work, extra_in, extra_out, *refs):
    count = len(plans)
    sources, refs = refs[:count], refs[count:]
    inputs, refs = refs[:extra_in], refs[extra_in:]
    outs, refs = refs[:count], refs[count:]
    results, semaphores = refs[:extra_out], refs[extra_out:]
    mesh_ids = pl.DeviceIdType.MESH
    barrier = pltpu.get_barrier_semaphore()
    steps = []
    for number, (axis, n, shared, position, member) in enumerate(plans):
        src_ref, out_ref = sources[number], outs[number]
        local_sem, send_sem, recv_sem = semaphores[3 * number : 3 * number + 3]
        index = lax.axis_index(axis)
        pos = position(index)

        def peer_copy(q, slot, src_ref=src_ref, out_ref=out_ref, send_sem=send_sem,
                      recv_sem=recv_sem, axis=axis, member=member, index=index, shared=shared):
            return pltpu.make_async_remote_copy(
                src_ref=src_ref.at[0] if shared else src_ref.at[q],
                dst_ref=out_ref.at[slot],
                send_sem=send_sem.at[q],
                recv_sem=recv_sem.at[slot],
                device_id={axis: member(index, q)},
                device_id_type=mesh_ids,
            )

        def greet(k, carry, n=n, pos=pos, axis=axis, member=member, index=index):
            q = (pos + k) % n
            pl.semaphore_signal(
                barrier, inc=1, device_id={axis: member(index, q)}, device_id_type=mesh_ids
            )
            return carry

        lax.fori_loop(1, n, greet, 0)
        local = pltpu.make_async_copy(
            src_ref.at[0] if shared else src_ref.at[pos], out_ref.at[pos], local_sem
        )
        steps.append((n, pos, peer_copy, local))
    carried = work[0](*inputs) if work is not None else None
    pl.semaphore_wait(barrier, sum(plan[1] - 1 for plan in plans))

    for n, pos, peer_copy, local in steps:
        local.start()

        def send(k, carry, n=n, pos=pos, peer_copy=peer_copy):
            peer_copy((pos + k) % n, pos).start()
            return carry

        lax.fori_loop(1, n, send, 0)

    if work is not None:
        work[1](carried, *inputs, *results)

    for n, pos, peer_copy, local in steps:

        def finish(k, carry, n=n, pos=pos, peer_copy=peer_copy):
            q = (pos + k) % n
            peer_copy(q, pos).wait_send()
            peer_copy(q, q).wait_recv()
            return carry

        lax.fori_loop(1, n, finish, 0)
        local.wait()


def contiguous(n):
    return (lambda index: index % n, lambda index, q: index - index % n + q)


def plane_group(index):
    return (index // 8) * 2 + index % 2


def plane_member(index, q):
    return ((q // 2) * 4 + (index // 2) % 4) * 2 + q % 2


def token_block(zc, p):
    return ((p // 2) * 4 + zc) * 2 + p % 2


def plane_rows(rows_ref, q, z):
    return rows_ref.at[q // 2, z, q % 2]


def column_group(index):
    return (index // 2) % 4


def column_member(index, q):
    return ((index // 8) * 4 + q) * 2 + index % 2


def exchange_all(collective_id, *requests, work=None, inputs=(), results=()):
    plans, blocks, shapes, scratch = [], [], [], []
    for data, axis, n, shared, group in requests:
        position, member = group if group is not None else contiguous(n)
        plans.append((axis, n, shared, position, member))
        blocks.append(data)
        shapes.append(jax.ShapeDtypeStruct((n,) + data.shape[1:], data.dtype))
        scratch += [
            pltpu.SemaphoreType.DMA,
            pltpu.SemaphoreType.DMA((n,)),
            pltpu.SemaphoreType.DMA((n,)),
        ]
    operands = blocks + list(inputs)
    out_shapes = shapes + list(results)
    return pl.pallas_call(
        functools.partial(_exchange_kernel, tuple(plans), work, len(inputs), len(results)),
        out_shape=tuple(out_shapes),
        in_specs=[pl.BlockSpec(memory_space=pltpu.VMEM)] * len(operands),
        out_specs=tuple(pl.BlockSpec(memory_space=pltpu.VMEM) for _ in out_shapes),
        scratch_shapes=scratch,
        compiler_params=pltpu.CompilerParams(collective_id=collective_id, has_side_effects=True),
    )(*operands)


def exchange(blocks, axis, n, shared, collective_id, group=None):
    return exchange_all(collective_id, (blocks, axis, n, shared, group))[0]


def _feedforward_up(normed_ref, upward_ref, downward_ref):
    upward = jnp.dot(normed_ref[...], upward_ref[...], preferred_element_type=jnp.float32)
    return (0.5 * upward * (1.0 + lax.erf(upward * math.sqrt(0.5)))).astype(jnp.bfloat16)


def _feedforward_down(hidden, normed_ref, upward_ref, downward_ref, out_ref):
    out_ref[...] = jnp.dot(hidden, downward_ref[...], preferred_element_type=jnp.float32)


def _signal(barrier, groups):
    index = lax.axis_index("tensor")
    total = 0
    for n, position, member in groups:
        pos = position(index)

        def greet(k, carry, n=n, pos=pos, member=member):
            pl.semaphore_signal(
                barrier,
                inc=1,
                device_id={"tensor": member(index, (pos + k) % n)},
                device_id_type=pl.DeviceIdType.MESH,
            )
            return carry

        lax.fori_loop(1, n, greet, 0)
        total += n - 1
    return total


def _greet(barrier, groups, extra=0):
    index = lax.axis_index("tensor")
    total = 0
    for n, position, member in groups:
        pos = position(index)

        def greet(k, carry, n=n, pos=pos, member=member):
            pl.semaphore_signal(
                barrier,
                inc=1,
                device_id={"tensor": member(index, (pos + k) % n)},
                device_id_type=pl.DeviceIdType.MESH,
            )
            return carry

        lax.fori_loop(1, n, greet, 0)
        total += n - 1
    pl.semaphore_wait(barrier, total + extra)


def _gather_kernel(n_col, n_y, col, ygroup, slot, x_ref, out_ref, local_sem, col_sem, y_sem, pair_sem,
                   recv_sem):
    index = lax.axis_index("tensor")
    z0, y0, c0 = col[0](index), ygroup[0](index), index % 2
    mesh_ids = pl.DeviceIdType.MESH
    sibling = (2, lambda t: t % 2, lambda t, q: t - t % 2 + q)
    _greet(pltpu.get_barrier_semaphore(), [(n_col, *col), (n_y, *ygroup), sibling])
    partner = index - c0 + 1 - c0

    def block(y, z, c):
        return out_ref.at[slot(y, z, c)]

    def col_copy(q):
        return pltpu.make_async_remote_copy(
            x_ref, block(y0, z0, c0), col_sem.at[q], recv_sem.at[y0, z0, c0],
            device_id={"tensor": col[1](index, q)}, device_id_type=mesh_ids,
        )

    def y_copy(z, q):
        return pltpu.make_async_remote_copy(
            block(y0, z, c0), block(y0, z, c0), y_sem.at[z, q], recv_sem.at[y0, z, c0],
            device_id={"tensor": ygroup[1](index, q)}, device_id_type=mesh_ids,
        )

    def pair_copy(y, z):
        return pltpu.make_async_remote_copy(
            block(y, z, c0), block(y, z, c0), pair_sem.at[y, z], recv_sem.at[y, z, c0],
            device_id={"tensor": partner}, device_id_type=mesh_ids,
        )

    def arrival(y, z, c):
        return pltpu.make_async_remote_copy(
            x_ref, block(y, z, c), col_sem.at[0], recv_sem.at[y, z, c],
            device_id={"tensor": index}, device_id_type=mesh_ids,
        )

    def spread(z):
        def send_y(m, carry):
            y_copy(z, (y0 + m) % n_y).start()
            return carry

        lax.fori_loop(1, n_y, send_y, 0)
        pair_copy(y0, z).start()

    local = pltpu.make_async_copy(x_ref, block(y0, z0, c0), local_sem)
    local.start()

    def send_col(k, carry):
        col_copy((z0 + k) % n_col).start()
        return carry

    lax.fori_loop(1, n_col, send_col, 0)
    local.wait()
    spread(z0)

    def relay_col(k, carry):
        z = (z0 + k) % n_col
        arrival(y0, z, c0).wait_recv()
        spread(z)
        return carry

    lax.fori_loop(1, n_col, relay_col, 0)

    def relay_y(m, carry):
        y = (y0 + m) % n_y

        def each(k, inner):
            z = (z0 + k) % n_col
            arrival(y, z, c0).wait_recv()
            pair_copy(y, z).start()
            return inner

        return lax.fori_loop(0, n_col, each, carry)

    lax.fori_loop(1, n_y, relay_y, 0)

    def finish_col(k, carry):
        col_copy((z0 + k) % n_col).wait_send()
        return carry

    lax.fori_loop(1, n_col, finish_col, 0)

    def finish_y(k, carry):
        z = (z0 + k) % n_col

        def each(m, inner):
            y_copy(z, (y0 + m) % n_y).wait_send()
            return inner

        return lax.fori_loop(1, n_y, each, carry)

    lax.fori_loop(0, n_col, finish_y, 0)

    def finish_pair(m, carry):
        y = (y0 + m) % n_y

        def each(k, inner):
            z = (z0 + k) % n_col
            pair_copy(y, z).wait_send()
            arrival(y, z, 1 - c0).wait_recv()
            return inner

        return lax.fori_loop(0, n_col, each, carry)

    lax.fori_loop(0, n_y, finish_pair, 0)


def gather_tokens(x, col, ygroup, slot, n_col, n_y, collective_id):
    return pl.pallas_call(
        functools.partial(_gather_kernel, n_col, n_y, col, ygroup, slot),
        out_shape=jax.ShapeDtypeStruct((n_col * n_y * 2,) + x.shape, x.dtype),
        in_specs=[pl.BlockSpec(memory_space=pltpu.VMEM)],
        out_specs=pl.BlockSpec(memory_space=pltpu.VMEM),
        scratch_shapes=[
            pltpu.SemaphoreType.DMA,
            pltpu.SemaphoreType.DMA((n_col,)),
            pltpu.SemaphoreType.DMA((n_col, n_y)),
            pltpu.SemaphoreType.DMA((n_y, n_col)),
            pltpu.SemaphoreType.DMA((n_y, n_col, 2)),
        ],
        compiler_params=pltpu.CompilerParams(collective_id=collective_id, has_side_effects=True),
    )(x)


def token_slot(y, z, c):
    return (y * 4 + z) * 2 + c


def _reduce_kernel(n_col, n_y, n_dp, col, ygroup, queries_ref, keys_ref, values_ref, seg_col_ref,
                   seg_row_ref, output_ref, feedforward_ref, x_ref,
                   pages_ref, out_ref, pages_out, rows_ref, inbox0, chip, inbox1, stage, inbox2, sem0,
                   local_sem, send_sem, recv_sem, send2_sem, recv2_sem, page_local_sem, page_send_sem,
                   page_recv_sem):
    index = lax.axis_index("tensor")
    cpos, ypos, core = col[0](index), ygroup[0](index), index % 2
    mesh_ids = pl.DeviceIdType.MESH
    barrier = pltpu.get_barrier_semaphore()
    group = lax.axis_index("dp")

    def page_copy(g, slot):
        return pltpu.make_async_remote_copy(
            pages_ref.at[g], pages_out.at[slot], page_send_sem.at[g], page_recv_sem.at[slot],
            device_id={"dp": g}, device_id_type=mesh_ids,
        )

    def greet_group(k, carry):
        pl.semaphore_signal(
            barrier, inc=1, device_id={"dp": (group + k) % n_dp}, device_id_type=mesh_ids
        )
        return carry

    lax.fori_loop(1, n_dp, greet_group, 0)
    sibling = (2, lambda t: t % 2, lambda t, q: t - t % 2 + q)
    total = _signal(barrier, [sibling, (n_y, *ygroup), (n_col, *col)])

    scores = lax.dot_general(
        queries_ref[...], keys_ref[...], (((1,), (1,)), ((), ())), preferred_element_type=jnp.float32
    ) * (queries_ref.shape[1] ** -0.5)
    shape = scores.shape
    allowed = (seg_col_ref[...] == seg_row_ref[...]) & (
        lax.broadcasted_iota(jnp.int32, shape, 1) <= lax.broadcasted_iota(jnp.int32, shape, 0)
    )
    peak = jnp.max(jnp.where(allowed, scores, -jnp.inf), axis=1, keepdims=True)
    weights = jnp.where(allowed, jnp.exp(scores - peak), 0.0)
    weight_sum = jnp.sum(weights, axis=1, keepdims=True)
    mixed = jnp.dot(weights.astype(jnp.bfloat16), values_ref[...], preferred_element_type=jnp.float32)
    attended = (mixed / weight_sum).astype(jnp.bfloat16)
    product = (
        jnp.dot(attended, output_ref[...], preferred_element_type=jnp.float32)
        + feedforward_ref[...]
    )
    rows = x_ref.shape[0]
    for owner in range(n_y * n_col * 2):
        rows_ref[owner // (2 * n_col), (owner // 2) % n_col, owner % 2] = product[
            owner * rows : (owner + 1) * rows
        ].astype(rows_ref.dtype)
    pl.semaphore_wait(barrier, total + n_dp - 1)
    page_local = pltpu.make_async_copy(pages_ref.at[group], pages_out.at[group], page_local_sem)
    page_local.start()

    def send_pages(k, carry):
        page_copy((group + k) % n_dp, group).start()
        return carry

    lax.fori_loop(1, n_dp, send_pages, 0)

    pair = pltpu.make_async_remote_copy(
        rows_ref.at[:, :, 1 - core], inbox0, sem0.at[0], sem0.at[1],
        device_id={"tensor": index - core + 1 - core}, device_id_type=mesh_ids,
    )
    pair.start()
    pair.wait_send()
    pair.wait_recv()
    for y in range(n_y):
        for z in range(n_col):
            chip[y, z] = (
                rows_ref[y, z, core].astype(jnp.float32) + inbox0[y, z].astype(jnp.float32)
            ).astype(chip.dtype)

    def plane_copy(q, z, slot):
        return pltpu.make_async_remote_copy(
            chip.at[q, z], inbox1.at[z, slot], send_sem.at[z, q], recv_sem.at[z, slot],
            device_id={"tensor": ygroup[1](index, q)}, device_id_type=mesh_ids,
        )

    def col_copy(q, slot):
        return pltpu.make_async_remote_copy(
            stage.at[q], inbox2.at[slot], send2_sem.at[q], recv2_sem.at[slot],
            device_id={"tensor": col[1](index, q)}, device_id_type=mesh_ids,
        )

    order = [(cpos + 1 + k) % n_col for k in range(n_col)]
    locals_ = []
    for z in order:
        local = pltpu.make_async_copy(chip.at[ypos, z], inbox1.at[z, ypos], local_sem.at[z])
        local.start()
        locals_.append(local)

        def send_plane(m, carry, z=z):
            plane_copy((ypos + m) % n_y, z, ypos).start()
            return carry

        lax.fori_loop(1, n_y, send_plane, 0)

    def plane_sum(z, local):
        def arrive(m, carry):
            plane_copy((ypos + m) % n_y, z, (ypos + m) % n_y).wait_recv()
            return carry

        lax.fori_loop(1, n_y, arrive, 0)
        local.wait()
        total = inbox1[z, 0].astype(jnp.float32)
        for sender in range(1, n_y):
            total = total + inbox1[z, sender].astype(jnp.float32)
        return total

    for z, local in zip(order[:-1], locals_[:-1]):
        stage[z] = plane_sum(z, local).astype(stage.dtype)
        col_copy(z, cpos).start()

    result = x_ref[...].astype(jnp.float32) + plane_sum(cpos, locals_[-1])

    def finish_plane(m, carry):
        q = (ypos + m) % n_y
        for z in order:
            plane_copy(q, z, ypos).wait_send()
        return carry

    lax.fori_loop(1, n_y, finish_plane, 0)

    for z in order[:-1]:
        col_copy(z, cpos).wait_send()
        col_copy(z, z).wait_recv()
        result = result + inbox2[z].astype(jnp.float32)
    out_ref[...] = result

    def finish_pages(k, carry):
        g = (group + k) % n_dp
        page_copy(g, group).wait_send()
        page_copy(g, g).wait_recv()
        return carry

    lax.fori_loop(1, n_dp, finish_pages, 0)
    page_local.wait()


def reduce_rows(attention, output_weight, feedforward, x, pages, col, ygroup, n_y, n_col, collective_id):
    block = x.shape
    n_dp = pages.shape[0]
    operands = (*attention, output_weight, feedforward, x, pages)
    return pl.pallas_call(
        functools.partial(_reduce_kernel, n_col, n_y, n_dp, col, ygroup),
        out_shape=(
            jax.ShapeDtypeStruct(block, jnp.float32),
            jax.ShapeDtypeStruct(pages.shape, pages.dtype),
        ),
        in_specs=[pl.BlockSpec(memory_space=pltpu.VMEM)] * len(operands),
        out_specs=(pl.BlockSpec(memory_space=pltpu.VMEM), pl.BlockSpec(memory_space=pltpu.VMEM)),
        scratch_shapes=[
            pltpu.VMEM((n_y, n_col, 2) + block, x.dtype),
            pltpu.VMEM((n_y, n_col) + block, x.dtype),
            pltpu.VMEM((n_y, n_col) + block, x.dtype),
            pltpu.VMEM((n_col, n_y) + block, x.dtype),
            pltpu.VMEM((n_col,) + block, x.dtype),
            pltpu.VMEM((n_col,) + block, x.dtype),
            pltpu.SemaphoreType.DMA((2,)),
            pltpu.SemaphoreType.DMA((n_col,)),
            pltpu.SemaphoreType.DMA((n_col, n_y)),
            pltpu.SemaphoreType.DMA((n_col, n_y)),
            pltpu.SemaphoreType.DMA((n_col,)),
            pltpu.SemaphoreType.DMA((n_col,)),
            pltpu.SemaphoreType.DMA,
            pltpu.SemaphoreType.DMA((n_dp,)),
            pltpu.SemaphoreType.DMA((n_dp,)),
        ],
        compiler_params=pltpu.CompilerParams(collective_id=collective_id, has_side_effects=True),
    )(*operands)


def same_core_group(index):
    return index // 8


def same_core_member(index, q):
    return q * 8 + index % 8


def shards(
    hidden_states,
    attention_gain,
    feedforward_gain,
    heads_weight,
    output_weight,
    upward_weight,
    downward_weight,
    segments,
    page_targets,
):
    tensor_count = lax.axis_size("tensor")
    replica_count = lax.axis_size("dp")
    tensor_index = lax.axis_index("tensor")
    quarters = tensor_count // H
    quarter_width = HD // quarters
    quarter_index = tensor_index % quarters
    stream = segments[0]
    tokens_total = stream.shape[0]
    local_rows = hidden_states.shape[0]

    width = hidden_states.shape[1]
    planes = tensor_count // 8
    gathered = gather_tokens(
        hidden_states,
        (column_group, column_member),
        (same_core_group, same_core_member),
        token_slot,
        planes,
        4,
        0,
    )
    tokens = gathered.reshape(tokens_total, width)
    normed_attention = layer_norm(tokens, attention_gain)
    normed_feedforward = layer_norm(tokens, feedforward_gain)
    joined = jnp.dot(normed_attention, heads_weight, preferred_element_type=jnp.float32).astype(
        jnp.bfloat16
    )

    indices, starting = positions_of(stream)
    offsets = indices - starting
    query_piece = joined[:, :quarter_width]
    key_piece = joined[:, quarter_width : 2 * quarter_width]
    value_piece = joined[:, 2 * quarter_width :]
    leading = quarter_index == 0
    query_piece = jnp.where(leading, rotate_leading(query_piece, offsets, ROT), query_piece)
    key_piece = jnp.where(leading, rotate_leading(key_piece, offsets, ROT), key_piece)

    page_count = tokens_total // PAGE
    page_rows = jnp.concatenate([key_piece, value_piece], 1).reshape(
        page_count, PAGE * 2 * quarter_width
    )
    targets = page_targets[:, 0]
    page_numbers = jnp.arange(page_count, dtype=jnp.int32)
    earlier = jnp.sum(
        (
            (targets[None, :] == targets[:, None]) & (page_numbers[None, :] < page_numbers[:, None])
        ).astype(jnp.int32),
        axis=1,
    )
    capacity = 2 * page_count // replica_count
    slot_numbers = targets * capacity + earlier
    placing = (
        jnp.arange(replica_count * capacity, dtype=jnp.int32)[:, None] == slot_numbers[None, :]
    ).astype(jnp.bfloat16)
    outgoing = jnp.dot(placing, page_rows, preferred_element_type=jnp.float32).astype(jnp.bfloat16)
    outgoing = outgoing.reshape(replica_count, capacity * PAGE, 2 * quarter_width)
    head_pieces, feedforward = exchange_all(
        1,
        (jnp.concatenate([query_piece, key_piece], 1)[None], "tensor", quarters, True, None),
        work=(_feedforward_up, _feedforward_down),
        inputs=(normed_feedforward, upward_weight, downward_weight),
        results=(jax.ShapeDtypeStruct((tokens_total, width), jnp.float32),),
    )
    queries = head_pieces[:, :, :quarter_width].transpose(1, 0, 2).reshape(tokens_total, HD)
    keys = head_pieces[:, :, quarter_width:].transpose(1, 0, 2).reshape(tokens_total, HD)

    layer_output, incoming = reduce_rows(
        (queries, keys, value_piece, stream[:, None], stream[None, :]),
        output_weight,
        feedforward,
        hidden_states,
        outgoing,
        (column_group, column_member),
        (same_core_group, same_core_member),
        4,
        planes,
        2,
    )

    cache_pages = incoming.reshape(1, replica_count, capacity, PAGE, 2 * quarter_width)
    return (layer_output, cache_pages)


def solution(mesh):
    in_specs = (
        P(("dp", "tensor"), None),
        P(),
        P(),
        P(None, "tensor"),
        P("tensor", None),
        P(None, "tensor"),
        P("tensor", None),
        P("dp", None),
        P("dp", None),
    )
    out_specs = (P(("dp", "tensor"), None), P("dp", None, None, None, "tensor"))
    return jax.shard_map(shards, mesh=mesh, in_specs=in_specs, out_specs=out_specs, check_vma=False)
```

```python
import functools
import math

import jax
import jax.numpy as jnp
from jax import lax
from jax.experimental import pallas as pl
from jax.experimental.pallas import tpu as pltpu
from jax.sharding import PartitionSpec as P

H = 8
HD = 256
ROT = 64
PAGE = 16


epsilon = 1e-05
rotary_base = 10000.0


def layer_norm(values, gain):
    floats = values.astype(jnp.float32)
    center = jnp.mean(floats, axis=-1, keepdims=True)
    shifted = floats - center
    spread = jnp.mean(shifted * shifted, axis=-1, keepdims=True)
    return (shifted * lax.rsqrt(spread + epsilon) * gain).astype(jnp.bfloat16)


def positions_of(stream):
    indices = jnp.arange(stream.shape[0], dtype=jnp.int32)
    boundary = jnp.concatenate([jnp.ones((1,), dtype=bool), stream[1:] != stream[:-1]])
    starting = lax.cummax(jnp.where(boundary, indices, jnp.zeros_like(indices)), axis=0)
    return (indices, starting)


def rotate_leading(vectors, offsets, rotary_dims):
    half_dims = rotary_dims // 2
    frequency = jnp.exp(
        jnp.arange(half_dims, dtype=jnp.float32) * (-2.0 * math.log(rotary_base) / rotary_dims)
    )
    angles = offsets.astype(jnp.float32)[:, None] * frequency[None, :]
    cosine = jnp.cos(angles)
    sine = jnp.sin(angles)
    floats = vectors.astype(jnp.float32)
    leading = floats[..., :half_dims]
    trailing = floats[..., half_dims:rotary_dims]
    rotated = jnp.concatenate(
        [
            leading * cosine - trailing * sine,
            trailing * cosine + leading * sine,
            floats[..., rotary_dims:],
        ],
        axis=-1,
    )
    return rotated.astype(jnp.bfloat16)


def _exchange_kernel(plans, work, extra_in, extra_out, *refs):
    count = len(plans)
    sources, refs = refs[:count], refs[count:]
    inputs, refs = refs[:extra_in], refs[extra_in:]
    outs, refs = refs[:count], refs[count:]
    results, semaphores = refs[:extra_out], refs[extra_out:]
    mesh_ids = pl.DeviceIdType.MESH
    barrier = pltpu.get_barrier_semaphore()
    steps = []
    for number, (axis, n, shared, position, member) in enumerate(plans):
        src_ref, out_ref = sources[number], outs[number]
        local_sem, send_sem, recv_sem = semaphores[3 * number : 3 * number + 3]
        index = lax.axis_index(axis)
        pos = position(index)

        def peer_copy(q, slot, src_ref=src_ref, out_ref=out_ref, send_sem=send_sem,
                      recv_sem=recv_sem, axis=axis, member=member, index=index, shared=shared):
            return pltpu.make_async_remote_copy(
                src_ref=src_ref.at[0] if shared else src_ref.at[q],
                dst_ref=out_ref.at[slot],
                send_sem=send_sem.at[q],
                recv_sem=recv_sem.at[slot],
                device_id={axis: member(index, q)},
                device_id_type=mesh_ids,
            )

        def greet(k, carry, n=n, pos=pos, axis=axis, member=member, index=index):
            q = (pos + k) % n
            pl.semaphore_signal(
                barrier, inc=1, device_id={axis: member(index, q)}, device_id_type=mesh_ids
            )
            return carry

        lax.fori_loop(1, n, greet, 0)
        local = pltpu.make_async_copy(
            src_ref.at[0] if shared else src_ref.at[pos], out_ref.at[pos], local_sem
        )
        steps.append((n, pos, peer_copy, local))
    carried = work[0](*inputs) if work is not None else None
    pl.semaphore_wait(barrier, sum(plan[1] - 1 for plan in plans))

    for n, pos, peer_copy, local in steps:
        local.start()

        def send(k, carry, n=n, pos=pos, peer_copy=peer_copy):
            peer_copy((pos + k) % n, pos).start()
            return carry

        lax.fori_loop(1, n, send, 0)

    if work is not None:
        work[1](carried, *inputs, *results)

    for n, pos, peer_copy, local in steps:

        def finish(k, carry, n=n, pos=pos, peer_copy=peer_copy):
            q = (pos + k) % n
            peer_copy(q, pos).wait_send()
            peer_copy(q, q).wait_recv()
            return carry

        lax.fori_loop(1, n, finish, 0)
        local.wait()


def contiguous(n):
    return (lambda index: index % n, lambda index, q: index - index % n + q)


def plane_group(index):
    return (index // 8) * 2 + index % 2


def plane_member(index, q):
    return ((q // 2) * 4 + (index // 2) % 4) * 2 + q % 2


def token_block(zc, p):
    return ((p // 2) * 4 + zc) * 2 + p % 2


def plane_rows(rows_ref, q, z):
    return rows_ref.at[q // 2, z, q % 2]


def column_group(index):
    return (index // 2) % 4


def column_member(index, q):
    return ((index // 8) * 4 + q) * 2 + index % 2


def exchange_all(collective_id, *requests, work=None, inputs=(), results=()):
    plans, blocks, shapes, scratch = [], [], [], []
    for data, axis, n, shared, group in requests:
        position, member = group if group is not None else contiguous(n)
        plans.append((axis, n, shared, position, member))
        blocks.append(data)
        shapes.append(jax.ShapeDtypeStruct((n,) + data.shape[1:], data.dtype))
        scratch += [
            pltpu.SemaphoreType.DMA,
            pltpu.SemaphoreType.DMA((n,)),
            pltpu.SemaphoreType.DMA((n,)),
        ]
    operands = blocks + list(inputs)
    out_shapes = shapes + list(results)
    return pl.pallas_call(
        functools.partial(_exchange_kernel, tuple(plans), work, len(inputs), len(results)),
        out_shape=tuple(out_shapes),
        in_specs=[pl.BlockSpec(memory_space=pltpu.VMEM)] * len(operands),
        out_specs=tuple(pl.BlockSpec(memory_space=pltpu.VMEM) for _ in out_shapes),
        scratch_shapes=scratch,
        compiler_params=pltpu.CompilerParams(collective_id=collective_id, has_side_effects=True),
    )(*operands)


def exchange(blocks, axis, n, shared, collective_id, group=None):
    return exchange_all(collective_id, (blocks, axis, n, shared, group))[0]


def _feedforward_up(normed_ref, upward_ref, downward_ref):
    upward = jnp.dot(normed_ref[...], upward_ref[...], preferred_element_type=jnp.float32)
    return (0.5 * upward * (1.0 + lax.erf(upward * math.sqrt(0.5)))).astype(jnp.bfloat16)


def _feedforward_down(hidden, normed_ref, upward_ref, downward_ref, out_ref):
    out_ref[...] = jnp.dot(hidden, downward_ref[...], preferred_element_type=jnp.float32)


def _signal(barrier, groups):
    index = lax.axis_index("tensor")
    total = 0
    for n, position, member in groups:
        pos = position(index)

        def greet(k, carry, n=n, pos=pos, member=member):
            pl.semaphore_signal(
                barrier,
                inc=1,
                device_id={"tensor": member(index, (pos + k) % n)},
                device_id_type=pl.DeviceIdType.MESH,
            )
            return carry

        lax.fori_loop(1, n, greet, 0)
        total += n - 1
    return total


def _greet(barrier, groups, extra=0):
    index = lax.axis_index("tensor")
    total = 0
    for n, position, member in groups:
        pos = position(index)

        def greet(k, carry, n=n, pos=pos, member=member):
            pl.semaphore_signal(
                barrier,
                inc=1,
                device_id={"tensor": member(index, (pos + k) % n)},
                device_id_type=pl.DeviceIdType.MESH,
            )
            return carry

        lax.fori_loop(1, n, greet, 0)
        total += n - 1
    pl.semaphore_wait(barrier, total + extra)


def _gather_kernel(n_col, n_y, col, ygroup, slot, x_ref, out_ref, local_sem, col_sem, y_sem, pair_sem,
                   recv_sem):
    index = lax.axis_index("tensor")
    z0, y0, c0 = col[0](index), ygroup[0](index), index % 2
    mesh_ids = pl.DeviceIdType.MESH
    sibling = (2, lambda t: t % 2, lambda t, q: t - t % 2 + q)
    _greet(pltpu.get_barrier_semaphore(), [(n_col, *col), (n_y, *ygroup), sibling])
    partner = index - c0 + 1 - c0

    def block(y, z, c):
        return out_ref.at[slot(y, z, c)]

    def col_copy(q):
        return pltpu.make_async_remote_copy(
            x_ref, block(y0, z0, c0), col_sem.at[q], recv_sem.at[y0, z0, c0],
            device_id={"tensor": col[1](index, q)}, device_id_type=mesh_ids,
        )

    def y_copy(z, q):
        return pltpu.make_async_remote_copy(
            block(y0, z, c0), block(y0, z, c0), y_sem.at[z, q], recv_sem.at[y0, z, c0],
            device_id={"tensor": ygroup[1](index, q)}, device_id_type=mesh_ids,
        )

    def pair_copy(y, z):
        return pltpu.make_async_remote_copy(
            block(y, z, c0), block(y, z, c0), pair_sem.at[y, z], recv_sem.at[y, z, c0],
            device_id={"tensor": partner}, device_id_type=mesh_ids,
        )

    def arrival(y, z, c):
        return pltpu.make_async_remote_copy(
            x_ref, block(y, z, c), col_sem.at[0], recv_sem.at[y, z, c],
            device_id={"tensor": index}, device_id_type=mesh_ids,
        )

    def spread(z):
        def send_y(m, carry):
            y_copy(z, (y0 + m) % n_y).start()
            return carry

        lax.fori_loop(1, n_y, send_y, 0)
        pair_copy(y0, z).start()

    local = pltpu.make_async_copy(x_ref, block(y0, z0, c0), local_sem)
    local.start()

    def send_col(k, carry):
        col_copy((z0 + k) % n_col).start()
        return carry

    lax.fori_loop(1, n_col, send_col, 0)
    local.wait()
    spread(z0)

    def relay_col(k, carry):
        z = (z0 + k) % n_col
        arrival(y0, z, c0).wait_recv()
        spread(z)
        return carry

    lax.fori_loop(1, n_col, relay_col, 0)

    def relay_y(m, carry):
        y = (y0 + m) % n_y

        def each(k, inner):
            z = (z0 + k) % n_col
            arrival(y, z, c0).wait_recv()
            pair_copy(y, z).start()
            return inner

        return lax.fori_loop(0, n_col, each, carry)

    lax.fori_loop(1, n_y, relay_y, 0)

    def finish_col(k, carry):
        col_copy((z0 + k) % n_col).wait_send()
        return carry

    lax.fori_loop(1, n_col, finish_col, 0)

    def finish_y(k, carry):
        z = (z0 + k) % n_col

        def each(m, inner):
            y_copy(z, (y0 + m) % n_y).wait_send()
            return inner

        return lax.fori_loop(1, n_y, each, carry)

    lax.fori_loop(0, n_col, finish_y, 0)

    def finish_pair(m, carry):
        y = (y0 + m) % n_y

        def each(k, inner):
            z = (z0 + k) % n_col
            pair_copy(y, z).wait_send()
            arrival(y, z, 1 - c0).wait_recv()
            return inner

        return lax.fori_loop(0, n_col, each, carry)

    lax.fori_loop(0, n_y, finish_pair, 0)


def gather_tokens(x, col, ygroup, slot, n_col, n_y, collective_id):
    return pl.pallas_call(
        functools.partial(_gather_kernel, n_col, n_y, col, ygroup, slot),
        out_shape=jax.ShapeDtypeStruct((n_col * n_y * 2,) + x.shape, x.dtype),
        in_specs=[pl.BlockSpec(memory_space=pltpu.VMEM)],
        out_specs=pl.BlockSpec(memory_space=pltpu.VMEM),
        scratch_shapes=[
            pltpu.SemaphoreType.DMA,
            pltpu.SemaphoreType.DMA((n_col,)),
            pltpu.SemaphoreType.DMA((n_col, n_y)),
            pltpu.SemaphoreType.DMA((n_y, n_col)),
            pltpu.SemaphoreType.DMA((n_y, n_col, 2)),
        ],
        compiler_params=pltpu.CompilerParams(collective_id=collective_id, has_side_effects=True),
    )(x)


def token_slot(y, z, c):
    return (y * 4 + z) * 2 + c


def _reduce_kernel(n_col, n_y, n_dp, col, ygroup, pieces_ref, values_ref, seg_col_ref,
                   seg_row_ref, output_ref, feedforward_ref, x_ref,
                   pages_ref, out_ref, pages_out, rows_ref, inbox0, chip, inbox1, stage, inbox2, sem0,
                   local_sem, send_sem, recv_sem, send2_sem, recv2_sem, page_local_sem, page_send_sem,
                   page_recv_sem):
    index = lax.axis_index("tensor")
    cpos, ypos, core = col[0](index), ygroup[0](index), index % 2
    mesh_ids = pl.DeviceIdType.MESH
    barrier = pltpu.get_barrier_semaphore()
    group = lax.axis_index("dp")

    def page_copy(g, slot):
        return pltpu.make_async_remote_copy(
            pages_ref.at[g], pages_out.at[slot], page_send_sem.at[g], page_recv_sem.at[slot],
            device_id={"dp": g}, device_id_type=mesh_ids,
        )

    def greet_group(k, carry):
        pl.semaphore_signal(
            barrier, inc=1, device_id={"dp": (group + k) % n_dp}, device_id_type=mesh_ids
        )
        return carry

    lax.fori_loop(1, n_dp, greet_group, 0)
    sibling = (2, lambda t: t % 2, lambda t, q: t - t % 2 + q)
    total = _signal(barrier, [sibling, (n_y, *ygroup), (n_col, *col)])

    quarter_count, head_dims = pieces_ref.shape[0], pieces_ref.shape[0] * pieces_ref.shape[3]
    scores = lax.dot_general(
        pieces_ref[0, 0], pieces_ref[0, 1], (((1,), (1,)), ((), ())), preferred_element_type=jnp.float32
    )
    for quarter in range(1, quarter_count):
        scores = scores + lax.dot_general(
            pieces_ref[quarter, 0], pieces_ref[quarter, 1], (((1,), (1,)), ((), ())),
            preferred_element_type=jnp.float32,
        )
    scores = scores * (head_dims ** -0.5)
    shape = scores.shape
    allowed = (seg_col_ref[...] == seg_row_ref[...]) & (
        lax.broadcasted_iota(jnp.int32, shape, 1) <= lax.broadcasted_iota(jnp.int32, shape, 0)
    )
    peak = jnp.max(jnp.where(allowed, scores, -jnp.inf), axis=1, keepdims=True)
    weights = jnp.where(allowed, jnp.exp(scores - peak), 0.0)
    weight_sum = jnp.sum(weights, axis=1, keepdims=True)
    mixed = jnp.dot(weights.astype(jnp.bfloat16), values_ref[...], preferred_element_type=jnp.float32)
    attended = (mixed / weight_sum).astype(jnp.bfloat16)
    product = (
        jnp.dot(attended, output_ref[...], preferred_element_type=jnp.float32)
        + feedforward_ref[...]
    )
    rows = x_ref.shape[0]
    for owner in range(n_y * n_col * 2):
        rows_ref[owner // (2 * n_col), (owner // 2) % n_col, owner % 2] = product[
            owner * rows : (owner + 1) * rows
        ].astype(rows_ref.dtype)
    pl.semaphore_wait(barrier, total + n_dp - 1)
    page_local = pltpu.make_async_copy(pages_ref.at[group], pages_out.at[group], page_local_sem)
    page_local.start()

    def send_pages(k, carry):
        page_copy((group + k) % n_dp, group).start()
        return carry

    lax.fori_loop(1, n_dp, send_pages, 0)

    pair = pltpu.make_async_remote_copy(
        rows_ref.at[:, :, 1 - core], inbox0, sem0.at[0], sem0.at[1],
        device_id={"tensor": index - core + 1 - core}, device_id_type=mesh_ids,
    )
    pair.start()
    pair.wait_send()
    pair.wait_recv()
    for y in range(n_y):
        for z in range(n_col):
            chip[y, z] = (
                rows_ref[y, z, core].astype(jnp.float32) + inbox0[y, z].astype(jnp.float32)
            ).astype(chip.dtype)

    def plane_copy(q, z, slot):
        return pltpu.make_async_remote_copy(
            chip.at[q, z], inbox1.at[z, slot], send_sem.at[z, q], recv_sem.at[z, slot],
            device_id={"tensor": ygroup[1](index, q)}, device_id_type=mesh_ids,
        )

    def col_copy(q, slot):
        return pltpu.make_async_remote_copy(
            stage.at[q], inbox2.at[slot], send2_sem.at[q], recv2_sem.at[slot],
            device_id={"tensor": col[1](index, q)}, device_id_type=mesh_ids,
        )

    order = [(cpos + 1 + k) % n_col for k in range(n_col)]
    locals_ = []
    for z in order:
        local = pltpu.make_async_copy(chip.at[ypos, z], inbox1.at[z, ypos], local_sem.at[z])
        local.start()
        locals_.append(local)

        def send_plane(m, carry, z=z):
            plane_copy((ypos + m) % n_y, z, ypos).start()
            return carry

        lax.fori_loop(1, n_y, send_plane, 0)

    def plane_sum(z, local):
        def arrive(m, carry):
            plane_copy((ypos + m) % n_y, z, (ypos + m) % n_y).wait_recv()
            return carry

        lax.fori_loop(1, n_y, arrive, 0)
        local.wait()
        total = inbox1[z, 0].astype(jnp.float32)
        for sender in range(1, n_y):
            total = total + inbox1[z, sender].astype(jnp.float32)
        return total

    for z, local in zip(order[:-1], locals_[:-1]):
        stage[z] = plane_sum(z, local).astype(stage.dtype)
        col_copy(z, cpos).start()

    result = x_ref[...].astype(jnp.float32) + plane_sum(cpos, locals_[-1])

    def finish_plane(m, carry):
        q = (ypos + m) % n_y
        for z in order:
            plane_copy(q, z, ypos).wait_send()
        return carry

    lax.fori_loop(1, n_y, finish_plane, 0)

    for z in order[:-1]:
        col_copy(z, cpos).wait_send()
        col_copy(z, z).wait_recv()
        result = result + inbox2[z].astype(jnp.float32)
    out_ref[...] = result

    def finish_pages(k, carry):
        g = (group + k) % n_dp
        page_copy(g, group).wait_send()
        page_copy(g, g).wait_recv()
        return carry

    lax.fori_loop(1, n_dp, finish_pages, 0)
    page_local.wait()


def reduce_rows(attention, output_weight, feedforward, x, pages, col, ygroup, n_y, n_col, collective_id):
    block = x.shape
    n_dp = pages.shape[0]
    operands = (*attention, output_weight, feedforward, x, pages)
    return pl.pallas_call(
        functools.partial(_reduce_kernel, n_col, n_y, n_dp, col, ygroup),
        out_shape=(
            jax.ShapeDtypeStruct(block, jnp.float32),
            jax.ShapeDtypeStruct(pages.shape, pages.dtype),
        ),
        in_specs=[pl.BlockSpec(memory_space=pltpu.VMEM)] * len(operands),
        out_specs=(pl.BlockSpec(memory_space=pltpu.VMEM), pl.BlockSpec(memory_space=pltpu.VMEM)),
        scratch_shapes=[
            pltpu.VMEM((n_y, n_col, 2) + block, x.dtype),
            pltpu.VMEM((n_y, n_col) + block, x.dtype),
            pltpu.VMEM((n_y, n_col) + block, x.dtype),
            pltpu.VMEM((n_col, n_y) + block, x.dtype),
            pltpu.VMEM((n_col,) + block, x.dtype),
            pltpu.VMEM((n_col,) + block, x.dtype),
            pltpu.SemaphoreType.DMA((2,)),
            pltpu.SemaphoreType.DMA((n_col,)),
            pltpu.SemaphoreType.DMA((n_col, n_y)),
            pltpu.SemaphoreType.DMA((n_col, n_y)),
            pltpu.SemaphoreType.DMA((n_col,)),
            pltpu.SemaphoreType.DMA((n_col,)),
            pltpu.SemaphoreType.DMA,
            pltpu.SemaphoreType.DMA((n_dp,)),
            pltpu.SemaphoreType.DMA((n_dp,)),
        ],
        compiler_params=pltpu.CompilerParams(collective_id=collective_id, has_side_effects=True),
    )(*operands)


def same_core_group(index):
    return index // 8


def same_core_member(index, q):
    return q * 8 + index % 8


def shards(
    hidden_states,
    attention_gain,
    feedforward_gain,
    heads_weight,
    output_weight,
    upward_weight,
    downward_weight,
    segments,
    page_targets,
):
    tensor_count = lax.axis_size("tensor")
    replica_count = lax.axis_size("dp")
    tensor_index = lax.axis_index("tensor")
    quarters = tensor_count // H
    quarter_width = HD // quarters
    quarter_index = tensor_index % quarters
    stream = segments[0]
    tokens_total = stream.shape[0]
    local_rows = hidden_states.shape[0]

    width = hidden_states.shape[1]
    planes = tensor_count // 8
    gathered = gather_tokens(
        hidden_states,
        (column_group, column_member),
        (same_core_group, same_core_member),
        token_slot,
        planes,
        4,
        0,
    )
    tokens = gathered.reshape(tokens_total, width)
    normed_attention = layer_norm(tokens, attention_gain)
    normed_feedforward = layer_norm(tokens, feedforward_gain)
    joined = jnp.dot(normed_attention, heads_weight, preferred_element_type=jnp.float32).astype(
        jnp.bfloat16
    )

    indices, starting = positions_of(stream)
    offsets = indices - starting
    query_piece = joined[:, :quarter_width]
    key_piece = joined[:, quarter_width : 2 * quarter_width]
    value_piece = joined[:, 2 * quarter_width :]
    leading = quarter_index == 0
    query_piece = jnp.where(leading, rotate_leading(query_piece, offsets, ROT), query_piece)
    key_piece = jnp.where(leading, rotate_leading(key_piece, offsets, ROT), key_piece)

    page_count = tokens_total // PAGE
    page_rows = jnp.concatenate([key_piece, value_piece], 1).reshape(
        page_count, PAGE * 2 * quarter_width
    )
    targets = page_targets[:, 0]
    page_numbers = jnp.arange(page_count, dtype=jnp.int32)
    earlier = jnp.sum(
        (
            (targets[None, :] == targets[:, None]) & (page_numbers[None, :] < page_numbers[:, None])
        ).astype(jnp.int32),
        axis=1,
    )
    capacity = 2 * page_count // replica_count
    slot_numbers = targets * capacity + earlier
    placing = (
        jnp.arange(replica_count * capacity, dtype=jnp.int32)[:, None] == slot_numbers[None, :]
    ).astype(jnp.bfloat16)
    outgoing = jnp.dot(placing, page_rows, preferred_element_type=jnp.float32).astype(jnp.bfloat16)
    outgoing = outgoing.reshape(replica_count, capacity * PAGE, 2 * quarter_width)
    head_pieces, feedforward = exchange_all(
        1,
        (jnp.stack([query_piece, key_piece])[None], "tensor", quarters, True, None),
        work=(_feedforward_up, _feedforward_down),
        inputs=(normed_feedforward, upward_weight, downward_weight),
        results=(jax.ShapeDtypeStruct((tokens_total, width), jnp.float32),),
    )

    layer_output, incoming = reduce_rows(
        (head_pieces, value_piece, stream[:, None], stream[None, :]),
        output_weight,
        feedforward,
        hidden_states,
        outgoing,
        (column_group, column_member),
        (same_core_group, same_core_member),
        4,
        planes,
        2,
    )

    cache_pages = incoming.reshape(1, replica_count, capacity, PAGE, 2 * quarter_width)
    return (layer_output, cache_pages)


def solution(mesh):
    in_specs = (
        P(("dp", "tensor"), None),
        P(),
        P(),
        P(None, "tensor"),
        P("tensor", None),
        P(None, "tensor"),
        P("tensor", None),
        P("dp", None),
        P("dp", None),
    )
    out_specs = (P(("dp", "tensor"), None), P("dp", None, None, None, "tensor"))
    return jax.shard_map(shards, mesh=mesh, in_specs=in_specs, out_specs=out_specs, check_vma=False)
```

```python
import functools
import math

import jax
import jax.numpy as jnp
from jax import lax
from jax.experimental import pallas as pl
from jax.experimental.pallas import tpu as pltpu
from jax.sharding import PartitionSpec as P

H = 8
HD = 256
ROT = 64
PAGE = 16


epsilon = 1e-05
rotary_base = 10000.0


def layer_norm(values, gain):
    floats = values.astype(jnp.float32)
    center = jnp.mean(floats, axis=-1, keepdims=True)
    shifted = floats - center
    spread = jnp.mean(shifted * shifted, axis=-1, keepdims=True)
    return (shifted * lax.rsqrt(spread + epsilon) * gain).astype(jnp.bfloat16)


def positions_of(stream):
    indices = jnp.arange(stream.shape[0], dtype=jnp.int32)
    boundary = jnp.concatenate([jnp.ones((1,), dtype=bool), stream[1:] != stream[:-1]])
    starting = lax.cummax(jnp.where(boundary, indices, jnp.zeros_like(indices)), axis=0)
    return (indices, starting)


def rotate_leading(vectors, offsets, rotary_dims):
    half_dims = rotary_dims // 2
    frequency = jnp.exp(
        jnp.arange(half_dims, dtype=jnp.float32) * (-2.0 * math.log(rotary_base) / rotary_dims)
    )
    angles = offsets.astype(jnp.float32)[:, None] * frequency[None, :]
    cosine = jnp.cos(angles)
    sine = jnp.sin(angles)
    floats = vectors.astype(jnp.float32)
    leading = floats[..., :half_dims]
    trailing = floats[..., half_dims:rotary_dims]
    rotated = jnp.concatenate(
        [
            leading * cosine - trailing * sine,
            trailing * cosine + leading * sine,
            floats[..., rotary_dims:],
        ],
        axis=-1,
    )
    return rotated.astype(jnp.bfloat16)


def _exchange_kernel(plans, work, extra_in, extra_out, *refs):
    count = len(plans)
    sources, refs = refs[:count], refs[count:]
    inputs, refs = refs[:extra_in], refs[extra_in:]
    outs, refs = refs[:count], refs[count:]
    results, semaphores = refs[:extra_out], refs[extra_out:]
    mesh_ids = pl.DeviceIdType.MESH
    barrier = pltpu.get_barrier_semaphore()
    steps = []
    for number, (axis, n, shared, position, member) in enumerate(plans):
        src_ref, out_ref = sources[number], outs[number]
        local_sem, send_sem, recv_sem = semaphores[3 * number : 3 * number + 3]
        index = lax.axis_index(axis)
        pos = position(index)

        def peer_copy(q, slot, src_ref=src_ref, out_ref=out_ref, send_sem=send_sem,
                      recv_sem=recv_sem, axis=axis, member=member, index=index, shared=shared):
            return pltpu.make_async_remote_copy(
                src_ref=src_ref.at[0] if shared else src_ref.at[q],
                dst_ref=out_ref.at[slot],
                send_sem=send_sem.at[q],
                recv_sem=recv_sem.at[slot],
                device_id={axis: member(index, q)},
                device_id_type=mesh_ids,
            )

        def greet(k, carry, n=n, pos=pos, axis=axis, member=member, index=index):
            q = (pos + k) % n
            pl.semaphore_signal(
                barrier, inc=1, device_id={axis: member(index, q)}, device_id_type=mesh_ids
            )
            return carry

        lax.fori_loop(1, n, greet, 0)
        local = pltpu.make_async_copy(
            src_ref.at[0] if shared else src_ref.at[pos], out_ref.at[pos], local_sem
        )
        steps.append((n, pos, peer_copy, local))
    carried = work[0](*inputs) if work is not None else None
    pl.semaphore_wait(barrier, sum(plan[1] - 1 for plan in plans))

    for n, pos, peer_copy, local in steps:
        local.start()

        def send(k, carry, n=n, pos=pos, peer_copy=peer_copy):
            peer_copy((pos + k) % n, pos).start()
            return carry

        lax.fori_loop(1, n, send, 0)

    if work is not None:
        work[1](carried, *inputs, *results)

    for n, pos, peer_copy, local in steps:

        def finish(k, carry, n=n, pos=pos, peer_copy=peer_copy):
            q = (pos + k) % n
            peer_copy(q, pos).wait_send()
            peer_copy(q, q).wait_recv()
            return carry

        lax.fori_loop(1, n, finish, 0)
        local.wait()


def contiguous(n):
    return (lambda index: index % n, lambda index, q: index - index % n + q)


def plane_group(index):
    return (index // 8) * 2 + index % 2


def plane_member(index, q):
    return ((q // 2) * 4 + (index // 2) % 4) * 2 + q % 2


def token_block(zc, p):
    return ((p // 2) * 4 + zc) * 2 + p % 2


def plane_rows(rows_ref, q, z):
    return rows_ref.at[q // 2, z, q % 2]


def column_group(index):
    return (index // 2) % 4


def column_member(index, q):
    return ((index // 8) * 4 + q) * 2 + index % 2


def exchange_all(collective_id, *requests, work=None, inputs=(), results=()):
    plans, blocks, shapes, scratch = [], [], [], []
    for data, axis, n, shared, group in requests:
        position, member = group if group is not None else contiguous(n)
        plans.append((axis, n, shared, position, member))
        blocks.append(data)
        shapes.append(jax.ShapeDtypeStruct((n,) + data.shape[1:], data.dtype))
        scratch += [
            pltpu.SemaphoreType.DMA,
            pltpu.SemaphoreType.DMA((n,)),
            pltpu.SemaphoreType.DMA((n,)),
        ]
    operands = blocks + list(inputs)
    out_shapes = shapes + list(results)
    return pl.pallas_call(
        functools.partial(_exchange_kernel, tuple(plans), work, len(inputs), len(results)),
        out_shape=tuple(out_shapes),
        in_specs=[pl.BlockSpec(memory_space=pltpu.VMEM)] * len(operands),
        out_specs=tuple(pl.BlockSpec(memory_space=pltpu.VMEM) for _ in out_shapes),
        scratch_shapes=scratch,
        compiler_params=pltpu.CompilerParams(collective_id=collective_id, has_side_effects=True),
    )(*operands)


def exchange(blocks, axis, n, shared, collective_id, group=None):
    return exchange_all(collective_id, (blocks, axis, n, shared, group))[0]


def _feedforward_up(normed_ref, upward_ref, downward_ref):
    upward = jnp.dot(normed_ref[...], upward_ref[...], preferred_element_type=jnp.float32)
    return (0.5 * upward * (1.0 + lax.erf(upward * math.sqrt(0.5)))).astype(jnp.bfloat16)


def _feedforward_down(hidden, normed_ref, upward_ref, downward_ref, out_ref):
    out_ref[...] = jnp.dot(hidden, downward_ref[...], preferred_element_type=jnp.float32)


def _signal(barrier, groups):
    index = lax.axis_index("tensor")
    total = 0
    for n, position, member in groups:
        pos = position(index)

        def greet(k, carry, n=n, pos=pos, member=member):
            pl.semaphore_signal(
                barrier,
                inc=1,
                device_id={"tensor": member(index, (pos + k) % n)},
                device_id_type=pl.DeviceIdType.MESH,
            )
            return carry

        lax.fori_loop(1, n, greet, 0)
        total += n - 1
    return total


def _greet(barrier, groups, extra=0):
    index = lax.axis_index("tensor")
    total = 0
    for n, position, member in groups:
        pos = position(index)

        def greet(k, carry, n=n, pos=pos, member=member):
            pl.semaphore_signal(
                barrier,
                inc=1,
                device_id={"tensor": member(index, (pos + k) % n)},
                device_id_type=pl.DeviceIdType.MESH,
            )
            return carry

        lax.fori_loop(1, n, greet, 0)
        total += n - 1
    pl.semaphore_wait(barrier, total + extra)


def _gather_kernel(n_col, n_y, col, ygroup, slot, x_ref, out_ref, local_sem, col_sem, y_sem, pair_sem,
                   recv_sem):
    index = lax.axis_index("tensor")
    z0, y0, c0 = col[0](index), ygroup[0](index), index % 2
    mesh_ids = pl.DeviceIdType.MESH
    sibling = (2, lambda t: t % 2, lambda t, q: t - t % 2 + q)
    _greet(pltpu.get_barrier_semaphore(), [(n_col, *col), (n_y, *ygroup), sibling])
    partner = index - c0 + 1 - c0

    def block(y, z, c):
        return out_ref.at[slot(y, z, c)]

    def col_copy(q):
        return pltpu.make_async_remote_copy(
            x_ref, block(y0, z0, c0), col_sem.at[q], recv_sem.at[y0, z0, c0],
            device_id={"tensor": col[1](index, q)}, device_id_type=mesh_ids,
        )

    def y_copy(z, q):
        return pltpu.make_async_remote_copy(
            block(y0, z, c0), block(y0, z, c0), y_sem.at[z, q], recv_sem.at[y0, z, c0],
            device_id={"tensor": ygroup[1](index, q)}, device_id_type=mesh_ids,
        )

    def pair_copy(y, z):
        return pltpu.make_async_remote_copy(
            block(y, z, c0), block(y, z, c0), pair_sem.at[y, z], recv_sem.at[y, z, c0],
            device_id={"tensor": partner}, device_id_type=mesh_ids,
        )

    def arrival(y, z, c):
        return pltpu.make_async_remote_copy(
            x_ref, block(y, z, c), col_sem.at[0], recv_sem.at[y, z, c],
            device_id={"tensor": index}, device_id_type=mesh_ids,
        )

    def spread(z):
        def send_y(m, carry):
            y_copy(z, (y0 + m) % n_y).start()
            return carry

        lax.fori_loop(1, n_y, send_y, 0)
        pair_copy(y0, z).start()

    local = pltpu.make_async_copy(x_ref, block(y0, z0, c0), local_sem)
    local.start()

    def send_col(k, carry):
        col_copy((z0 + k) % n_col).start()
        return carry

    lax.fori_loop(1, n_col, send_col, 0)
    local.wait()
    spread(z0)

    def relay_col(k, carry):
        z = (z0 + k) % n_col
        arrival(y0, z, c0).wait_recv()
        spread(z)
        return carry

    lax.fori_loop(1, n_col, relay_col, 0)

    def relay_y(m, carry):
        y = (y0 + m) % n_y

        def each(k, inner):
            z = (z0 + k) % n_col
            arrival(y, z, c0).wait_recv()
            pair_copy(y, z).start()
            return inner

        return lax.fori_loop(0, n_col, each, carry)

    lax.fori_loop(1, n_y, relay_y, 0)

    def finish_col(k, carry):
        col_copy((z0 + k) % n_col).wait_send()
        return carry

    lax.fori_loop(1, n_col, finish_col, 0)

    def finish_y(k, carry):
        z = (z0 + k) % n_col

        def each(m, inner):
            y_copy(z, (y0 + m) % n_y).wait_send()
            return inner

        return lax.fori_loop(1, n_y, each, carry)

    lax.fori_loop(0, n_col, finish_y, 0)

    def finish_pair(m, carry):
        y = (y0 + m) % n_y

        def each(k, inner):
            z = (z0 + k) % n_col
            pair_copy(y, z).wait_send()
            arrival(y, z, 1 - c0).wait_recv()
            return inner

        return lax.fori_loop(0, n_col, each, carry)

    lax.fori_loop(0, n_y, finish_pair, 0)


def gather_tokens(x, col, ygroup, slot, n_col, n_y, collective_id):
    return pl.pallas_call(
        functools.partial(_gather_kernel, n_col, n_y, col, ygroup, slot),
        out_shape=jax.ShapeDtypeStruct((n_col * n_y * 2,) + x.shape, x.dtype),
        in_specs=[pl.BlockSpec(memory_space=pltpu.VMEM)],
        out_specs=pl.BlockSpec(memory_space=pltpu.VMEM),
        scratch_shapes=[
            pltpu.SemaphoreType.DMA,
            pltpu.SemaphoreType.DMA((n_col,)),
            pltpu.SemaphoreType.DMA((n_col, n_y)),
            pltpu.SemaphoreType.DMA((n_y, n_col)),
            pltpu.SemaphoreType.DMA((n_y, n_col, 2)),
        ],
        compiler_params=pltpu.CompilerParams(collective_id=collective_id, has_side_effects=True),
    )(x)


def token_slot(y, z, c):
    return (y * 4 + z) * 2 + c


def _reduce_kernel(n_col, n_y, n_dp, col, ygroup, attended_ref, output_ref, feedforward_ref, x_ref,
                   pages_ref, out_ref, pages_out, rows_ref, inbox0, chip, inbox1, stage, inbox2, sem0,
                   local_sem, send_sem, recv_sem, send2_sem, recv2_sem, page_local_sem, page_send_sem,
                   page_recv_sem):
    index = lax.axis_index("tensor")
    cpos, ypos, core = col[0](index), ygroup[0](index), index % 2
    mesh_ids = pl.DeviceIdType.MESH
    barrier = pltpu.get_barrier_semaphore()
    group = lax.axis_index("dp")

    def page_copy(g, slot):
        return pltpu.make_async_remote_copy(
            pages_ref.at[g], pages_out.at[slot], page_send_sem.at[g], page_recv_sem.at[slot],
            device_id={"dp": g}, device_id_type=mesh_ids,
        )

    def greet_group(k, carry):
        pl.semaphore_signal(
            barrier, inc=1, device_id={"dp": (group + k) % n_dp}, device_id_type=mesh_ids
        )
        return carry

    lax.fori_loop(1, n_dp, greet_group, 0)
    sibling = (2, lambda t: t % 2, lambda t, q: t - t % 2 + q)
    total = _signal(barrier, [sibling, (n_y, *ygroup), (n_col, *col)])

    product = (
        jnp.dot(attended_ref[...], output_ref[...], preferred_element_type=jnp.float32)
        + feedforward_ref[...]
    )
    rows = x_ref.shape[0]
    for owner in range(n_y * n_col * 2):
        rows_ref[owner // (2 * n_col), (owner // 2) % n_col, owner % 2] = product[
            owner * rows : (owner + 1) * rows
        ].astype(rows_ref.dtype)
    pl.semaphore_wait(barrier, total + n_dp - 1)
    page_local = pltpu.make_async_copy(pages_ref.at[group], pages_out.at[group], page_local_sem)
    page_local.start()

    def send_pages(k, carry):
        page_copy((group + k) % n_dp, group).start()
        return carry

    lax.fori_loop(1, n_dp, send_pages, 0)

    pair = pltpu.make_async_remote_copy(
        rows_ref.at[:, :, 1 - core], inbox0, sem0.at[0], sem0.at[1],
        device_id={"tensor": index - core + 1 - core}, device_id_type=mesh_ids,
    )
    pair.start()
    pair.wait_send()
    pair.wait_recv()
    for y in range(n_y):
        for z in range(n_col):
            chip[y, z] = (
                rows_ref[y, z, core].astype(jnp.float32) + inbox0[y, z].astype(jnp.float32)
            ).astype(chip.dtype)

    def plane_copy(q, z, slot):
        return pltpu.make_async_remote_copy(
            chip.at[q, z], inbox1.at[z, slot], send_sem.at[z, q], recv_sem.at[z, slot],
            device_id={"tensor": ygroup[1](index, q)}, device_id_type=mesh_ids,
        )

    def col_copy(q, slot):
        return pltpu.make_async_remote_copy(
            stage.at[q], inbox2.at[slot], send2_sem.at[q], recv2_sem.at[slot],
            device_id={"tensor": col[1](index, q)}, device_id_type=mesh_ids,
        )

    order = [(cpos + 1 + k) % n_col for k in range(n_col)]
    locals_ = []
    for z in order:
        local = pltpu.make_async_copy(chip.at[ypos, z], inbox1.at[z, ypos], local_sem.at[z])
        local.start()
        locals_.append(local)

        def send_plane(m, carry, z=z):
            plane_copy((ypos + m) % n_y, z, ypos).start()
            return carry

        lax.fori_loop(1, n_y, send_plane, 0)

    def plane_sum(z, local):
        def arrive(m, carry):
            plane_copy((ypos + m) % n_y, z, (ypos + m) % n_y).wait_recv()
            return carry

        lax.fori_loop(1, n_y, arrive, 0)
        local.wait()
        total = inbox1[z, 0].astype(jnp.float32)
        for sender in range(1, n_y):
            total = total + inbox1[z, sender].astype(jnp.float32)
        return total

    for z, local in zip(order[:-1], locals_[:-1]):
        stage[z] = plane_sum(z, local).astype(stage.dtype)
        col_copy(z, cpos).start()

    result = x_ref[...].astype(jnp.float32) + plane_sum(cpos, locals_[-1])

    def finish_plane(m, carry):
        q = (ypos + m) % n_y
        for z in order:
            plane_copy(q, z, ypos).wait_send()
        return carry

    lax.fori_loop(1, n_y, finish_plane, 0)

    for z in order[:-1]:
        col_copy(z, cpos).wait_send()
        col_copy(z, z).wait_recv()
        result = result + inbox2[z].astype(jnp.float32)
    out_ref[...] = result

    def finish_pages(k, carry):
        g = (group + k) % n_dp
        page_copy(g, group).wait_send()
        page_copy(g, g).wait_recv()
        return carry

    lax.fori_loop(1, n_dp, finish_pages, 0)
    page_local.wait()


def reduce_rows(attended, output_weight, feedforward, x, pages, col, ygroup, n_y, n_col, collective_id):
    block = x.shape
    n_dp = pages.shape[0]
    operands = (attended, output_weight, feedforward, x, pages)
    return pl.pallas_call(
        functools.partial(_reduce_kernel, n_col, n_y, n_dp, col, ygroup),
        out_shape=(
            jax.ShapeDtypeStruct(block, jnp.float32),
            jax.ShapeDtypeStruct(pages.shape, pages.dtype),
        ),
        in_specs=[pl.BlockSpec(memory_space=pltpu.VMEM)] * len(operands),
        out_specs=(pl.BlockSpec(memory_space=pltpu.VMEM), pl.BlockSpec(memory_space=pltpu.VMEM)),
        scratch_shapes=[
            pltpu.VMEM((n_y, n_col, 2) + block, x.dtype),
            pltpu.VMEM((n_y, n_col) + block, x.dtype),
            pltpu.VMEM((n_y, n_col) + block, x.dtype),
            pltpu.VMEM((n_col, n_y) + block, x.dtype),
            pltpu.VMEM((n_col,) + block, x.dtype),
            pltpu.VMEM((n_col,) + block, x.dtype),
            pltpu.SemaphoreType.DMA((2,)),
            pltpu.SemaphoreType.DMA((n_col,)),
            pltpu.SemaphoreType.DMA((n_col, n_y)),
            pltpu.SemaphoreType.DMA((n_col, n_y)),
            pltpu.SemaphoreType.DMA((n_col,)),
            pltpu.SemaphoreType.DMA((n_col,)),
            pltpu.SemaphoreType.DMA,
            pltpu.SemaphoreType.DMA((n_dp,)),
            pltpu.SemaphoreType.DMA((n_dp,)),
        ],
        compiler_params=pltpu.CompilerParams(collective_id=collective_id, has_side_effects=True),
    )(*operands)


def same_core_group(index):
    return index // 8


def same_core_member(index, q):
    return q * 8 + index % 8


def shards(
    hidden_states,
    attention_gain,
    feedforward_gain,
    heads_weight,
    output_weight,
    upward_weight,
    downward_weight,
    segments,
    page_targets,
):
    tensor_count = lax.axis_size("tensor")
    replica_count = lax.axis_size("dp")
    tensor_index = lax.axis_index("tensor")
    quarters = tensor_count // H
    quarter_width = HD // quarters
    quarter_index = tensor_index % quarters
    stream = segments[0]
    tokens_total = stream.shape[0]
    local_rows = hidden_states.shape[0]

    width = hidden_states.shape[1]
    planes = tensor_count // 8
    gathered = gather_tokens(
        hidden_states,
        (column_group, column_member),
        (same_core_group, same_core_member),
        token_slot,
        planes,
        4,
        0,
    )
    tokens = gathered.reshape(tokens_total, width)
    normed_attention = layer_norm(tokens, attention_gain)
    normed_feedforward = layer_norm(tokens, feedforward_gain)
    joined = jnp.dot(normed_attention, heads_weight, preferred_element_type=jnp.float32).astype(
        jnp.bfloat16
    )

    indices, starting = positions_of(stream)
    offsets = indices - starting
    query_piece = joined[:, :quarter_width]
    key_piece = joined[:, quarter_width : 2 * quarter_width]
    value_piece = joined[:, 2 * quarter_width :]
    leading = quarter_index == 0
    query_piece = jnp.where(leading, rotate_leading(query_piece, offsets, ROT), query_piece)
    key_piece = jnp.where(leading, rotate_leading(key_piece, offsets, ROT), key_piece)

    page_count = tokens_total // PAGE
    page_rows = jnp.concatenate([key_piece, value_piece], 1)
    targets = page_targets[:, 0]
    page_numbers = jnp.arange(page_count, dtype=jnp.int32)
    earlier = jnp.sum(
        (
            (targets[None, :] == targets[:, None]) & (page_numbers[None, :] < page_numbers[:, None])
        ).astype(jnp.int32),
        axis=1,
    )
    capacity = 2 * page_count // replica_count
    slot_numbers = targets * capacity + earlier
    token_slots = jnp.repeat(slot_numbers, PAGE)
    slot_rows = jnp.arange(replica_count * capacity * PAGE, dtype=jnp.int32)
    token_numbers = jnp.arange(tokens_total, dtype=jnp.int32)
    placing = (
        (token_slots[None, :] == slot_rows[:, None] // PAGE)
        & (token_numbers[None, :] % PAGE == slot_rows[:, None] % PAGE)
    ).astype(jnp.bfloat16)
    outgoing = jnp.dot(placing, page_rows, preferred_element_type=jnp.float32).astype(jnp.bfloat16)
    outgoing = outgoing.reshape(replica_count, capacity * PAGE, 2 * quarter_width)
    head_pieces, feedforward = exchange_all(
        1,
        (jnp.concatenate([query_piece, key_piece], 1)[None], "tensor", quarters, True, None),
        work=(_feedforward_up, _feedforward_down),
        inputs=(normed_feedforward, upward_weight, downward_weight),
        results=(jax.ShapeDtypeStruct((tokens_total, width), jnp.float32),),
    )
    queries = head_pieces[:, :, :quarter_width].transpose(1, 0, 2).reshape(tokens_total, HD)
    keys = head_pieces[:, :, quarter_width:].transpose(1, 0, 2).reshape(tokens_total, HD)

    scores = jnp.dot(queries, keys.T, preferred_element_type=jnp.float32) * HD ** (-0.5)
    allowed = (stream[None, :] == stream[:, None]) & (indices[None, :] <= indices[:, None])
    peak = jnp.max(jnp.where(allowed, scores, -jnp.inf), axis=1, keepdims=True)
    weights = jnp.where(allowed, jnp.exp(scores - peak), 0.0)
    weight_sum = jnp.sum(weights, axis=1, keepdims=True)
    mixed = jnp.dot(weights.astype(jnp.bfloat16), value_piece, preferred_element_type=jnp.float32)
    attended = (mixed / weight_sum).astype(jnp.bfloat16)

    layer_output, incoming = reduce_rows(
        attended,
        output_weight,
        feedforward,
        hidden_states,
        outgoing,
        (column_group, column_member),
        (same_core_group, same_core_member),
        4,
        planes,
        2,
    )

    cache_pages = incoming.reshape(1, replica_count, capacity, PAGE, 2 * quarter_width)
    return (layer_output, cache_pages)


def solution(mesh):
    in_specs = (
        P(("dp", "tensor"), None),
        P(),
        P(),
        P(None, "tensor"),
        P("tensor", None),
        P(None, "tensor"),
        P("tensor", None),
        P("dp", None),
        P("dp", None),
    )
    out_specs = (P(("dp", "tensor"), None), P("dp", None, None, None, "tensor"))
    return jax.shard_map(shards, mesh=mesh, in_specs=in_specs, out_specs=out_specs, check_vma=False)
```

```python
import functools
import math

import jax
import jax.numpy as jnp
from jax import lax
from jax.experimental import pallas as pl
from jax.experimental.pallas import tpu as pltpu
from jax.sharding import PartitionSpec as P

H = 8
HD = 256
ROT = 64
PAGE = 16


epsilon = 1e-05
rotary_base = 10000.0


def layer_norm(values, gain):
    floats = values.astype(jnp.float32)
    center = jnp.mean(floats, axis=-1, keepdims=True)
    shifted = floats - center
    spread = jnp.mean(shifted * shifted, axis=-1, keepdims=True)
    return (shifted * lax.rsqrt(spread + epsilon) * gain).astype(jnp.bfloat16)


def positions_of(stream):
    indices = jnp.arange(stream.shape[0], dtype=jnp.int32)
    boundary = jnp.concatenate([jnp.ones((1,), dtype=bool), stream[1:] != stream[:-1]])
    starting = lax.cummax(jnp.where(boundary, indices, jnp.zeros_like(indices)), axis=0)
    return (indices, starting)


def rotate_leading(vectors, offsets, rotary_dims):
    half_dims = rotary_dims // 2
    frequency = jnp.exp(
        jnp.arange(half_dims, dtype=jnp.float32) * (-2.0 * math.log(rotary_base) / rotary_dims)
    )
    angles = offsets.astype(jnp.float32)[:, None] * frequency[None, :]
    cosine = jnp.cos(angles)
    sine = jnp.sin(angles)
    floats = vectors.astype(jnp.float32)
    leading = floats[..., :half_dims]
    trailing = floats[..., half_dims:rotary_dims]
    rotated = jnp.concatenate(
        [
            leading * cosine - trailing * sine,
            trailing * cosine + leading * sine,
            floats[..., rotary_dims:],
        ],
        axis=-1,
    )
    return rotated.astype(jnp.bfloat16)


def _exchange_kernel(plans, work, extra_in, extra_out, *refs):
    count = len(plans)
    sources, refs = refs[:count], refs[count:]
    inputs, refs = refs[:extra_in], refs[extra_in:]
    outs, refs = refs[:count], refs[count:]
    results, semaphores = refs[:extra_out], refs[extra_out:]
    mesh_ids = pl.DeviceIdType.MESH
    barrier = pltpu.get_barrier_semaphore()
    steps = []
    for number, (axis, n, shared, position, member) in enumerate(plans):
        src_ref, out_ref = sources[number], outs[number]
        local_sem, send_sem, recv_sem = semaphores[3 * number : 3 * number + 3]
        index = lax.axis_index(axis)
        pos = position(index)

        def peer_copy(q, slot, src_ref=src_ref, out_ref=out_ref, send_sem=send_sem,
                      recv_sem=recv_sem, axis=axis, member=member, index=index, shared=shared):
            return pltpu.make_async_remote_copy(
                src_ref=src_ref.at[0] if shared else src_ref.at[q],
                dst_ref=out_ref.at[slot],
                send_sem=send_sem.at[q],
                recv_sem=recv_sem.at[slot],
                device_id={axis: member(index, q)},
                device_id_type=mesh_ids,
            )

        def greet(k, carry, n=n, pos=pos, axis=axis, member=member, index=index):
            q = (pos + k) % n
            pl.semaphore_signal(
                barrier, inc=1, device_id={axis: member(index, q)}, device_id_type=mesh_ids
            )
            return carry

        lax.fori_loop(1, n, greet, 0)
        local = pltpu.make_async_copy(
            src_ref.at[0] if shared else src_ref.at[pos], out_ref.at[pos], local_sem
        )
        steps.append((n, pos, peer_copy, local))
    carried = work[0](*inputs) if work is not None else None
    pl.semaphore_wait(barrier, sum(plan[1] - 1 for plan in plans))

    for n, pos, peer_copy, local in steps:
        local.start()

        def send(k, carry, n=n, pos=pos, peer_copy=peer_copy):
            peer_copy((pos + k) % n, pos).start()
            return carry

        lax.fori_loop(1, n, send, 0)

    if work is not None:
        work[1](carried, *inputs, *results)

    for n, pos, peer_copy, local in steps:

        def finish(k, carry, n=n, pos=pos, peer_copy=peer_copy):
            q = (pos + k) % n
            peer_copy(q, pos).wait_send()
            peer_copy(q, q).wait_recv()
            return carry

        lax.fori_loop(1, n, finish, 0)
        local.wait()


def contiguous(n):
    return (lambda index: index % n, lambda index, q: index - index % n + q)


def plane_group(index):
    return (index // 8) * 2 + index % 2


def plane_member(index, q):
    return ((q // 2) * 4 + (index // 2) % 4) * 2 + q % 2


def token_block(zc, p):
    return ((p // 2) * 4 + zc) * 2 + p % 2


def plane_rows(rows_ref, q, z):
    return rows_ref.at[q // 2, z, q % 2]


def column_group(index):
    return (index // 2) % 4


def column_member(index, q):
    return ((index // 8) * 4 + q) * 2 + index % 2


def exchange_all(collective_id, *requests, work=None, inputs=(), results=()):
    plans, blocks, shapes, scratch = [], [], [], []
    for data, axis, n, shared, group in requests:
        position, member = group if group is not None else contiguous(n)
        plans.append((axis, n, shared, position, member))
        blocks.append(data)
        shapes.append(jax.ShapeDtypeStruct((n,) + data.shape[1:], data.dtype))
        scratch += [
            pltpu.SemaphoreType.DMA,
            pltpu.SemaphoreType.DMA((n,)),
            pltpu.SemaphoreType.DMA((n,)),
        ]
    operands = blocks + list(inputs)
    out_shapes = shapes + list(results)
    return pl.pallas_call(
        functools.partial(_exchange_kernel, tuple(plans), work, len(inputs), len(results)),
        out_shape=tuple(out_shapes),
        in_specs=[pl.BlockSpec(memory_space=pltpu.VMEM)] * len(operands),
        out_specs=tuple(pl.BlockSpec(memory_space=pltpu.VMEM) for _ in out_shapes),
        scratch_shapes=scratch,
        compiler_params=pltpu.CompilerParams(collective_id=collective_id, has_side_effects=True),
    )(*operands)


def exchange(blocks, axis, n, shared, collective_id, group=None):
    return exchange_all(collective_id, (blocks, axis, n, shared, group))[0]


def _feedforward_up(normed_ref, upward_ref, downward_ref):
    upward = jnp.dot(normed_ref[...], upward_ref[...], preferred_element_type=jnp.float32)
    return (0.5 * upward * (1.0 + lax.erf(upward * math.sqrt(0.5)))).astype(jnp.bfloat16)


def _feedforward_down(hidden, normed_ref, upward_ref, downward_ref, out_ref):
    out_ref[...] = jnp.dot(hidden, downward_ref[...], preferred_element_type=jnp.float32)


def _signal(barrier, groups):
    index = lax.axis_index("tensor")
    total = 0
    for n, position, member in groups:
        pos = position(index)

        def greet(k, carry, n=n, pos=pos, member=member):
            pl.semaphore_signal(
                barrier,
                inc=1,
                device_id={"tensor": member(index, (pos + k) % n)},
                device_id_type=pl.DeviceIdType.MESH,
            )
            return carry

        lax.fori_loop(1, n, greet, 0)
        total += n - 1
    return total


def _greet(barrier, groups, extra=0):
    index = lax.axis_index("tensor")
    total = 0
    for n, position, member in groups:
        pos = position(index)

        def greet(k, carry, n=n, pos=pos, member=member):
            pl.semaphore_signal(
                barrier,
                inc=1,
                device_id={"tensor": member(index, (pos + k) % n)},
                device_id_type=pl.DeviceIdType.MESH,
            )
            return carry

        lax.fori_loop(1, n, greet, 0)
        total += n - 1
    pl.semaphore_wait(barrier, total + extra)


def _gather_kernel(n_col, n_y, col, ygroup, slot, x_ref, out_ref, local_sem, col_sem, y_sem, pair_sem,
                   recv_sem):
    index = lax.axis_index("tensor")
    z0, y0, c0 = col[0](index), ygroup[0](index), index % 2
    mesh_ids = pl.DeviceIdType.MESH
    sibling = (2, lambda t: t % 2, lambda t, q: t - t % 2 + q)
    _greet(pltpu.get_barrier_semaphore(), [(n_col, *col), (n_y, *ygroup), sibling])
    partner = index - c0 + 1 - c0

    def block(y, z, c):
        return out_ref.at[slot(y, z, c)]

    def col_copy(q):
        return pltpu.make_async_remote_copy(
            x_ref, block(y0, z0, c0), col_sem.at[q], recv_sem.at[y0, z0, c0],
            device_id={"tensor": col[1](index, q)}, device_id_type=mesh_ids,
        )

    def y_copy(z, q):
        return pltpu.make_async_remote_copy(
            block(y0, z, c0), block(y0, z, c0), y_sem.at[z, q], recv_sem.at[y0, z, c0],
            device_id={"tensor": ygroup[1](index, q)}, device_id_type=mesh_ids,
        )

    def pair_copy(y, z):
        return pltpu.make_async_remote_copy(
            block(y, z, c0), block(y, z, c0), pair_sem.at[y, z], recv_sem.at[y, z, c0],
            device_id={"tensor": partner}, device_id_type=mesh_ids,
        )

    def arrival(y, z, c):
        return pltpu.make_async_remote_copy(
            x_ref, block(y, z, c), col_sem.at[0], recv_sem.at[y, z, c],
            device_id={"tensor": index}, device_id_type=mesh_ids,
        )

    def spread(z):
        def send_y(m, carry):
            y_copy(z, (y0 + m) % n_y).start()
            return carry

        lax.fori_loop(1, n_y, send_y, 0)
        pair_copy(y0, z).start()

    local = pltpu.make_async_copy(x_ref, block(y0, z0, c0), local_sem)
    local.start()

    def send_col(k, carry):
        col_copy((z0 + k) % n_col).start()
        return carry

    lax.fori_loop(1, n_col, send_col, 0)
    local.wait()
    spread(z0)

    def relay_col(k, carry):
        z = (z0 + k) % n_col
        arrival(y0, z, c0).wait_recv()
        spread(z)
        return carry

    lax.fori_loop(1, n_col, relay_col, 0)

    def relay_y(m, carry):
        y = (y0 + m) % n_y

        def each(k, inner):
            z = (z0 + k) % n_col
            arrival(y, z, c0).wait_recv()
            pair_copy(y, z).start()
            return inner

        return lax.fori_loop(0, n_col, each, carry)

    lax.fori_loop(1, n_y, relay_y, 0)

    def finish_col(k, carry):
        col_copy((z0 + k) % n_col).wait_send()
        return carry

    lax.fori_loop(1, n_col, finish_col, 0)

    def finish_y(k, carry):
        z = (z0 + k) % n_col

        def each(m, inner):
            y_copy(z, (y0 + m) % n_y).wait_send()
            return inner

        return lax.fori_loop(1, n_y, each, carry)

    lax.fori_loop(0, n_col, finish_y, 0)

    def finish_pair(m, carry):
        y = (y0 + m) % n_y

        def each(k, inner):
            z = (z0 + k) % n_col
            pair_copy(y, z).wait_send()
            arrival(y, z, 1 - c0).wait_recv()
            return inner

        return lax.fori_loop(0, n_col, each, carry)

    lax.fori_loop(0, n_y, finish_pair, 0)


def gather_tokens(x, col, ygroup, slot, n_col, n_y, collective_id):
    return pl.pallas_call(
        functools.partial(_gather_kernel, n_col, n_y, col, ygroup, slot),
        out_shape=jax.ShapeDtypeStruct((n_col * n_y * 2,) + x.shape, x.dtype),
        in_specs=[pl.BlockSpec(memory_space=pltpu.VMEM)],
        out_specs=pl.BlockSpec(memory_space=pltpu.VMEM),
        scratch_shapes=[
            pltpu.SemaphoreType.DMA,
            pltpu.SemaphoreType.DMA((n_col,)),
            pltpu.SemaphoreType.DMA((n_col, n_y)),
            pltpu.SemaphoreType.DMA((n_y, n_col)),
            pltpu.SemaphoreType.DMA((n_y, n_col, 2)),
        ],
        compiler_params=pltpu.CompilerParams(collective_id=collective_id, has_side_effects=True),
    )(x)


def token_slot(y, z, c):
    return (y * 4 + z) * 2 + c


def _reduce_kernel(n_col, n_y, n_dp, col, ygroup, attended_ref, output_ref, feedforward_ref, x_ref,
                   pages_ref, out_ref, pages_out, rows_ref, inbox0, chip, inbox1, stage, inbox2, sem0,
                   local_sem, send_sem, recv_sem, send2_sem, recv2_sem, page_local_sem, page_send_sem,
                   page_recv_sem):
    index = lax.axis_index("tensor")
    cpos, ypos, core = col[0](index), ygroup[0](index), index % 2
    mesh_ids = pl.DeviceIdType.MESH
    barrier = pltpu.get_barrier_semaphore()
    group = lax.axis_index("dp")

    def page_copy(g, slot):
        return pltpu.make_async_remote_copy(
            pages_ref.at[g], pages_out.at[slot], page_send_sem.at[g], page_recv_sem.at[slot],
            device_id={"dp": g}, device_id_type=mesh_ids,
        )

    def greet_group(k, carry):
        pl.semaphore_signal(
            barrier, inc=1, device_id={"dp": (group + k) % n_dp}, device_id_type=mesh_ids
        )
        return carry

    lax.fori_loop(1, n_dp, greet_group, 0)
    sibling = (2, lambda t: t % 2, lambda t, q: t - t % 2 + q)
    total = _signal(barrier, [sibling, (n_y, *ygroup), (n_col, *col)])

    product = (
        jnp.dot(attended_ref[...], output_ref[...], preferred_element_type=jnp.float32)
        + feedforward_ref[...]
    )
    rows = x_ref.shape[0]
    for owner in range(n_y * n_col * 2):
        rows_ref[owner // (2 * n_col), (owner // 2) % n_col, owner % 2] = product[
            owner * rows : (owner + 1) * rows
        ].astype(rows_ref.dtype)
    pl.semaphore_wait(barrier, total + n_dp - 1)
    page_local = pltpu.make_async_copy(pages_ref.at[group], pages_out.at[group], page_local_sem)
    page_local.start()

    def send_pages(k, carry):
        page_copy((group + k) % n_dp, group).start()
        return carry

    lax.fori_loop(1, n_dp, send_pages, 0)

    pair = pltpu.make_async_remote_copy(
        rows_ref.at[:, :, 1 - core], inbox0, sem0.at[0], sem0.at[1],
        device_id={"tensor": index - core + 1 - core}, device_id_type=mesh_ids,
    )
    pair.start()
    pair.wait_send()
    pair.wait_recv()
    for y in range(n_y):
        for z in range(n_col):
            chip[y, z] = (
                rows_ref[y, z, core].astype(jnp.float32) + inbox0[y, z].astype(jnp.float32)
            ).astype(chip.dtype)

    def plane_copy(q, z, slot):
        return pltpu.make_async_remote_copy(
            chip.at[q, z], inbox1.at[z, slot], send_sem.at[z, q], recv_sem.at[z, slot],
            device_id={"tensor": ygroup[1](index, q)}, device_id_type=mesh_ids,
        )

    def col_copy(q, slot):
        return pltpu.make_async_remote_copy(
            stage.at[q], inbox2.at[slot], send2_sem.at[q], recv2_sem.at[slot],
            device_id={"tensor": col[1](index, q)}, device_id_type=mesh_ids,
        )

    order = [(cpos + 1 + k) % n_col for k in range(n_col)]
    locals_ = []
    for z in order:
        local = pltpu.make_async_copy(chip.at[ypos, z], inbox1.at[z, ypos], local_sem.at[z])
        local.start()
        locals_.append(local)

        def send_plane(m, carry, z=z):
            plane_copy((ypos + m) % n_y, z, ypos).start()
            return carry

        lax.fori_loop(1, n_y, send_plane, 0)

    def plane_sum(z, local):
        def arrive(m, carry):
            plane_copy((ypos + m) % n_y, z, (ypos + m) % n_y).wait_recv()
            return carry

        lax.fori_loop(1, n_y, arrive, 0)
        local.wait()
        total = inbox1[z, 0].astype(jnp.float32)
        for sender in range(1, n_y):
            total = total + inbox1[z, sender].astype(jnp.float32)
        return total

    for z, local in zip(order[:-1], locals_[:-1]):
        stage[z] = plane_sum(z, local).astype(stage.dtype)
        col_copy(z, cpos).start()

    result = x_ref[...].astype(jnp.float32) + plane_sum(cpos, locals_[-1])

    def finish_plane(m, carry):
        q = (ypos + m) % n_y
        for z in order:
            plane_copy(q, z, ypos).wait_send()
        return carry

    lax.fori_loop(1, n_y, finish_plane, 0)

    for z in order[:-1]:
        col_copy(z, cpos).wait_send()
        col_copy(z, z).wait_recv()
        result = result + inbox2[z].astype(jnp.float32)
    out_ref[...] = result

    def finish_pages(k, carry):
        g = (group + k) % n_dp
        page_copy(g, group).wait_send()
        page_copy(g, g).wait_recv()
        return carry

    lax.fori_loop(1, n_dp, finish_pages, 0)
    page_local.wait()


def reduce_rows(attended, output_weight, feedforward, x, pages, col, ygroup, n_y, n_col, collective_id):
    block = x.shape
    n_dp = pages.shape[0]
    operands = (attended, output_weight, feedforward, x, pages)
    return pl.pallas_call(
        functools.partial(_reduce_kernel, n_col, n_y, n_dp, col, ygroup),
        out_shape=(
            jax.ShapeDtypeStruct(block, jnp.float32),
            jax.ShapeDtypeStruct(pages.shape, pages.dtype),
        ),
        in_specs=[pl.BlockSpec(memory_space=pltpu.VMEM)] * len(operands),
        out_specs=(pl.BlockSpec(memory_space=pltpu.VMEM), pl.BlockSpec(memory_space=pltpu.VMEM)),
        scratch_shapes=[
            pltpu.VMEM((n_y, n_col, 2) + block, x.dtype),
            pltpu.VMEM((n_y, n_col) + block, x.dtype),
            pltpu.VMEM((n_y, n_col) + block, x.dtype),
            pltpu.VMEM((n_col, n_y) + block, x.dtype),
            pltpu.VMEM((n_col,) + block, x.dtype),
            pltpu.VMEM((n_col,) + block, x.dtype),
            pltpu.SemaphoreType.DMA((2,)),
            pltpu.SemaphoreType.DMA((n_col,)),
            pltpu.SemaphoreType.DMA((n_col, n_y)),
            pltpu.SemaphoreType.DMA((n_col, n_y)),
            pltpu.SemaphoreType.DMA((n_col,)),
            pltpu.SemaphoreType.DMA((n_col,)),
            pltpu.SemaphoreType.DMA,
            pltpu.SemaphoreType.DMA((n_dp,)),
            pltpu.SemaphoreType.DMA((n_dp,)),
        ],
        compiler_params=pltpu.CompilerParams(collective_id=collective_id, has_side_effects=True),
    )(*operands)


def same_core_group(index):
    return index // 8


def same_core_member(index, q):
    return q * 8 + index % 8


def shards(
    hidden_states,
    attention_gain,
    feedforward_gain,
    heads_weight,
    output_weight,
    upward_weight,
    downward_weight,
    segments,
    page_targets,
):
    tensor_count = lax.axis_size("tensor")
    replica_count = lax.axis_size("dp")
    tensor_index = lax.axis_index("tensor")
    quarters = tensor_count // H
    quarter_width = HD // quarters
    quarter_index = tensor_index % quarters
    stream = segments[0]
    tokens_total = stream.shape[0]
    local_rows = hidden_states.shape[0]

    width = hidden_states.shape[1]
    planes = tensor_count // 8
    gathered = gather_tokens(
        hidden_states,
        (column_group, column_member),
        (same_core_group, same_core_member),
        token_slot,
        planes,
        4,
        0,
    )
    tokens = gathered.reshape(tokens_total, width)
    ones = jnp.ones((width, 1), jnp.bfloat16)
    center = jnp.dot(tokens, ones, preferred_element_type=jnp.float32) / width
    shifted = tokens.astype(jnp.float32) - center
    spread = (
        jnp.dot(
            shifted * shifted,
            ones.astype(jnp.float32),
            precision=lax.Precision.HIGHEST,
            preferred_element_type=jnp.float32,
        )
        / width
    )
    scaled = shifted * lax.rsqrt(spread + epsilon)
    normed_attention = (scaled * attention_gain).astype(jnp.bfloat16)
    normed_feedforward = (scaled * feedforward_gain).astype(jnp.bfloat16)
    joined = jnp.dot(normed_attention, heads_weight, preferred_element_type=jnp.float32).astype(
        jnp.bfloat16
    )

    indices, starting = positions_of(stream)
    offsets = indices - starting
    query_piece = joined[:, :quarter_width]
    key_piece = joined[:, quarter_width : 2 * quarter_width]
    value_piece = joined[:, 2 * quarter_width :]
    leading = quarter_index == 0
    query_piece = jnp.where(leading, rotate_leading(query_piece, offsets, ROT), query_piece)
    key_piece = jnp.where(leading, rotate_leading(key_piece, offsets, ROT), key_piece)

    page_count = tokens_total // PAGE
    page_rows = jnp.concatenate([key_piece, value_piece], 1).reshape(
        page_count, PAGE * 2 * quarter_width
    )
    targets = page_targets[:, 0]
    page_numbers = jnp.arange(page_count, dtype=jnp.int32)
    earlier = jnp.sum(
        (
            (targets[None, :] == targets[:, None]) & (page_numbers[None, :] < page_numbers[:, None])
        ).astype(jnp.int32),
        axis=1,
    )
    capacity = 2 * page_count // replica_count
    slot_numbers = targets * capacity + earlier
    placing = (
        jnp.arange(replica_count * capacity, dtype=jnp.int32)[:, None] == slot_numbers[None, :]
    ).astype(jnp.bfloat16)
    outgoing = jnp.dot(placing, page_rows, preferred_element_type=jnp.float32).astype(jnp.bfloat16)
    outgoing = outgoing.reshape(replica_count, capacity * PAGE, 2 * quarter_width)
    head_pieces, feedforward = exchange_all(
        1,
        (jnp.concatenate([query_piece, key_piece], 1)[None], "tensor", quarters, True, None),
        work=(_feedforward_up, _feedforward_down),
        inputs=(normed_feedforward, upward_weight, downward_weight),
        results=(jax.ShapeDtypeStruct((tokens_total, width), jnp.float32),),
    )
    queries = head_pieces[:, :, :quarter_width].transpose(1, 0, 2).reshape(tokens_total, HD)
    keys = head_pieces[:, :, quarter_width:].transpose(1, 0, 2).reshape(tokens_total, HD)

    scores = jnp.dot(queries, keys.T, preferred_element_type=jnp.float32) * HD ** (-0.5)
    allowed = (stream[None, :] == stream[:, None]) & (indices[None, :] <= indices[:, None])
    peak = jnp.max(jnp.where(allowed, scores, -jnp.inf), axis=1, keepdims=True)
    weights = jnp.where(allowed, jnp.exp(scores - peak), 0.0)
    weight_sum = jnp.sum(weights, axis=1, keepdims=True)
    mixed = jnp.dot(weights.astype(jnp.bfloat16), value_piece, preferred_element_type=jnp.float32)
    attended = (mixed / weight_sum).astype(jnp.bfloat16)

    layer_output, incoming = reduce_rows(
        attended,
        output_weight,
        feedforward,
        hidden_states,
        outgoing,
        (column_group, column_member),
        (same_core_group, same_core_member),
        4,
        planes,
        2,
    )

    cache_pages = incoming.reshape(1, replica_count, capacity, PAGE, 2 * quarter_width)
    return (layer_output, cache_pages)


def solution(mesh):
    in_specs = (
        P(("dp", "tensor"), None),
        P(),
        P(),
        P(None, "tensor"),
        P("tensor", None),
        P(None, "tensor"),
        P("tensor", None),
        P("dp", None),
        P("dp", None),
    )
    out_specs = (P(("dp", "tensor"), None), P("dp", None, None, None, "tensor"))
    return jax.shard_map(shards, mesh=mesh, in_specs=in_specs, out_specs=out_specs, check_vma=False)
```

```python
import functools
import math

import jax
import jax.numpy as jnp
from jax import lax
from jax.experimental import pallas as pl
from jax.experimental.pallas import tpu as pltpu
from jax.sharding import PartitionSpec as P

H = 8
HD = 256
ROT = 64
PAGE = 16


epsilon = 1e-05
rotary_base = 10000.0


def layer_norm(values, gain):
    floats = values.astype(jnp.float32)
    center = jnp.mean(floats, axis=-1, keepdims=True)
    shifted = floats - center
    spread = jnp.mean(shifted * shifted, axis=-1, keepdims=True)
    return (shifted * lax.rsqrt(spread + epsilon) * gain).astype(jnp.bfloat16)


def positions_of(stream):
    indices = jnp.arange(stream.shape[0], dtype=jnp.int32)
    boundary = jnp.concatenate([jnp.ones((1,), dtype=bool), stream[1:] != stream[:-1]])
    starting = lax.cummax(jnp.where(boundary, indices, jnp.zeros_like(indices)), axis=0)
    return (indices, starting)


def rotate_leading(vectors, offsets, rotary_dims):
    half_dims = rotary_dims // 2
    frequency = jnp.exp(
        jnp.arange(half_dims, dtype=jnp.float32) * (-2.0 * math.log(rotary_base) / rotary_dims)
    )
    angles = offsets.astype(jnp.float32)[:, None] * frequency[None, :]
    cosine = jnp.cos(angles)
    sine = jnp.sin(angles)
    floats = vectors.astype(jnp.float32)
    leading = floats[..., :half_dims]
    trailing = floats[..., half_dims:rotary_dims]
    rotated = jnp.concatenate(
        [
            leading * cosine - trailing * sine,
            trailing * cosine + leading * sine,
            floats[..., rotary_dims:],
        ],
        axis=-1,
    )
    return rotated.astype(jnp.bfloat16)


def _exchange_kernel(plans, work, extra_in, extra_out, *refs):
    count = len(plans)
    sources, refs = refs[:count], refs[count:]
    inputs, refs = refs[:extra_in], refs[extra_in:]
    outs, refs = refs[:count], refs[count:]
    results, semaphores = refs[:extra_out], refs[extra_out:]
    mesh_ids = pl.DeviceIdType.MESH
    barrier = pltpu.get_barrier_semaphore()
    steps = []
    for number, (axis, n, shared, position, member) in enumerate(plans):
        src_ref, out_ref = sources[number], outs[number]
        local_sem, send_sem, recv_sem = semaphores[3 * number : 3 * number + 3]
        index = lax.axis_index(axis)
        pos = position(index)

        def peer_copy(q, slot, src_ref=src_ref, out_ref=out_ref, send_sem=send_sem,
                      recv_sem=recv_sem, axis=axis, member=member, index=index, shared=shared):
            return pltpu.make_async_remote_copy(
                src_ref=src_ref.at[0] if shared else src_ref.at[q],
                dst_ref=out_ref.at[slot],
                send_sem=send_sem.at[q],
                recv_sem=recv_sem.at[slot],
                device_id={axis: member(index, q)},
                device_id_type=mesh_ids,
            )

        def greet(k, carry, n=n, pos=pos, axis=axis, member=member, index=index):
            q = (pos + k) % n
            pl.semaphore_signal(
                barrier, inc=1, device_id={axis: member(index, q)}, device_id_type=mesh_ids
            )
            return carry

        lax.fori_loop(1, n, greet, 0)
        local = pltpu.make_async_copy(
            src_ref.at[0] if shared else src_ref.at[pos], out_ref.at[pos], local_sem
        )
        steps.append((n, pos, peer_copy, local))
    carried = work[0](*inputs) if work is not None else None
    pl.semaphore_wait(barrier, sum(plan[1] - 1 for plan in plans))

    for n, pos, peer_copy, local in steps:
        local.start()

        def send(k, carry, n=n, pos=pos, peer_copy=peer_copy):
            peer_copy((pos + k) % n, pos).start()
            return carry

        lax.fori_loop(1, n, send, 0)

    if work is not None:
        work[1](carried, *inputs, *results)

    for n, pos, peer_copy, local in steps:

        def finish(k, carry, n=n, pos=pos, peer_copy=peer_copy):
            q = (pos + k) % n
            peer_copy(q, pos).wait_send()
            peer_copy(q, q).wait_recv()
            return carry

        lax.fori_loop(1, n, finish, 0)
        local.wait()


def contiguous(n):
    return (lambda index: index % n, lambda index, q: index - index % n + q)


def plane_group(index):
    return (index // 8) * 2 + index % 2


def plane_member(index, q):
    return ((q // 2) * 4 + (index // 2) % 4) * 2 + q % 2


def token_block(zc, p):
    return ((p // 2) * 4 + zc) * 2 + p % 2


def plane_rows(rows_ref, q, z):
    return rows_ref.at[q // 2, z, q % 2]


def column_group(index):
    return (index // 2) % 4


def column_member(index, q):
    return ((index // 8) * 4 + q) * 2 + index % 2


def exchange_all(collective_id, *requests, work=None, inputs=(), results=()):
    plans, blocks, shapes, scratch = [], [], [], []
    for data, axis, n, shared, group in requests:
        position, member = group if group is not None else contiguous(n)
        plans.append((axis, n, shared, position, member))
        blocks.append(data)
        shapes.append(jax.ShapeDtypeStruct((n,) + data.shape[1:], data.dtype))
        scratch += [
            pltpu.SemaphoreType.DMA,
            pltpu.SemaphoreType.DMA((n,)),
            pltpu.SemaphoreType.DMA((n,)),
        ]
    operands = blocks + list(inputs)
    out_shapes = shapes + list(results)
    return pl.pallas_call(
        functools.partial(_exchange_kernel, tuple(plans), work, len(inputs), len(results)),
        out_shape=tuple(out_shapes),
        in_specs=[pl.BlockSpec(memory_space=pltpu.VMEM)] * len(operands),
        out_specs=tuple(pl.BlockSpec(memory_space=pltpu.VMEM) for _ in out_shapes),
        scratch_shapes=scratch,
        compiler_params=pltpu.CompilerParams(collective_id=collective_id, has_side_effects=True),
    )(*operands)


def exchange(blocks, axis, n, shared, collective_id, group=None):
    return exchange_all(collective_id, (blocks, axis, n, shared, group))[0]


def _feedforward_up(normed_ref, upward_ref, downward_ref):
    upward = jnp.dot(normed_ref[...], upward_ref[...], preferred_element_type=jnp.float32)
    return (0.5 * upward * (1.0 + lax.erf(upward * math.sqrt(0.5)))).astype(jnp.bfloat16)


def _feedforward_down(hidden, normed_ref, upward_ref, downward_ref, out_ref):
    out_ref[...] = jnp.dot(hidden, downward_ref[...], preferred_element_type=jnp.float32)


def _signal(barrier, groups):
    index = lax.axis_index("tensor")
    total = 0
    for n, position, member in groups:
        pos = position(index)

        def greet(k, carry, n=n, pos=pos, member=member):
            pl.semaphore_signal(
                barrier,
                inc=1,
                device_id={"tensor": member(index, (pos + k) % n)},
                device_id_type=pl.DeviceIdType.MESH,
            )
            return carry

        lax.fori_loop(1, n, greet, 0)
        total += n - 1
    return total


def _greet(barrier, groups, extra=0):
    index = lax.axis_index("tensor")
    total = 0
    for n, position, member in groups:
        pos = position(index)

        def greet(k, carry, n=n, pos=pos, member=member):
            pl.semaphore_signal(
                barrier,
                inc=1,
                device_id={"tensor": member(index, (pos + k) % n)},
                device_id_type=pl.DeviceIdType.MESH,
            )
            return carry

        lax.fori_loop(1, n, greet, 0)
        total += n - 1
    pl.semaphore_wait(barrier, total + extra)


def _gather_kernel(n_col, n_y, col, ygroup, slot, x_ref, out_ref, local_sem, col_sem, y_sem, pair_sem,
                   recv_sem):
    index = lax.axis_index("tensor")
    z0, y0, c0 = col[0](index), ygroup[0](index), index % 2
    mesh_ids = pl.DeviceIdType.MESH
    sibling = (2, lambda t: t % 2, lambda t, q: t - t % 2 + q)
    _greet(pltpu.get_barrier_semaphore(), [(n_col, *col), (n_y, *ygroup), sibling])
    partner = index - c0 + 1 - c0

    def block(y, z, c):
        return out_ref.at[slot(y, z, c)]

    def col_copy(q):
        return pltpu.make_async_remote_copy(
            x_ref, block(y0, z0, c0), col_sem.at[q], recv_sem.at[y0, z0, c0],
            device_id={"tensor": col[1](index, q)}, device_id_type=mesh_ids,
        )

    def y_copy(z, q):
        return pltpu.make_async_remote_copy(
            block(y0, z, c0), block(y0, z, c0), y_sem.at[z, q], recv_sem.at[y0, z, c0],
            device_id={"tensor": ygroup[1](index, q)}, device_id_type=mesh_ids,
        )

    def pair_copy(y, z):
        return pltpu.make_async_remote_copy(
            block(y, z, c0), block(y, z, c0), pair_sem.at[y, z], recv_sem.at[y, z, c0],
            device_id={"tensor": partner}, device_id_type=mesh_ids,
        )

    def arrival(y, z, c):
        return pltpu.make_async_remote_copy(
            x_ref, block(y, z, c), col_sem.at[0], recv_sem.at[y, z, c],
            device_id={"tensor": index}, device_id_type=mesh_ids,
        )

    def spread(z):
        def send_y(m, carry):
            y_copy(z, (y0 + m) % n_y).start()
            return carry

        lax.fori_loop(1, n_y, send_y, 0)
        pair_copy(y0, z).start()

    local = pltpu.make_async_copy(x_ref, block(y0, z0, c0), local_sem)
    local.start()

    def send_col(k, carry):
        col_copy((z0 + k) % n_col).start()
        return carry

    lax.fori_loop(1, n_col, send_col, 0)
    local.wait()
    spread(z0)

    def relay_col(k, carry):
        z = (z0 + k) % n_col
        arrival(y0, z, c0).wait_recv()
        spread(z)
        return carry

    lax.fori_loop(1, n_col, relay_col, 0)

    def relay_y(m, carry):
        y = (y0 + m) % n_y

        def each(k, inner):
            z = (z0 + k) % n_col
            arrival(y, z, c0).wait_recv()
            pair_copy(y, z).start()
            return inner

        return lax.fori_loop(0, n_col, each, carry)

    lax.fori_loop(1, n_y, relay_y, 0)

    def finish_col(k, carry):
        col_copy((z0 + k) % n_col).wait_send()
        return carry

    lax.fori_loop(1, n_col, finish_col, 0)

    def finish_y(k, carry):
        z = (z0 + k) % n_col

        def each(m, inner):
            y_copy(z, (y0 + m) % n_y).wait_send()
            return inner

        return lax.fori_loop(1, n_y, each, carry)

    lax.fori_loop(0, n_col, finish_y, 0)

    def finish_pair(m, carry):
        y = (y0 + m) % n_y

        def each(k, inner):
            z = (z0 + k) % n_col
            pair_copy(y, z).wait_send()
            arrival(y, z, 1 - c0).wait_recv()
            return inner

        return lax.fori_loop(0, n_col, each, carry)

    lax.fori_loop(0, n_y, finish_pair, 0)


def gather_tokens(x, col, ygroup, slot, n_col, n_y, collective_id):
    return pl.pallas_call(
        functools.partial(_gather_kernel, n_col, n_y, col, ygroup, slot),
        out_shape=jax.ShapeDtypeStruct((n_col * n_y * 2,) + x.shape, x.dtype),
        in_specs=[pl.BlockSpec(memory_space=pltpu.VMEM)],
        out_specs=pl.BlockSpec(memory_space=pltpu.VMEM),
        scratch_shapes=[
            pltpu.SemaphoreType.DMA,
            pltpu.SemaphoreType.DMA((n_col,)),
            pltpu.SemaphoreType.DMA((n_col, n_y)),
            pltpu.SemaphoreType.DMA((n_y, n_col)),
            pltpu.SemaphoreType.DMA((n_y, n_col, 2)),
        ],
        compiler_params=pltpu.CompilerParams(collective_id=collective_id, has_side_effects=True),
    )(x)


def token_slot(y, z, c):
    return (y * 4 + z) * 2 + c


def _reduce_kernel(n_col, n_y, n_dp, col, ygroup, attended_ref, output_ref, feedforward_ref, x_ref,
                   pages_ref, out_ref, pages_out, rows_ref, inbox0, chip, inbox1, stage, inbox2, sem0,
                   local_sem, send_sem, recv_sem, send2_sem, recv2_sem, page_local_sem, page_send_sem,
                   page_recv_sem):
    index = lax.axis_index("tensor")
    cpos, ypos, core = col[0](index), ygroup[0](index), index % 2
    mesh_ids = pl.DeviceIdType.MESH
    barrier = pltpu.get_barrier_semaphore()
    group = lax.axis_index("dp")

    def page_copy(g, slot):
        return pltpu.make_async_remote_copy(
            pages_ref.at[g], pages_out.at[slot], page_send_sem.at[g], page_recv_sem.at[slot],
            device_id={"dp": g}, device_id_type=mesh_ids,
        )

    def greet_group(k, carry):
        pl.semaphore_signal(
            barrier, inc=1, device_id={"dp": (group + k) % n_dp}, device_id_type=mesh_ids
        )
        return carry

    lax.fori_loop(1, n_dp, greet_group, 0)
    sibling = (2, lambda t: t % 2, lambda t, q: t - t % 2 + q)
    total = _signal(barrier, [sibling, (n_y, *ygroup), (n_col, *col)])

    product = (
        jnp.dot(attended_ref[...], output_ref[...], preferred_element_type=jnp.float32)
        + feedforward_ref[...]
    )
    rows = x_ref.shape[0]
    for owner in range(n_y * n_col * 2):
        rows_ref[owner // (2 * n_col), (owner // 2) % n_col, owner % 2] = product[
            owner * rows : (owner + 1) * rows
        ].astype(rows_ref.dtype)
    pl.semaphore_wait(barrier, total + n_dp - 1)

    pair = pltpu.make_async_remote_copy(
        rows_ref.at[:, :, 1 - core], inbox0, sem0.at[0], sem0.at[1],
        device_id={"tensor": index - core + 1 - core}, device_id_type=mesh_ids,
    )
    pair.start()
    pair.wait_send()
    pair.wait_recv()
    for y in range(n_y):
        for z in range(n_col):
            chip[y, z] = (
                rows_ref[y, z, core].astype(jnp.float32) + inbox0[y, z].astype(jnp.float32)
            ).astype(chip.dtype)

    def plane_copy(q, z, slot):
        return pltpu.make_async_remote_copy(
            chip.at[q, z], inbox1.at[z, slot], send_sem.at[z, q], recv_sem.at[z, slot],
            device_id={"tensor": ygroup[1](index, q)}, device_id_type=mesh_ids,
        )

    def col_copy(q, slot):
        return pltpu.make_async_remote_copy(
            stage.at[q], inbox2.at[slot], send2_sem.at[q], recv2_sem.at[slot],
            device_id={"tensor": col[1](index, q)}, device_id_type=mesh_ids,
        )

    order = [(cpos + 1 + k) % n_col for k in range(n_col)]
    locals_ = []
    for z in order:
        local = pltpu.make_async_copy(chip.at[ypos, z], inbox1.at[z, ypos], local_sem.at[z])
        local.start()
        locals_.append(local)

        def send_plane(m, carry, z=z):
            plane_copy((ypos + m) % n_y, z, ypos).start()
            return carry

        lax.fori_loop(1, n_y, send_plane, 0)

    def plane_sum(z, local):
        def arrive(m, carry):
            plane_copy((ypos + m) % n_y, z, (ypos + m) % n_y).wait_recv()
            return carry

        lax.fori_loop(1, n_y, arrive, 0)
        local.wait()
        total = inbox1[z, 0].astype(jnp.float32)
        for sender in range(1, n_y):
            total = total + inbox1[z, sender].astype(jnp.float32)
        return total

    for z, local in zip(order[:-1], locals_[:-1]):
        stage[z] = plane_sum(z, local).astype(stage.dtype)
        col_copy(z, cpos).start()

    page_local = pltpu.make_async_copy(pages_ref.at[group], pages_out.at[group], page_local_sem)
    page_local.start()

    def send_pages(k, carry):
        page_copy((group + k) % n_dp, group).start()
        return carry

    lax.fori_loop(1, n_dp, send_pages, 0)

    result = x_ref[...].astype(jnp.float32) + plane_sum(cpos, locals_[-1])

    def finish_plane(m, carry):
        q = (ypos + m) % n_y
        for z in order:
            plane_copy(q, z, ypos).wait_send()
        return carry

    lax.fori_loop(1, n_y, finish_plane, 0)

    for z in order[:-1]:
        col_copy(z, cpos).wait_send()
        col_copy(z, z).wait_recv()
        result = result + inbox2[z].astype(jnp.float32)
    out_ref[...] = result

    def finish_pages(k, carry):
        g = (group + k) % n_dp
        page_copy(g, group).wait_send()
        page_copy(g, g).wait_recv()
        return carry

    lax.fori_loop(1, n_dp, finish_pages, 0)
    page_local.wait()


def reduce_rows(attended, output_weight, feedforward, x, pages, col, ygroup, n_y, n_col, collective_id):
    block = x.shape
    n_dp = pages.shape[0]
    operands = (attended, output_weight, feedforward, x, pages)
    return pl.pallas_call(
        functools.partial(_reduce_kernel, n_col, n_y, n_dp, col, ygroup),
        out_shape=(
            jax.ShapeDtypeStruct(block, jnp.float32),
            jax.ShapeDtypeStruct(pages.shape, pages.dtype),
        ),
        in_specs=[pl.BlockSpec(memory_space=pltpu.VMEM)] * len(operands),
        out_specs=(pl.BlockSpec(memory_space=pltpu.VMEM), pl.BlockSpec(memory_space=pltpu.VMEM)),
        scratch_shapes=[
            pltpu.VMEM((n_y, n_col, 2) + block, x.dtype),
            pltpu.VMEM((n_y, n_col) + block, x.dtype),
            pltpu.VMEM((n_y, n_col) + block, x.dtype),
            pltpu.VMEM((n_col, n_y) + block, x.dtype),
            pltpu.VMEM((n_col,) + block, x.dtype),
            pltpu.VMEM((n_col,) + block, x.dtype),
            pltpu.SemaphoreType.DMA((2,)),
            pltpu.SemaphoreType.DMA((n_col,)),
            pltpu.SemaphoreType.DMA((n_col, n_y)),
            pltpu.SemaphoreType.DMA((n_col, n_y)),
            pltpu.SemaphoreType.DMA((n_col,)),
            pltpu.SemaphoreType.DMA((n_col,)),
            pltpu.SemaphoreType.DMA,
            pltpu.SemaphoreType.DMA((n_dp,)),
            pltpu.SemaphoreType.DMA((n_dp,)),
        ],
        compiler_params=pltpu.CompilerParams(collective_id=collective_id, has_side_effects=True),
    )(*operands)


def same_core_group(index):
    return index // 8


def same_core_member(index, q):
    return q * 8 + index % 8


def shards(
    hidden_states,
    attention_gain,
    feedforward_gain,
    heads_weight,
    output_weight,
    upward_weight,
    downward_weight,
    segments,
    page_targets,
):
    tensor_count = lax.axis_size("tensor")
    replica_count = lax.axis_size("dp")
    tensor_index = lax.axis_index("tensor")
    quarters = tensor_count // H
    quarter_width = HD // quarters
    quarter_index = tensor_index % quarters
    stream = segments[0]
    tokens_total = stream.shape[0]
    local_rows = hidden_states.shape[0]

    width = hidden_states.shape[1]
    planes = tensor_count // 8
    gathered = gather_tokens(
        hidden_states,
        (column_group, column_member),
        (same_core_group, same_core_member),
        token_slot,
        planes,
        4,
        0,
    )
    tokens = gathered.reshape(tokens_total, width)
    normed_attention = layer_norm(tokens, attention_gain)
    normed_feedforward = layer_norm(tokens, feedforward_gain)
    joined = jnp.dot(normed_attention, heads_weight, preferred_element_type=jnp.float32).astype(
        jnp.bfloat16
    )

    indices, starting = positions_of(stream)
    offsets = indices - starting
    query_piece = joined[:, :quarter_width]
    key_piece = joined[:, quarter_width : 2 * quarter_width]
    value_piece = joined[:, 2 * quarter_width :]
    leading = quarter_index == 0
    query_piece = jnp.where(leading, rotate_leading(query_piece, offsets, ROT), query_piece)
    key_piece = jnp.where(leading, rotate_leading(key_piece, offsets, ROT), key_piece)

    page_count = tokens_total // PAGE
    page_rows = jnp.concatenate([key_piece, value_piece], 1).reshape(
        page_count, PAGE * 2 * quarter_width
    )
    targets = page_targets[:, 0]
    page_numbers = jnp.arange(page_count, dtype=jnp.int32)
    earlier = jnp.sum(
        (
            (targets[None, :] == targets[:, None]) & (page_numbers[None, :] < page_numbers[:, None])
        ).astype(jnp.int32),
        axis=1,
    )
    capacity = 2 * page_count // replica_count
    slot_numbers = targets * capacity + earlier
    placing = (
        jnp.arange(replica_count * capacity, dtype=jnp.int32)[:, None] == slot_numbers[None, :]
    ).astype(jnp.bfloat16)
    outgoing = jnp.dot(placing, page_rows, preferred_element_type=jnp.float32).astype(jnp.bfloat16)
    outgoing = outgoing.reshape(replica_count, capacity * PAGE, 2 * quarter_width)
    head_pieces, feedforward = exchange_all(
        1,
        (jnp.concatenate([query_piece, key_piece], 1)[None], "tensor", quarters, True, None),
        work=(_feedforward_up, _feedforward_down),
        inputs=(normed_feedforward, upward_weight, downward_weight),
        results=(jax.ShapeDtypeStruct((tokens_total, width), jnp.float32),),
    )
    queries = head_pieces[:, :, :quarter_width].transpose(1, 0, 2).reshape(tokens_total, HD)
    keys = head_pieces[:, :, quarter_width:].transpose(1, 0, 2).reshape(tokens_total, HD)

    scores = jnp.dot(queries, keys.T, preferred_element_type=jnp.float32) * HD ** (-0.5)
    allowed = (stream[None, :] == stream[:, None]) & (indices[None, :] <= indices[:, None])
    peak = jnp.max(jnp.where(allowed, scores, -jnp.inf), axis=1, keepdims=True)
    weights = jnp.where(allowed, jnp.exp(scores - peak), 0.0)
    weight_sum = jnp.sum(weights, axis=1, keepdims=True)
    mixed = jnp.dot(weights.astype(jnp.bfloat16), value_piece, preferred_element_type=jnp.float32)
    attended = (mixed / weight_sum).astype(jnp.bfloat16)

    layer_output, incoming = reduce_rows(
        attended,
        output_weight,
        feedforward,
        hidden_states,
        outgoing,
        (column_group, column_member),
        (same_core_group, same_core_member),
        4,
        planes,
        2,
    )

    cache_pages = incoming.reshape(1, replica_count, capacity, PAGE, 2 * quarter_width)
    return (layer_output, cache_pages)


def solution(mesh):
    in_specs = (
        P(("dp", "tensor"), None),
        P(),
        P(),
        P(None, "tensor"),
        P("tensor", None),
        P(None, "tensor"),
        P("tensor", None),
        P("dp", None),
        P("dp", None),
    )
    out_specs = (P(("dp", "tensor"), None), P("dp", None, None, None, "tensor"))
    return jax.shard_map(shards, mesh=mesh, in_specs=in_specs, out_specs=out_specs, check_vma=False)
```

```python
import functools
import math

import jax
import jax.numpy as jnp
from jax import lax
from jax.experimental import pallas as pl
from jax.experimental.pallas import tpu as pltpu
from jax.sharding import PartitionSpec as P

H = 8
HD = 256
ROT = 64
PAGE = 16


epsilon = 1e-05
rotary_base = 10000.0


def layer_norm(values, gain):
    floats = values.astype(jnp.float32)
    center = jnp.mean(floats, axis=-1, keepdims=True)
    shifted = floats - center
    spread = jnp.mean(shifted * shifted, axis=-1, keepdims=True)
    return (shifted * lax.rsqrt(spread + epsilon) * gain).astype(jnp.bfloat16)


def positions_of(stream):
    indices = jnp.arange(stream.shape[0], dtype=jnp.int32)
    boundary = jnp.concatenate([jnp.ones((1,), dtype=bool), stream[1:] != stream[:-1]])
    starting = lax.cummax(jnp.where(boundary, indices, jnp.zeros_like(indices)), axis=0)
    return (indices, starting)


def rotate_leading(vectors, offsets, rotary_dims):
    half_dims = rotary_dims // 2
    frequency = jnp.exp(
        jnp.arange(half_dims, dtype=jnp.float32) * (-2.0 * math.log(rotary_base) / rotary_dims)
    )
    angles = offsets.astype(jnp.float32)[:, None] * frequency[None, :]
    cosine = jnp.cos(angles)
    sine = jnp.sin(angles)
    floats = vectors.astype(jnp.float32)
    leading = floats[..., :half_dims]
    trailing = floats[..., half_dims:rotary_dims]
    rotated = jnp.concatenate(
        [
            leading * cosine - trailing * sine,
            trailing * cosine + leading * sine,
            floats[..., rotary_dims:],
        ],
        axis=-1,
    )
    return rotated.astype(jnp.bfloat16)


def _exchange_kernel(plans, work, extra_in, extra_out, *refs):
    count = len(plans)
    sources, refs = refs[:count], refs[count:]
    inputs, refs = refs[:extra_in], refs[extra_in:]
    outs, refs = refs[:count], refs[count:]
    results, semaphores = refs[:extra_out], refs[extra_out:]
    mesh_ids = pl.DeviceIdType.MESH
    barrier = pltpu.get_barrier_semaphore()
    steps = []
    for number, (axis, n, shared, position, member) in enumerate(plans):
        src_ref, out_ref = sources[number], outs[number]
        local_sem, send_sem, recv_sem = semaphores[3 * number : 3 * number + 3]
        index = lax.axis_index(axis)
        pos = position(index)

        def peer_copy(q, slot, src_ref=src_ref, out_ref=out_ref, send_sem=send_sem,
                      recv_sem=recv_sem, axis=axis, member=member, index=index, shared=shared):
            return pltpu.make_async_remote_copy(
                src_ref=src_ref.at[0] if shared else src_ref.at[q],
                dst_ref=out_ref.at[slot],
                send_sem=send_sem.at[q],
                recv_sem=recv_sem.at[slot],
                device_id={axis: member(index, q)},
                device_id_type=mesh_ids,
            )

        def greet(k, carry, n=n, pos=pos, axis=axis, member=member, index=index):
            q = (pos + k) % n
            pl.semaphore_signal(
                barrier, inc=1, device_id={axis: member(index, q)}, device_id_type=mesh_ids
            )
            return carry

        lax.fori_loop(1, n, greet, 0)
        local = pltpu.make_async_copy(
            src_ref.at[0] if shared else src_ref.at[pos], out_ref.at[pos], local_sem
        )
        steps.append((n, pos, peer_copy, local))
    carried = work[0](*inputs) if work is not None else None
    pl.semaphore_wait(barrier, sum(plan[1] - 1 for plan in plans))

    for n, pos, peer_copy, local in steps:
        local.start()

        def send(k, carry, n=n, pos=pos, peer_copy=peer_copy):
            peer_copy((pos + k) % n, pos).start()
            return carry

        lax.fori_loop(1, n, send, 0)

    if work is not None:
        work[1](carried, *inputs, *results)

    for n, pos, peer_copy, local in steps:

        def finish(k, carry, n=n, pos=pos, peer_copy=peer_copy):
            q = (pos + k) % n
            peer_copy(q, pos).wait_send()
            peer_copy(q, q).wait_recv()
            return carry

        lax.fori_loop(1, n, finish, 0)
        local.wait()


def contiguous(n):
    return (lambda index: index % n, lambda index, q: index - index % n + q)


def plane_group(index):
    return (index // 8) * 2 + index % 2


def plane_member(index, q):
    return ((q // 2) * 4 + (index // 2) % 4) * 2 + q % 2


def token_block(zc, p):
    return ((p // 2) * 4 + zc) * 2 + p % 2


def plane_rows(rows_ref, q, z):
    return rows_ref.at[q // 2, z, q % 2]


def column_group(index):
    return (index // 2) % 4


def column_member(index, q):
    return ((index // 8) * 4 + q) * 2 + index % 2


def exchange_all(collective_id, *requests, work=None, inputs=(), results=()):
    plans, blocks, shapes, scratch = [], [], [], []
    for data, axis, n, shared, group in requests:
        position, member = group if group is not None else contiguous(n)
        plans.append((axis, n, shared, position, member))
        blocks.append(data)
        shapes.append(jax.ShapeDtypeStruct((n,) + data.shape[1:], data.dtype))
        scratch += [
            pltpu.SemaphoreType.DMA,
            pltpu.SemaphoreType.DMA((n,)),
            pltpu.SemaphoreType.DMA((n,)),
        ]
    operands = blocks + list(inputs)
    out_shapes = shapes + list(results)
    return pl.pallas_call(
        functools.partial(_exchange_kernel, tuple(plans), work, len(inputs), len(results)),
        out_shape=tuple(out_shapes),
        in_specs=[pl.BlockSpec(memory_space=pltpu.VMEM)] * len(operands),
        out_specs=tuple(pl.BlockSpec(memory_space=pltpu.VMEM) for _ in out_shapes),
        scratch_shapes=scratch,
        compiler_params=pltpu.CompilerParams(collective_id=collective_id, has_side_effects=True),
    )(*operands)


def exchange(blocks, axis, n, shared, collective_id, group=None):
    return exchange_all(collective_id, (blocks, axis, n, shared, group))[0]


def _feedforward_up(normed_ref, upward_ref, downward_ref):
    upward = jnp.dot(normed_ref[...], upward_ref[...], preferred_element_type=jnp.float32)
    return (0.5 * upward * (1.0 + lax.erf(upward * math.sqrt(0.5)))).astype(jnp.bfloat16)


def _feedforward_down(hidden, normed_ref, upward_ref, downward_ref, out_ref):
    out_ref[...] = jnp.dot(hidden, downward_ref[...], preferred_element_type=jnp.float32)


def _signal(barrier, groups):
    index = lax.axis_index("tensor")
    total = 0
    for n, position, member in groups:
        pos = position(index)

        def greet(k, carry, n=n, pos=pos, member=member):
            pl.semaphore_signal(
                barrier,
                inc=1,
                device_id={"tensor": member(index, (pos + k) % n)},
                device_id_type=pl.DeviceIdType.MESH,
            )
            return carry

        lax.fori_loop(1, n, greet, 0)
        total += n - 1
    return total


def _greet(barrier, groups, extra=0):
    index = lax.axis_index("tensor")
    total = 0
    for n, position, member in groups:
        pos = position(index)

        def greet(k, carry, n=n, pos=pos, member=member):
            pl.semaphore_signal(
                barrier,
                inc=1,
                device_id={"tensor": member(index, (pos + k) % n)},
                device_id_type=pl.DeviceIdType.MESH,
            )
            return carry

        lax.fori_loop(1, n, greet, 0)
        total += n - 1
    pl.semaphore_wait(barrier, total + extra)


def _gather_kernel(n_col, n_y, col, ygroup, slot, x_ref, out_ref, local_sem, col_sem, y_sem, pair_sem,
                   recv_sem):
    index = lax.axis_index("tensor")
    z0, y0, c0 = col[0](index), ygroup[0](index), index % 2
    mesh_ids = pl.DeviceIdType.MESH
    sibling = (2, lambda t: t % 2, lambda t, q: t - t % 2 + q)
    _greet(pltpu.get_barrier_semaphore(), [(n_col, *col), (n_y, *ygroup), sibling])
    partner = index - c0 + 1 - c0

    def block(y, z, c):
        return out_ref.at[slot(y, z, c)]

    def col_copy(q):
        return pltpu.make_async_remote_copy(
            x_ref, block(y0, z0, c0), col_sem.at[q], recv_sem.at[y0, z0, c0],
            device_id={"tensor": col[1](index, q)}, device_id_type=mesh_ids,
        )

    def y_copy(z, q):
        return pltpu.make_async_remote_copy(
            block(y0, z, c0), block(y0, z, c0), y_sem.at[z, q], recv_sem.at[y0, z, c0],
            device_id={"tensor": ygroup[1](index, q)}, device_id_type=mesh_ids,
        )

    def pair_copy(y, z):
        return pltpu.make_async_remote_copy(
            block(y, z, c0), block(y, z, c0), pair_sem.at[y, z], recv_sem.at[y, z, c0],
            device_id={"tensor": partner}, device_id_type=mesh_ids,
        )

    def arrival(y, z, c):
        return pltpu.make_async_remote_copy(
            x_ref, block(y, z, c), col_sem.at[0], recv_sem.at[y, z, c],
            device_id={"tensor": index}, device_id_type=mesh_ids,
        )

    def spread(z):
        def send_y(m, carry):
            y_copy(z, (y0 + m) % n_y).start()
            return carry

        lax.fori_loop(1, n_y, send_y, 0)
        pair_copy(y0, z).start()

    local = pltpu.make_async_copy(x_ref, block(y0, z0, c0), local_sem)
    local.start()

    def send_col(k, carry):
        col_copy((z0 + k) % n_col).start()
        return carry

    lax.fori_loop(1, n_col, send_col, 0)
    local.wait()
    spread(z0)

    def relay_col(k, carry):
        z = (z0 + k) % n_col
        arrival(y0, z, c0).wait_recv()
        spread(z)
        return carry

    lax.fori_loop(1, n_col, relay_col, 0)

    def relay_y(m, carry):
        y = (y0 + m) % n_y

        def each(k, inner):
            z = (z0 + k) % n_col
            arrival(y, z, c0).wait_recv()
            pair_copy(y, z).start()
            return inner

        return lax.fori_loop(0, n_col, each, carry)

    lax.fori_loop(1, n_y, relay_y, 0)

    def finish_col(k, carry):
        col_copy((z0 + k) % n_col).wait_send()
        return carry

    lax.fori_loop(1, n_col, finish_col, 0)

    def finish_y(k, carry):
        z = (z0 + k) % n_col

        def each(m, inner):
            y_copy(z, (y0 + m) % n_y).wait_send()
            return inner

        return lax.fori_loop(1, n_y, each, carry)

    lax.fori_loop(0, n_col, finish_y, 0)

    def finish_pair(m, carry):
        y = (y0 + m) % n_y

        def each(k, inner):
            z = (z0 + k) % n_col
            pair_copy(y, z).wait_send()
            arrival(y, z, 1 - c0).wait_recv()
            return inner

        return lax.fori_loop(0, n_col, each, carry)

    lax.fori_loop(0, n_y, finish_pair, 0)


def gather_tokens(x, col, ygroup, slot, n_col, n_y, collective_id):
    return pl.pallas_call(
        functools.partial(_gather_kernel, n_col, n_y, col, ygroup, slot),
        out_shape=jax.ShapeDtypeStruct((n_col * n_y * 2,) + x.shape, x.dtype),
        in_specs=[pl.BlockSpec(memory_space=pltpu.VMEM)],
        out_specs=pl.BlockSpec(memory_space=pltpu.VMEM),
        scratch_shapes=[
            pltpu.SemaphoreType.DMA,
            pltpu.SemaphoreType.DMA((n_col,)),
            pltpu.SemaphoreType.DMA((n_col, n_y)),
            pltpu.SemaphoreType.DMA((n_y, n_col)),
            pltpu.SemaphoreType.DMA((n_y, n_col, 2)),
        ],
        compiler_params=pltpu.CompilerParams(collective_id=collective_id, has_side_effects=True),
    )(x)


def token_slot(y, z, c):
    return (y * 4 + z) * 2 + c


def _reduce_kernel(n_col, n_y, n_dp, col, ygroup, attended_ref, output_ref, feedforward_ref, x_ref,
                   pages_ref, out_ref, pages_out, rows_ref, inbox0, chip, inbox1, stage, inbox2, sem0,
                   local_sem, send_sem, recv_sem, send2_sem, recv2_sem, page_local_sem, page_send_sem,
                   page_recv_sem):
    index = lax.axis_index("tensor")
    cpos, ypos, core = col[0](index), ygroup[0](index), index % 2
    mesh_ids = pl.DeviceIdType.MESH
    barrier = pltpu.get_barrier_semaphore()
    group = lax.axis_index("dp")

    def page_copy(g, slot):
        return pltpu.make_async_remote_copy(
            pages_ref.at[g], pages_out.at[slot], page_send_sem.at[g], page_recv_sem.at[slot],
            device_id={"dp": g}, device_id_type=mesh_ids,
        )

    def greet_group(k, carry):
        pl.semaphore_signal(
            barrier, inc=1, device_id={"dp": (group + k) % n_dp}, device_id_type=mesh_ids
        )
        return carry

    lax.fori_loop(1, n_dp, greet_group, 0)
    sibling = (2, lambda t: t % 2, lambda t, q: t - t % 2 + q)
    total = _signal(barrier, [sibling, (n_y, *ygroup), (n_col, *col)])

    product = (
        jnp.dot(attended_ref[...], output_ref[...], preferred_element_type=jnp.float32)
        + feedforward_ref[...]
    )
    rows = x_ref.shape[0]
    for owner in range(n_y * n_col * 2):
        rows_ref[owner // (2 * n_col), (owner // 2) % n_col, owner % 2] = product[
            owner * rows : (owner + 1) * rows
        ].astype(rows_ref.dtype)
    pl.semaphore_wait(barrier, total + n_dp - 1)
    page_local = pltpu.make_async_copy(pages_ref.at[group], pages_out.at[group], page_local_sem)
    page_local.start()

    def send_pages(k, carry):
        page_copy((group + k) % n_dp, group).start()
        return carry

    lax.fori_loop(1, n_dp, send_pages, 0)

    def pair_copy(z):
        return pltpu.make_async_remote_copy(
            rows_ref.at[:, z, 1 - core], inbox0.at[:, z], sem0.at[0, z], sem0.at[1, z],
            device_id={"tensor": index - core + 1 - core}, device_id_type=mesh_ids,
        )

    order = [(cpos + 1 + k) % n_col for k in range(n_col)]
    for z in order:
        pair_copy(z).start()

    def plane_copy(q, z, slot):
        return pltpu.make_async_remote_copy(
            chip.at[q, z], inbox1.at[z, slot], send_sem.at[z, q], recv_sem.at[z, slot],
            device_id={"tensor": ygroup[1](index, q)}, device_id_type=mesh_ids,
        )

    def col_copy(q, slot):
        return pltpu.make_async_remote_copy(
            stage.at[q], inbox2.at[slot], send2_sem.at[q], recv2_sem.at[slot],
            device_id={"tensor": col[1](index, q)}, device_id_type=mesh_ids,
        )

    locals_ = []
    for z in order:
        pair_copy(z).wait_send()
        pair_copy(z).wait_recv()
        for y in range(n_y):
            chip[y, z] = (
                rows_ref[y, z, core].astype(jnp.float32) + inbox0[y, z].astype(jnp.float32)
            ).astype(chip.dtype)
        local = pltpu.make_async_copy(chip.at[ypos, z], inbox1.at[z, ypos], local_sem.at[z])
        local.start()
        locals_.append(local)

        def send_plane(m, carry, z=z):
            plane_copy((ypos + m) % n_y, z, ypos).start()
            return carry

        lax.fori_loop(1, n_y, send_plane, 0)

    def plane_sum(z, local):
        def arrive(m, carry):
            plane_copy((ypos + m) % n_y, z, (ypos + m) % n_y).wait_recv()
            return carry

        lax.fori_loop(1, n_y, arrive, 0)
        local.wait()
        total = inbox1[z, 0].astype(jnp.float32)
        for sender in range(1, n_y):
            total = total + inbox1[z, sender].astype(jnp.float32)
        return total

    for z, local in zip(order[:-1], locals_[:-1]):
        stage[z] = plane_sum(z, local).astype(stage.dtype)
        col_copy(z, cpos).start()

    result = x_ref[...].astype(jnp.float32) + plane_sum(cpos, locals_[-1])

    def finish_plane(m, carry):
        q = (ypos + m) % n_y
        for z in order:
            plane_copy(q, z, ypos).wait_send()
        return carry

    lax.fori_loop(1, n_y, finish_plane, 0)

    for z in order[:-1]:
        col_copy(z, cpos).wait_send()
        col_copy(z, z).wait_recv()
        result = result + inbox2[z].astype(jnp.float32)
    out_ref[...] = result

    def finish_pages(k, carry):
        g = (group + k) % n_dp
        page_copy(g, group).wait_send()
        page_copy(g, g).wait_recv()
        return carry

    lax.fori_loop(1, n_dp, finish_pages, 0)
    page_local.wait()


def reduce_rows(attended, output_weight, feedforward, x, pages, col, ygroup, n_y, n_col, collective_id):
    block = x.shape
    n_dp = pages.shape[0]
    operands = (attended, output_weight, feedforward, x, pages)
    return pl.pallas_call(
        functools.partial(_reduce_kernel, n_col, n_y, n_dp, col, ygroup),
        out_shape=(
            jax.ShapeDtypeStruct(block, jnp.float32),
            jax.ShapeDtypeStruct(pages.shape, pages.dtype),
        ),
        in_specs=[pl.BlockSpec(memory_space=pltpu.VMEM)] * len(operands),
        out_specs=(pl.BlockSpec(memory_space=pltpu.VMEM), pl.BlockSpec(memory_space=pltpu.VMEM)),
        scratch_shapes=[
            pltpu.VMEM((n_y, n_col, 2) + block, x.dtype),
            pltpu.VMEM((n_y, n_col) + block, x.dtype),
            pltpu.VMEM((n_y, n_col) + block, x.dtype),
            pltpu.VMEM((n_col, n_y) + block, x.dtype),
            pltpu.VMEM((n_col,) + block, x.dtype),
            pltpu.VMEM((n_col,) + block, x.dtype),
            pltpu.SemaphoreType.DMA((2, n_col)),
            pltpu.SemaphoreType.DMA((n_col,)),
            pltpu.SemaphoreType.DMA((n_col, n_y)),
            pltpu.SemaphoreType.DMA((n_col, n_y)),
            pltpu.SemaphoreType.DMA((n_col,)),
            pltpu.SemaphoreType.DMA((n_col,)),
            pltpu.SemaphoreType.DMA,
            pltpu.SemaphoreType.DMA((n_dp,)),
            pltpu.SemaphoreType.DMA((n_dp,)),
        ],
        compiler_params=pltpu.CompilerParams(collective_id=collective_id, has_side_effects=True),
    )(*operands)


def same_core_group(index):
    return index // 8


def same_core_member(index, q):
    return q * 8 + index % 8


def shards(
    hidden_states,
    attention_gain,
    feedforward_gain,
    heads_weight,
    output_weight,
    upward_weight,
    downward_weight,
    segments,
    page_targets,
):
    tensor_count = lax.axis_size("tensor")
    replica_count = lax.axis_size("dp")
    tensor_index = lax.axis_index("tensor")
    quarters = tensor_count // H
    quarter_width = HD // quarters
    quarter_index = tensor_index % quarters
    stream = segments[0]
    tokens_total = stream.shape[0]
    local_rows = hidden_states.shape[0]

    width = hidden_states.shape[1]
    planes = tensor_count // 8
    gathered = gather_tokens(
        hidden_states,
        (column_group, column_member),
        (same_core_group, same_core_member),
        token_slot,
        planes,
        4,
        0,
    )
    tokens = gathered.reshape(tokens_total, width)
    normed_attention = layer_norm(tokens, attention_gain)
    normed_feedforward = layer_norm(tokens, feedforward_gain)
    joined = jnp.dot(normed_attention, heads_weight, preferred_element_type=jnp.float32).astype(
        jnp.bfloat16
    )

    indices, starting = positions_of(stream)
    offsets = indices - starting
    query_piece = joined[:, :quarter_width]
    key_piece = joined[:, quarter_width : 2 * quarter_width]
    value_piece = joined[:, 2 * quarter_width :]
    leading = quarter_index == 0
    query_piece = jnp.where(leading, rotate_leading(query_piece, offsets, ROT), query_piece)
    key_piece = jnp.where(leading, rotate_leading(key_piece, offsets, ROT), key_piece)

    page_count = tokens_total // PAGE
    page_rows = jnp.concatenate([key_piece, value_piece], 1).reshape(
        page_count, PAGE * 2 * quarter_width
    )
    targets = page_targets[:, 0]
    page_numbers = jnp.arange(page_count, dtype=jnp.int32)
    earlier = jnp.sum(
        (
            (targets[None, :] == targets[:, None]) & (page_numbers[None, :] < page_numbers[:, None])
        ).astype(jnp.int32),
        axis=1,
    )
    capacity = 2 * page_count // replica_count
    slot_numbers = targets * capacity + earlier
    placing = (
        jnp.arange(replica_count * capacity, dtype=jnp.int32)[:, None] == slot_numbers[None, :]
    ).astype(jnp.bfloat16)
    outgoing = jnp.dot(placing, page_rows, preferred_element_type=jnp.float32).astype(jnp.bfloat16)
    outgoing = outgoing.reshape(replica_count, capacity * PAGE, 2 * quarter_width)
    head_pieces, feedforward = exchange_all(
        1,
        (jnp.concatenate([query_piece, key_piece], 1)[None], "tensor", quarters, True, None),
        work=(_feedforward_up, _feedforward_down),
        inputs=(normed_feedforward, upward_weight, downward_weight),
        results=(jax.ShapeDtypeStruct((tokens_total, width), jnp.float32),),
    )
    queries = head_pieces[:, :, :quarter_width].transpose(1, 0, 2).reshape(tokens_total, HD)
    keys = head_pieces[:, :, quarter_width:].transpose(1, 0, 2).reshape(tokens_total, HD)

    scores = jnp.dot(queries, keys.T, preferred_element_type=jnp.float32) * HD ** (-0.5)
    allowed = (stream[None, :] == stream[:, None]) & (indices[None, :] <= indices[:, None])
    peak = jnp.max(jnp.where(allowed, scores, -jnp.inf), axis=1, keepdims=True)
    weights = jnp.where(allowed, jnp.exp(scores - peak), 0.0)
    weight_sum = jnp.sum(weights, axis=1, keepdims=True)
    mixed = jnp.dot(weights.astype(jnp.bfloat16), value_piece, preferred_element_type=jnp.float32)
    attended = (mixed / weight_sum).astype(jnp.bfloat16)

    layer_output, incoming = reduce_rows(
        attended,
        output_weight,
        feedforward,
        hidden_states,
        outgoing,
        (column_group, column_member),
        (same_core_group, same_core_member),
        4,
        planes,
        2,
    )

    cache_pages = incoming.reshape(1, replica_count, capacity, PAGE, 2 * quarter_width)
    return (layer_output, cache_pages)


def solution(mesh):
    in_specs = (
        P(("dp", "tensor"), None),
        P(),
        P(),
        P(None, "tensor"),
        P("tensor", None),
        P(None, "tensor"),
        P("tensor", None),
        P("dp", None),
        P("dp", None),
    )
    out_specs = (P(("dp", "tensor"), None), P("dp", None, None, None, "tensor"))
    return jax.shard_map(shards, mesh=mesh, in_specs=in_specs, out_specs=out_specs, check_vma=False)
```
